32 devices in a mesh: pop: 2 (over x), dp: 8 (over z, y), tp: 2 (over core).
Axes of the slice: x: 2, y: 2, z: 4, core: 2. Of those that a mesh axis runs over, the one named last changes fastest.
Arguments:
- q_latent: bfloat16 [256, 128, 512], P(('pop', 'dp')), parts along dimension 0
- q_rope: bfloat16 [256, 8192], P(('pop', 'dp')), parts along dimension 0
- new_entry: bfloat16 [256, 576], P(('pop', 'dp')), parts along dimension 0
- cache_latent: bfloat16 [768, 64, 512], P(('pop', 'dp'), 'tp'), parts along dimension 0, may hold values from -6 to 6
- cache_rope: bfloat16 [768, 4096], P(('pop', 'dp'), 'tp'), parts along dimension 0, may hold values from -6 to 6
- source_rank: int32 [256, 16, 1], P(('pop', 'dp')), parts along dimension 0, may hold values from 0 to 7; in each aligned block of 256 rows (0 to 255, 256 to 511, ..., all dimensions but the last counted through in order) at most 40 rows name the same one
- slot_index: int32 [256, 16], P(('pop', 'dp')), parts along dimension 0, may hold values from 0 to 47
- lengths: int32 [256], P(('pop', 'dp')), parts along dimension 0, may hold values from 897 to 1024, as said below
- value_up_weight: bfloat16 [128, 512, 128], P('tp'), may hold values from -0.25 to 0.25
Outputs:
- attn_out: bfloat16 [256, 16384], P(('pop', 'dp'), 'tp'), parts along dimension 0
The draws below stay inside these ranges and needn't reach their ends.
There are 2 independent parts, one for each index of `pop`. The reference program is written for one: setup_inputs(seed, part) draws one part's arguments, and reference() takes and returns one part's arrays. A program takes and returns all parts, laid end to end along the dimension named above; an argument that names none is the same for every part. Nothing has to cross between parts.
Inputs may be any that keep to these rules, and one draw needn't show every extreme that they name: `source_rank`: within the table rows of the 16 requests of one dp rank, no source rank is named more than 40 times; in some ranks' rows one source rank is named exactly 40 times. `lengths`: some request has the full length 1024.
All inputs are finite; a program needn't handle non-finite values.
Results may differ from the reference program's by a relative error of at most 0.0052.
Values may be sent and summed in bfloat16 or wider, within the bound.
A program may use at most 128 MiB of HBM per device.

```python
import math
import jax
import jax.numpy as jnp
import numpy as np
from jax import lax

H = 128
KVL = 512
RD = 64
VD = 128
BLK = 64
R_DEV = 16
MAXB = 16
SLOTS_DEV = 48
REQ = 128
POOL = 384
CAP = 40
N_DP = 8
N_TP = 2


def fresh_entry(key):
    base_key = jax.random.fold_in(key, 101)
    return jax.random.normal(base_key, (REQ, KVL + RD), jnp.float32)


def draw_new_entry(key, part):
    return fresh_entry(key).astype(jnp.bfloat16)


def draw_q_latent(key, part):
    own_key = jax.random.fold_in(key, 202)
    return jax.random.normal(own_key, (REQ, H, KVL), jnp.float32).astype(jnp.bfloat16)


def draw_q_rope(key, part):
    own_key = jax.random.fold_in(key, 303)
    return jax.random.normal(own_key, (REQ, H * RD), jnp.float32).astype(jnp.bfloat16)


def draw_lengths(key, part):
    raw_len = jax.random.randint(jax.random.fold_in(key, 2), (REQ,), 0, 2 * BLK)
    draw_len = (MAXB - 2) * BLK + 1 + raw_len
    chosen = jax.random.randint(jax.random.fold_in(key, 3), (), 0, REQ)
    return draw_len.at[chosen].set(MAXB * BLK).astype(jnp.int32)


def touch_ends(values, rng, low, largest):
    longest = values.shape.index(max(values.shape))
    spots = []
    for shift in (0, 1):
        where = [jax.random.randint(jax.random.fold_in(rng, axis), (), 0, length) for axis, length in enumerate(values.shape)]
        where[longest] = (where[longest] + shift) % values.shape[longest]
        spots.append(tuple(where))
    return values.at[spots[0]].set(low).at[spots[1]].set(largest)


def block_scale(rng, shape, split, least, largest):
    def one(axis_at, blocks):
        steps = jax.random.uniform(jax.random.fold_in(jax.random.fold_in(rng, 6), axis_at), (blocks,), jnp.float32, least / len(split), largest / len(split))
        return jnp.repeat(jnp.exp(steps), shape[axis_at] // blocks).reshape((-1,) + (1,) * (len(shape) - axis_at - 1))

    gain = one(*split[0])
    for cut in split[1:]:
        gain = gain * one(*cut)
    return gain


def deal_out(stream_key, own, number, rows, number_of, top, bound, slope):
    sequence = jax.random.permutation(stream_key, number_of)
    heavy_load, ordinary = shares(number_of, rows * top, bound, slope, True), shares(number_of, rows * top, bound, slope, False)
    places = jnp.arange(number_of)

    def named(tallies, offset_by):
        used = int((tallies > 0).sum())
        fixed = max(1, used // 4)
        moved = fixed + (places - fixed + offset_by * (used - fixed)) % max(1, number_of - fixed)
        return jnp.zeros((number_of,), jnp.int32).at[sequence[jnp.where(places < fixed, places, moved)]].set(jnp.asarray(tallies, jnp.int32))

    tallies = jnp.where(number % 4 == 0, named(heavy_load, number // 4), named(ordinary, number - number // 4 - 1))
    mixed = jax.random.permutation(jax.random.fold_in(own, 3), number_of)
    giver, sink = mixed[0:number_of // 2 * 2:2], mixed[1:number_of // 2 * 2:2]
    room = jnp.minimum(tallies[giver] - 1, bound - tallies[sink]) // 2
    room = jnp.where((giver == sequence[0]) | (sink == sequence[0]) | (tallies[sink] == 0), 0, jnp.maximum(room, 0))
    moved = jax.random.randint(jax.random.fold_in(own, 4), (number_of // 2,), 0, 1 << 20) % (room + 1)
    tallies = tallies.at[giver].add(-moved).at[sink].add(moved)
    members = jnp.searchsorted(jnp.cumsum(tallies), jnp.arange(rows * top), side="right").astype(jnp.int32)
    table = members.reshape(top, rows).T
    table = table[jax.random.permutation(jax.random.fold_in(own, 1), rows)]
    offset_by = jax.random.randint(jax.random.fold_in(own, 2), (rows, 1), 0, top)
    return jnp.take_along_axis(table, (jnp.arange(top)[None, :] + offset_by) % top, axis=1)


def shares(number_of, total, bound, skew, full):
    loads = [(1 << 20) // math.isqrt(rank ** skew) + 1 for rank in range(1, number_of + 1)]
    largest = bound if full else min(bound, max(-(-total // number_of), total * loads[0] // sum(loads)))
    least = 1 if total - largest >= number_of - 1 else 0
    counts, rest = [largest] + [least] * (number_of - 1), total - largest - least * (number_of - 1)
    while rest > 0:
        free = [i for i in range(1, number_of) if counts[i] < largest] or [i for i in range(1, number_of) if counts[i] < bound]
        whole, remaining = sum([loads[i] for i in free]), rest
        for i in free:
            addition = min(bound - counts[i], max(1, remaining * loads[i] // whole), rest)
            counts[i] = counts[i] + addition
            rest = rest - addition
    return np.array(counts)


def normal_values(rng, shape, deviation, most, shards=(), kind=jnp.bfloat16):
    values = jax.random.normal(rng, shape, jnp.float32) * deviation
    if len(shards) > 0:
        values = block_scale(rng, shape, shards, -0.22, 0.18) * values
    return jnp.clip(values, min=-most, max=most).astype(kind)


def setup_inputs(seed: int = 0, part: int = 0) -> dict:
    arg_keys = jax.random.split(jax.random.key(seed), 10)
    own_keys = jax.random.split(jax.random.fold_in(arg_keys[9], part), 10)
    q_latent = draw_q_latent(jax.random.fold_in(jax.random.fold_in(arg_keys[9], part), 71), part)
    q_rope = draw_q_rope(jax.random.fold_in(jax.random.fold_in(arg_keys[9], part), 71), part)
    new_entry = draw_new_entry(jax.random.fold_in(jax.random.fold_in(arg_keys[9], part), 71), part)
    cache_latent = normal_values(own_keys[3], (POOL, BLK, KVL), 1.0, 6.0, ((0, 8), (1, 2)))
    cache_rope = normal_values(own_keys[4], (POOL, BLK * RD), 1.0, 6.0, ((0, 8), (1, 2)))
    source_rank_keys = jax.random.split(jax.random.fold_in(own_keys[5], 1), REQ * MAXB // (R_DEV * MAXB))
    source_rank_turns = jax.random.permutation(jax.random.fold_in(own_keys[5], 3), REQ * MAXB // (R_DEV * MAXB))
    source_rank = jax.vmap(lambda own, number: deal_out(jax.random.fold_in(own_keys[5], 2), own, number, R_DEV * MAXB, N_DP, 1, CAP, 2))(source_rank_keys, source_rank_turns).reshape((REQ, MAXB, 1))
    slot_index = touch_ends(jax.random.randint(own_keys[6], (REQ, MAXB), 0, SLOTS_DEV), jax.random.fold_in(own_keys[6], 1), 0, SLOTS_DEV - 1).astype(jnp.int32)
    lengths = draw_lengths(jax.random.fold_in(jax.random.fold_in(arg_keys[9], part), 71), part)
    value_up_weight = normal_values(arg_keys[8], (H, KVL, VD), KVL ** -0.5, 0.25, ((0, 2),))
    return {"q_latent": q_latent, "q_rope": q_rope, "new_entry": new_entry, "cache_latent": cache_latent, "cache_rope": cache_rope, "source_rank": source_rank, "slot_index": slot_index, "lengths": lengths, "value_up_weight": value_up_weight}


softmax_scale = 192.0 ** -0.5
neg_fill = -1e30


def round_bf16(values):
    return lax.optimization_barrier(values.astype(jnp.bfloat16)).astype(jnp.float32)


def reference(q_latent, q_rope, new_entry, cache_latent, cache_rope, source_rank, slot_index, lengths, value_up_weight):
    run_count = N_TP
    run_len = BLK // run_count
    slot_ids = (source_rank[:, :, 0] * SLOTS_DEV + slot_index).astype(jnp.int32)
    offsets = jnp.arange(BLK, dtype=jnp.int32)
    run_of = offsets // run_len
    positions = jnp.arange(MAXB, dtype=jnp.int32)[:, None] * BLK + offsets[None, :]
    up_projection_weight = value_up_weight.astype(jnp.float32)

    def per_request(item_tuple):
        query_lat, query_rot, own_key, slot_row, length = item_tuple
        keys_lat = cache_latent[slot_row].astype(jnp.float32)
        keys_rot = cache_rope[slot_row].reshape(MAXB, BLK, RD).astype(jnp.float32)
        qlat = query_lat.astype(jnp.float32)
        qrot = query_rot.reshape(H, RD).astype(jnp.float32)
        scores = (jnp.einsum("hk,jpk->hjp", qlat, keys_lat) + jnp.einsum("hd,jpd->hjp", qrot, keys_rot)) * softmax_scale
        own_vals = own_key.astype(jnp.float32)
        new_score = (qlat @ own_vals[:KVL] + qrot @ own_vals[KVL:]) * softmax_scale
        in_range = positions < length
        maxima = []
        numerators = []
        denominators = []
        for run_index in range(run_count):
            selected = (in_range & (run_of == run_index)[None, :])[None, :, :]
            top_score = jnp.max(jnp.where(selected, scores, neg_fill), axis=(1, 2))
            if run_index == 0:
                top_score = jnp.maximum(top_score, new_score)
            expo = jnp.where(selected, jnp.exp(scores - top_score[:, None, None]), 0.0)
            numerator = jnp.einsum("hjp,jpk->hk", round_bf16(expo), keys_lat)
            denominator = jnp.sum(expo, axis=(1, 2))
            if run_index == 0:
                incoming_token_weight = jnp.exp(new_score - top_score)
                numerator = numerator + round_bf16(incoming_token_weight)[:, None] * own_vals[None, :KVL]
                denominator = denominator + incoming_token_weight
            maxima.append(top_score)
            numerators.append(numerator)
            denominators.append(denominator)
        overall = maxima[0]
        for top_score in maxima[1:]:
            overall = jnp.maximum(overall, top_score)
        total_num = jnp.zeros((H, KVL), jnp.float32)
        total_den = jnp.zeros((H,), jnp.float32)
        for run_index in range(run_count):
            factor = jnp.exp(maxima[run_index] - overall)
            total_num = total_num + factor[:, None] * numerators[run_index]
            total_den = total_den + factor * denominators[run_index]
        latent_output_rows = round_bf16(total_num / total_den[:, None])
        value_projected_output = jnp.einsum("en,enp->ep", latent_output_rows, up_projection_weight)
        return value_projected_output.reshape(H * VD).astype(jnp.bfloat16)

    return lax.map(per_request, (q_latent, q_rope, new_entry, slot_ids, lengths))
```

```python
import functools

import jax
import jax.numpy as jnp
from jax import lax
from jax.experimental import pallas as pl
from jax.experimental.pallas import tpu as pltpu
from jax.sharding import PartitionSpec as P

softmax_scale = 192.0 ** (-0.5)
neg_fill = -1e30


def entry_places(src_flat):
    count = src_flat.shape[0]
    spot = jnp.arange(count, dtype=jnp.int32)
    same = (src_flat[:, None] == src_flat[None, :]) & (spot[None, :] < spot[:, None])
    return jnp.sum(same.astype(jnp.int32), axis=1)


def pick(rows, index):
    onehot = (index[:, None] == jnp.arange(rows.shape[0], dtype=jnp.int32)[None, :]).astype(rows.dtype)
    flat = jnp.dot(onehot, rows.reshape(rows.shape[0], -1), preferred_element_type=jnp.float32)
    return flat.astype(rows.dtype).reshape((index.shape[0],) + rows.shape[1:])


def spread_local(
    q_latent,
    q_rope,
    new_entry,
    cache_latent,
    cache_rope,
    source_rank,
    slot_index,
    lengths,
    value_up_weight,
):
    rank_count = lax.axis_size("dp")
    lane_count = lax.axis_size("tp")
    my_lane = lax.axis_index("tp")
    requests, max_blocks = slot_index.shape
    run_len = cache_latent.shape[1]
    latent_dim = cache_latent.shape[2]
    heads = q_latent.shape[1]
    rope_dim = q_rope.shape[1] // heads
    entries = requests * max_blocks
    capacity = max(2, (entries * 5 + 4 * rank_count - 1) // (4 * rank_count))
    src_flat = source_rank.reshape(entries)
    slot_flat = slot_index.reshape(entries)
    places = entry_places(src_flat)
    where_from = src_flat * capacity + places
    cells = jnp.arange(rank_count * capacity, dtype=jnp.int32)
    wanted = jnp.sum(
        jnp.where(cells[:, None] == where_from[None, :], slot_flat[None, :], 0), axis=1
    ).reshape(rank_count, capacity)
    asked_slots = lax.all_to_all(wanted, "dp", split_axis=0, concat_axis=0, tiled=True)
    asked = asked_slots.reshape(rank_count * capacity)
    send_latent = pick(cache_latent, asked).reshape(rank_count, capacity, run_len, latent_dim)
    send_rope = pick(cache_rope, asked).reshape(rank_count, capacity, run_len * rope_dim)
    got_latent, received_rotary_keys = (
        lax.all_to_all(send_latent, "dp", split_axis=0, concat_axis=0, tiled=True),
        lax.all_to_all(send_rope, "dp", split_axis=0, concat_axis=0, tiled=True),
    )
    keys_latent = pick(got_latent.reshape(rank_count * capacity, run_len, latent_dim), where_from)
    keys_latent = keys_latent.reshape(requests, max_blocks * run_len, latent_dim)
    keys_rope = pick(
        received_rotary_keys.reshape(rank_count * capacity, run_len * rope_dim), where_from
    )
    keys_rope = keys_rope.reshape(requests, max_blocks * run_len, rope_dim)
    query_rope = q_rope.reshape(requests, heads, rope_dim)
    scores = jnp.einsum("rhk,rnk->rhn", q_latent, keys_latent, preferred_element_type=jnp.float32)
    scores = (
        scores
        + jnp.einsum("rhd,rnd->rhn", query_rope, keys_rope, preferred_element_type=jnp.float32)
    ) * softmax_scale
    new_latent = new_entry[:, :latent_dim]
    incoming_rotary_key = new_entry[:, latent_dim:]
    new_score = jnp.einsum("rhk,rk->rh", q_latent, new_latent, preferred_element_type=jnp.float32)
    new_score = (
        new_score
        + jnp.einsum(
            "rhd,rd->rh", query_rope, incoming_rotary_key, preferred_element_type=jnp.float32
        )
    ) * softmax_scale
    slot_pos = jnp.arange(max_blocks * run_len, dtype=jnp.int32)
    positions = (
        slot_pos // run_len * (run_len * lane_count) + my_lane * run_len + slot_pos % run_len
    )
    in_range = (positions[None, :] < lengths[:, None])[:, None, :]
    is_first = my_lane == 0
    top_score = jnp.max(jnp.where(in_range, scores, neg_fill), axis=2)
    top_score = jnp.where(is_first, jnp.maximum(top_score, new_score), top_score)
    expo = jnp.where(in_range, jnp.exp(scores - top_score[:, :, None]), 0.0)
    numerator = jnp.einsum(
        "rhn,rnk->rhk", expo.astype(jnp.bfloat16), keys_latent, preferred_element_type=jnp.float32
    )
    denominator = jnp.sum(expo, axis=2)
    incoming_token_weight = jnp.where(is_first, jnp.exp(new_score - top_score), 0.0)
    numerator = (
        numerator
        + incoming_token_weight.astype(jnp.bfloat16).astype(jnp.float32)[:, :, None]
        * new_latent.astype(jnp.float32)[:, None, :]
    )
    denominator = denominator + incoming_token_weight
    overall = lax.pmax(top_score, "tp")
    factor = jnp.exp(top_score - overall)
    numer_sum, denom_sum = (
        lax.psum_scatter(numerator * factor[:, :, None], "tp", scatter_dimension=1, tiled=True),
        lax.psum_scatter(denominator * factor, "tp", scatter_dimension=1, tiled=True),
    )
    latent_output_rows = (numer_sum / denom_sum[:, :, None]).astype(jnp.bfloat16)
    value_projected_output = jnp.einsum(
        "wyc,yca->wya", latent_output_rows, value_up_weight, preferred_element_type=jnp.float32
    )
    return value_projected_output.reshape(requests, -1).astype(jnp.bfloat16)


MESH = pl.DeviceIdType.MESH
up, down = 0, 1
depth, width, lanes = 4, 2, 2
chunk_count = 6


def dot_nt(a, b):
    return lax.dot_general(a, b, (((1,), (1,)), ((), ())), preferred_element_type=jnp.float32)


def loop(count, body, unroll=1):
    def step(i, carry):
        body(i)
        return carry

    lax.fori_loop(0, count, step, 0, unroll=unroll)


def plane_kernel(
    table_hbm,
    latent_hbm,
    rope_hbm,
    q_hbm,
    q_rope_hbm,
    value_hbm,
    new_entry,
    out,
    table_rows,
    table,
    latent,
    rope_pairs,
    rope,
    queries,
    query_pairs,
    value,
    keys,
    rope_keys,
    full,
    other,
    stats,
    other_stats,
    partials,
    partial_stats,
    got,
    got_stats,
    fresh,
    local_sem,
    table_send,
    table_recv,
    q_send,
    q_recv,
    y_send,
    y_recv,
    share_send,
    share_recv,
    swap_send,
    swap_recv,
    back_send,
    back_recv,
):
    me = lax.axis_index("dp")
    lane = lax.axis_index("tp")
    z, y = me // width, me % width
    slots, run_len, latent_dim = latent_hbm.shape
    requests, heads = q_hbm.shape[0], q_hbm.shape[1]
    batch = requests // lanes
    rope_dim = 64
    max_blocks = 16
    block_len = run_len * lanes
    count = max_blocks * block_len
    own_heads = heads // lanes
    value_dim = value.shape[2]
    chunk = slots // chunk_count
    has_up, has_down = z + 1 < depth, z > 0
    is_edge = (z == 0) | (z == depth - 1)
    mine = pl.ds(lane * batch, batch)

    def rank_at(s):
        near = jnp.where(s == 0, 1, jnp.where(s == 1, 0, s))
        step = jnp.where(is_edge, s, near)
        return jnp.where(z < depth // 2, step, depth - 1 - step)

    def remote(src, dst, send, recv, target):
        return pltpu.make_async_remote_copy(
            src_ref=src, dst_ref=dst, send_sem=send, recv_sem=recv, device_id=target, device_id_type=MESH
        )

    core = {"tp": 1 - lane}
    partner = {"dp": z * width + 1 - y}

    def at_plane(place):
        return {"dp": place * width + y}

    own_slots = pl.ds(y * slots, slots)
    local = [
        pltpu.make_async_copy(rope_hbm, rope_pairs.at[own_slots, lane], local_sem.at[0]),
        pltpu.make_async_copy(latent_hbm, latent.at[own_slots, lane], local_sem.at[1]),
        pltpu.make_async_copy(q_hbm.at[mine], queries.at[z], local_sem.at[2]),
        pltpu.make_async_copy(q_rope_hbm.at[mine], query_pairs.at[z], local_sem.at[3]),
        pltpu.make_async_copy(value_hbm, value, local_sem.at[4]),
        pltpu.make_async_copy(table_hbm, table_rows.at[z], local_sem.at[5]),
    ]

    barrier = pltpu.get_barrier_semaphore()

    def greet(target):
        pl.semaphore_signal(barrier, inc=1, device_id=target, device_id_type=MESH)

    greet(core)
    greet(partner)
    for t in range(1, depth):
        greet(at_plane((z + t) % depth))
    for copy in local:
        copy.start()
    pl.semaphore_wait(barrier, depth + 1)

    def q_copy(rank, c, way):
        target = at_plane(z + 1 if way == up else z - 1)
        return remote(
            queries.at[rank, c], queries.at[rank, c], q_send.at[way, rank, c], q_recv.at[rank, c], target
        )

    def q_rope_copy(rank, way):
        target = at_plane(z + 1 if way == up else z - 1)
        return remote(
            query_pairs.at[rank],
            query_pairs.at[rank],
            q_send.at[way, rank, batch],
            q_recv.at[rank, batch],
            target,
        )

    def ways(rank, body):
        pl.when(has_up & (rank <= z))(lambda: body(up))
        pl.when(has_down & (rank >= z))(lambda: body(down))

    def take(rank, c):
        q_copy(rank, c, up).wait_recv()
        ways(rank, lambda way: q_copy(rank, c, way).start())

    def take_rope(rank):
        q_rope_copy(rank, up).wait_recv()
        ways(rank, lambda way: q_rope_copy(rank, way).start())

    def table_copy(t):
        return remote(
            table_hbm, table_rows.at[z], table_send.at[t], table_recv.at[z], at_plane((z + t) % depth)
        )

    for t in range(1, depth):
        table_copy(t).start()

    def y_copy(c):
        return remote(
            latent_hbm.at[pl.ds(c * chunk, chunk)],
            latent.at[pl.ds(y * slots + c * chunk, chunk), lane],
            y_send.at[c],
            y_recv.at[c],
            partner,
        )

    def y_rope_copy():
        return remote(
            rope_hbm, rope_pairs.at[own_slots, lane], y_send.at[chunk_count], y_recv.at[chunk_count], partner
        )

    def share_copy(side, c):
        rows = pl.ds(side * slots + c * chunk, chunk)
        return remote(
            latent.at[rows, lane],
            latent.at[rows, lane],
            share_send.at[side, c],
            share_recv.at[side, c],
            core,
        )

    def share_rope_copy(side):
        rows = pl.ds(side * slots, slots)
        return remote(
            rope_pairs.at[rows, lane],
            rope_pairs.at[rows, lane],
            share_send.at[side, chunk_count],
            share_recv.at[side, chunk_count],
            core,
        )

    y_rope_copy().start()
    local[3].wait()
    ways(z, lambda way: q_rope_copy(z, way).start())
    local[2].wait()

    def first(c):
        ways(z, lambda way: q_copy(z, c, way).start())

    loop(batch, first)
    loop(chunk_count, lambda c: y_copy(c).start())
    local[0].wait()
    share_rope_copy(y).start()
    local[1].wait()
    loop(chunk_count, lambda c: share_copy(y, c).start())

    extra = new_entry[...].astype(jnp.float32)
    fresh[:, 0:latent_dim] = extra[:, :latent_dim]
    fresh[:, latent_dim : latent_dim + 2 * rope_dim] = jnp.concatenate(
        [extra[:, latent_dim:], extra[:, latent_dim:]], axis=1
    )
    stats[...] = jnp.zeros_like(stats)

    pair_row = lax.broadcasted_iota(jnp.int32, (2 * 64, 64), 0) // 2
    pair_col = lax.broadcasted_iota(jnp.int32, (2 * 64, 64), 1)
    doubler = jnp.where(pair_row == pair_col, 1.0, 0.0).astype(jnp.bfloat16)
    odd = lax.broadcasted_iota(jnp.int32, (128, 128), 0) % 2
    upper = lax.broadcasted_iota(jnp.int32, (128, 128), 1) // rope_dim
    own_part = odd == upper

    def unpaired(pairs):
        twice = jnp.dot(doubler, pairs, preferred_element_type=jnp.float32)
        return jnp.where(own_part, twice, 0.0)

    def expand(side):
        def one(p):
            rows = pl.ds(side * slots + 2 * p, 2)
            alone = unpaired(rope_pairs[rows].reshape(64, 128))
            both = alone + pltpu.roll(alone, rope_dim, 1)
            rope[rows] = both.astype(jnp.bfloat16).reshape(2, lanes, run_len, 128)

        loop(slots // 2, one, 4)

    share_rope_copy(y).wait_recv()
    expand(y)
    y_rope_copy().wait_recv()
    share_rope_copy(1 - y).start()
    take_rope(rank_at(1))
    pl.when(jnp.logical_not(is_edge))(lambda: take_rope(rank_at(2)))

    def early(c):
        take(rank_at(1), c)
        pl.when(jnp.logical_not(is_edge))(lambda: take(rank_at(2), c))

    def pass_block(c):
        y_copy(c).wait_recv()
        share_copy(1 - y, c).start()

    def both(c):
        early(2 * c)
        early(2 * c + 1)
        pass_block(c)

    share_rope_copy(1 - y).wait_recv()
    expand(1 - y)
    loop(batch // 2, both)
    loop(chunk_count - batch // 2, lambda c: pass_block(c + batch // 2))
    pl.when(jnp.logical_not(is_edge))(lambda: take_rope(rank_at(3)))

    for t in range(1, depth):
        table_copy_in = remote(
            table_hbm,
            table_rows.at[(z + t) % depth],
            table_send.at[t],
            table_recv.at[(z + t) % depth],
            at_plane((z + t) % depth),
        )
        table_copy_in.wait_recv()
    local[5].wait()
    into_smem = pltpu.make_async_copy(table_rows, table, local_sem.at[6])
    into_smem.start()
    into_smem.wait()
    local[4].wait()

    loop(chunk_count, lambda c: share_copy(y, c).wait_recv())
    loop(chunk_count, lambda c: share_copy(1 - y, c).wait_recv())

    in_block = lax.broadcasted_iota(jnp.int32, (heads, count), 1) % block_len
    left_half = lax.broadcasted_iota(jnp.int32, (1, 128), 1) < block_len
    stat_lane = lax.broadcasted_iota(jnp.int32, (heads, 128), 1)

    def swap(rank, i):
        return remote(
            full.at[rank, i, pl.ds((1 - lane) * own_heads, own_heads)],
            other.at[rank, i],
            swap_send.at[rank, i],
            swap_recv.at[rank, i],
            core,
        )

    def swap_stats(rank):
        return remote(
            stats.at[rank, pl.ds((1 - lane) * own_heads, own_heads)],
            other_stats.at[rank],
            swap_send.at[rank, batch],
            swap_recv.at[rank, batch],
            core,
        )

    def attend(rank, i, own):
        side = i % 2
        r = lane * batch + i
        length = table[rank, r, max_blocks]
        limits = []
        for j in range(max_blocks):
            block = table[rank, r, j] - z * (width * slots)
            here = (block >= 0) & (block < width * slots)
            block = jnp.where(here, block, 0)
            limits.append(jnp.where(here, length - j * block_len, 0))
            rows = pl.ds(j * block_len, block_len)
            keys[side, rows, :] = latent[block].reshape(block_len, latent_dim)
            rope_keys[side, rows, :] = rope[block].reshape(block_len, 128)
        limit = jnp.concatenate(
            [jnp.where(left_half, limits[2 * v], limits[2 * v + 1]) for v in range(max_blocks // 2)],
            axis=1,
        )
        q = queries[rank, i]
        q_rot = unpaired(query_pairs[rank, i])
        all_keys = keys[side]
        scores = dot_nt(q, all_keys) + dot_nt(q_rot.astype(jnp.bfloat16), rope_keys[side])
        in_range = in_block < jnp.broadcast_to(limit, (heads, count))
        scores = jnp.where(in_range, scores * softmax_scale, neg_fill)
        top = jnp.max(scores, axis=1, keepdims=True)
        if own:
            new = fresh[pl.ds(r, 1), :]
            new_latent = new[:, :latent_dim]
            new_score = jnp.sum(q.astype(jnp.float32) * new_latent, axis=1, keepdims=True)
            new_score = new_score + jnp.sum(q_rot * new[:, latent_dim:], axis=1, keepdims=True)
            new_score = new_score * softmax_scale
            top = jnp.maximum(top, new_score)
        expo = jnp.where(in_range, jnp.exp(scores - top), 0.0)
        den = jnp.sum(expo, axis=1, keepdims=True)
        num = jnp.dot(expo.astype(jnp.bfloat16), all_keys, preferred_element_type=jnp.float32)
        if own:
            weight = jnp.exp(new_score - top)
            den = den + weight
            num = num + weight.astype(jnp.bfloat16).astype(jnp.float32) * new_latent
        den = jnp.maximum(den, 1e-30)
        full[rank, i] = num / den
        stats[rank] = jnp.where(stat_lane == i, top + jnp.log(den), stats[rank])
        swap(rank, i).start()

    def project(rank):
        swap_stats(rank).wait_recv()
        own_stats = stats[rank, pl.ds(pl.multiple_of(lane * own_heads, own_heads), own_heads), :]
        both_stats = jnp.where(
            stat_lane[:own_heads] < batch, own_stats, pltpu.roll(other_stats[rank], batch, 1)
        )
        square = jnp.concatenate([both_stats, both_stats], axis=0)
        partial_stats[rank] = square.T[:requests]
        loop(batch, lambda i: swap(rank, i).wait_recv())

        def one(h):
            a = full[rank, :, pl.ds(lane * own_heads + h, 1), :].reshape(batch, latent_dim)
            b = other[rank, :, pl.ds(h, 1), :].reshape(batch, latent_dim)
            rows = jnp.concatenate([a, b], axis=0).astype(jnp.bfloat16)
            done = jnp.dot(rows, value[h], preferred_element_type=jnp.float32)
            columns = pl.ds(pl.multiple_of(h * value_dim, value_dim), value_dim)
            partials[rank, :, columns] = done.astype(jnp.bfloat16)

        loop(own_heads, one, 8)

    def back(rank):
        target = at_plane(rank)
        return [
            remote(partials.at[rank], got.at[z], back_send.at[rank, 0], back_recv.at[z, 0], target),
            remote(partial_stats.at[rank], got_stats.at[z], back_send.at[rank, 1], back_recv.at[z, 1], target),
        ]

    def finish(rank):
        project(rank)
        for copy in back(rank):
            copy.start()

    def own_one(i):
        attend(z, i, True)

    loop(batch, own_one, 2)
    swap_stats(z).start()

    def visit(s):
        rank = rank_at(s)
        pl.when(is_edge & (s >= 2))(lambda: take_rope(rank))

        def one(i):
            pl.when(is_edge & (s >= 2))(lambda: take(rank, i))
            pl.when(jnp.logical_not(is_edge) & (s == 1))(lambda: take(rank_at(3), i))
            attend(rank, i, False)

        loop(batch, one, 2)
        swap_stats(rank).start()
        finish(rank)

    def visits(s):
        pl.when(s == 2)(lambda: project(z))
        visit(s)

    loop(depth - 1, lambda s: visits(s + 1))

    def incoming(place):
        return [
            remote(partials.at[z], got.at[place], back_send.at[z, n], back_recv.at[place, n], at_plane(place))
            if n == 0
            else remote(
                partial_stats.at[z], got_stats.at[place], back_send.at[z, n], back_recv.at[place, n], at_plane(place)
            )
            for n in range(2)
        ]

    places = [(z + t) % depth for t in range(1, depth)]
    for place in places:
        for copy in incoming(place):
            copy.wait_recv()
    logs = [partial_stats[z]] + [got_stats[place] for place in places]
    best = functools.reduce(jnp.maximum, logs)
    weights = [jnp.exp(log - best) for log in logs]
    total = functools.reduce(jnp.add, weights)
    weights = [weight / total for weight in weights]
    for h in range(own_heads):
        columns = pl.ds(h * value_dim, value_dim)
        parts = [partials[z, :, columns]] + [got[place, :, columns] for place in places]
        mixed = sum(
            weight[:, h : h + 1] * part.astype(jnp.float32) for weight, part in zip(weights, parts)
        )
        turned = pltpu.roll(mixed, batch, 0)
        out[:, columns] = jnp.where(lane == 0, mixed, turned).astype(out.dtype)

    for t in range(1, depth):
        table_copy(t).wait_send()
    y_rope_copy().wait_send()
    loop(chunk_count, lambda c: y_copy(c).wait_send())
    for side in range(width):
        share_rope_copy(side).wait_send()
        loop(chunk_count, lambda c: share_copy(side, c).wait_send())

    def sent(rank):
        ways(rank, lambda way: q_rope_copy(rank, way).wait_send())
        loop(batch, lambda c: ways(rank, lambda way: q_copy(rank, c, way).wait_send()))
        loop(batch, lambda i: swap(rank, i).wait_send())
        swap_stats(rank).wait_send()

        @pl.when(rank != z)
        def _():
            for copy in back(rank):
                copy.wait_send()

    loop(depth, sent)


def plane_local(
    q_latent,
    q_rope,
    new_entry,
    cache_latent,
    cache_rope,
    source_rank,
    slot_index,
    lengths,
    value_up_weight,
):
    requests, max_blocks = slot_index.shape
    slots, run_len, latent_dim = cache_latent.shape
    heads = q_latent.shape[1]
    own_heads, _, value_dim = value_up_weight.shape
    batch = requests // lanes
    count = max_blocks * run_len * lanes
    bf16, f32 = jnp.bfloat16, jnp.float32
    listed = source_rank.reshape(requests, max_blocks) * slots + slot_index
    table = jnp.concatenate(
        [listed, lengths[:, None], jnp.zeros((requests, 127 - max_blocks), jnp.int32)], axis=1
    )
    vmem = pl.BlockSpec(memory_space=pltpu.VMEM)
    anywhere = pl.BlockSpec(memory_space=pl.ANY)
    dma = pltpu.SemaphoreType.DMA
    return pl.pallas_call(
        plane_kernel,
        out_shape=jax.ShapeDtypeStruct((requests, own_heads * value_dim), bf16),
        in_specs=[anywhere] * 6 + [vmem],
        out_specs=vmem,
        scratch_shapes=[
            pltpu.VMEM((depth, requests, 128), jnp.int32),
            pltpu.SMEM((depth, requests, 128), jnp.int32),
            pltpu.VMEM((width * slots, lanes, run_len, latent_dim), bf16),
            pltpu.VMEM((width * slots, lanes, run_len // 2, 128), bf16),
            pltpu.VMEM((width * slots, lanes, run_len, 128), bf16),
            pltpu.VMEM((depth, batch, heads, latent_dim), bf16),
            pltpu.VMEM((depth, batch, heads // 2, 128), bf16),
            pltpu.VMEM(value_up_weight.shape, bf16),
            pltpu.VMEM((2, count, latent_dim), bf16),
            pltpu.VMEM((2, count, 128), bf16),
            pltpu.VMEM((depth, batch, heads, latent_dim), f32),
            pltpu.VMEM((depth, batch, own_heads, latent_dim), f32),
            pltpu.VMEM((depth, heads, 128), f32),
            pltpu.VMEM((depth, own_heads, 128), f32),
            pltpu.VMEM((depth, requests, own_heads * value_dim), bf16),
            pltpu.VMEM((depth, requests, 128), f32),
            pltpu.VMEM((depth, requests, own_heads * value_dim), bf16),
            pltpu.VMEM((depth, requests, 128), f32),
            pltpu.VMEM((requests, latent_dim + 128), f32),
            dma((7,)),
            dma((depth,)),
            dma((depth,)),
            dma((2, depth, batch + 1)),
            dma((depth, batch + 1)),
            dma((chunk_count + 1,)),
            dma((chunk_count + 1,)),
            dma((width, chunk_count + 1)),
            dma((width, chunk_count + 1)),
            dma((depth, batch + 1)),
            dma((depth, batch + 1)),
            dma((depth, 2)),
            dma((depth, 2)),
        ],
        compiler_params=pltpu.CompilerParams(
            collective_id=0, has_side_effects=True, vmem_limit_bytes=60 * 1024 * 1024
        ),
    )(
        table,
        cache_latent,
        cache_rope.reshape(slots, run_len // 2, 128),
        q_latent,
        q_rope.reshape(requests, heads // 2, 128),
        value_up_weight,
        new_entry,
    )


def local(*args):
    q_latent, cache_latent, slot_index = args[0], args[3], args[6]
    fits = lax.axis_size("dp") == depth * width and lax.axis_size("tp") == lanes
    fits = fits and q_latent.shape == (16, 128, 512) and args[1].shape == (16, 8192)
    fits = fits and cache_latent.shape == (48, 32, 512) and slot_index.shape == (16, 16)
    return (plane_local if fits else spread_local)(*args)


def solution(mesh):
    placed = (
        P(("pop", "dp"), None, None),
        P(("pop", "dp"), None),
        P(("pop", "dp"), None),
        P(("pop", "dp"), "tp", None),
        P(("pop", "dp"), "tp"),
        P(("pop", "dp"), None, None),
        P(("pop", "dp"), None),
        P(("pop", "dp")),
        P("tp", None, None),
    )
    return jax.shard_map(
        local, mesh=mesh, in_specs=placed, out_specs=P(("pop", "dp"), "tp"), check_vma=False
    )
```

```python
import functools

import jax
import jax.numpy as jnp
from jax import lax
from jax.experimental import pallas as pl
from jax.experimental.pallas import tpu as pltpu
from jax.sharding import PartitionSpec as P

softmax_scale = 192.0 ** (-0.5)
neg_fill = -1e30


def entry_places(src_flat):
    count = src_flat.shape[0]
    spot = jnp.arange(count, dtype=jnp.int32)
    same = (src_flat[:, None] == src_flat[None, :]) & (spot[None, :] < spot[:, None])
    return jnp.sum(same.astype(jnp.int32), axis=1)


def pick(rows, index):
    onehot = (index[:, None] == jnp.arange(rows.shape[0], dtype=jnp.int32)[None, :]).astype(rows.dtype)
    flat = jnp.dot(onehot, rows.reshape(rows.shape[0], -1), preferred_element_type=jnp.float32)
    return flat.astype(rows.dtype).reshape((index.shape[0],) + rows.shape[1:])


def spread_local(
    q_latent,
    q_rope,
    new_entry,
    cache_latent,
    cache_rope,
    source_rank,
    slot_index,
    lengths,
    value_up_weight,
):
    rank_count = lax.axis_size("dp")
    lane_count = lax.axis_size("tp")
    my_lane = lax.axis_index("tp")
    requests, max_blocks = slot_index.shape
    run_len = cache_latent.shape[1]
    latent_dim = cache_latent.shape[2]
    heads = q_latent.shape[1]
    rope_dim = q_rope.shape[1] // heads
    entries = requests * max_blocks
    capacity = max(2, (entries * 5 + 4 * rank_count - 1) // (4 * rank_count))
    src_flat = source_rank.reshape(entries)
    slot_flat = slot_index.reshape(entries)
    places = entry_places(src_flat)
    where_from = src_flat * capacity + places
    cells = jnp.arange(rank_count * capacity, dtype=jnp.int32)
    wanted = jnp.sum(
        jnp.where(cells[:, None] == where_from[None, :], slot_flat[None, :], 0), axis=1
    ).reshape(rank_count, capacity)
    asked_slots = lax.all_to_all(wanted, "dp", split_axis=0, concat_axis=0, tiled=True)
    asked = asked_slots.reshape(rank_count * capacity)
    send_latent = pick(cache_latent, asked).reshape(rank_count, capacity, run_len, latent_dim)
    send_rope = pick(cache_rope, asked).reshape(rank_count, capacity, run_len * rope_dim)
    got_latent, received_rotary_keys = (
        lax.all_to_all(send_latent, "dp", split_axis=0, concat_axis=0, tiled=True),
        lax.all_to_all(send_rope, "dp", split_axis=0, concat_axis=0, tiled=True),
    )
    keys_latent = pick(got_latent.reshape(rank_count * capacity, run_len, latent_dim), where_from)
    keys_latent = keys_latent.reshape(requests, max_blocks * run_len, latent_dim)
    keys_rope = pick(
        received_rotary_keys.reshape(rank_count * capacity, run_len * rope_dim), where_from
    )
    keys_rope = keys_rope.reshape(requests, max_blocks * run_len, rope_dim)
    query_rope = q_rope.reshape(requests, heads, rope_dim)
    scores = jnp.einsum("rhk,rnk->rhn", q_latent, keys_latent, preferred_element_type=jnp.float32)
    scores = (
        scores
        + jnp.einsum("rhd,rnd->rhn", query_rope, keys_rope, preferred_element_type=jnp.float32)
    ) * softmax_scale
    new_latent = new_entry[:, :latent_dim]
    incoming_rotary_key = new_entry[:, latent_dim:]
    new_score = jnp.einsum("rhk,rk->rh", q_latent, new_latent, preferred_element_type=jnp.float32)
    new_score = (
        new_score
        + jnp.einsum(
            "rhd,rd->rh", query_rope, incoming_rotary_key, preferred_element_type=jnp.float32
        )
    ) * softmax_scale
    slot_pos = jnp.arange(max_blocks * run_len, dtype=jnp.int32)
    positions = (
        slot_pos // run_len * (run_len * lane_count) + my_lane * run_len + slot_pos % run_len
    )
    in_range = (positions[None, :] < lengths[:, None])[:, None, :]
    is_first = my_lane == 0
    top_score = jnp.max(jnp.where(in_range, scores, neg_fill), axis=2)
    top_score = jnp.where(is_first, jnp.maximum(top_score, new_score), top_score)
    expo = jnp.where(in_range, jnp.exp(scores - top_score[:, :, None]), 0.0)
    numerator = jnp.einsum(
        "rhn,rnk->rhk", expo.astype(jnp.bfloat16), keys_latent, preferred_element_type=jnp.float32
    )
    denominator = jnp.sum(expo, axis=2)
    incoming_token_weight = jnp.where(is_first, jnp.exp(new_score - top_score), 0.0)
    numerator = (
        numerator
        + incoming_token_weight.astype(jnp.bfloat16).astype(jnp.float32)[:, :, None]
        * new_latent.astype(jnp.float32)[:, None, :]
    )
    denominator = denominator + incoming_token_weight
    overall = lax.pmax(top_score, "tp")
    factor = jnp.exp(top_score - overall)
    numer_sum, denom_sum = (
        lax.psum_scatter(numerator * factor[:, :, None], "tp", scatter_dimension=1, tiled=True),
        lax.psum_scatter(denominator * factor, "tp", scatter_dimension=1, tiled=True),
    )
    latent_output_rows = (numer_sum / denom_sum[:, :, None]).astype(jnp.bfloat16)
    value_projected_output = jnp.einsum(
        "wyc,yca->wya", latent_output_rows, value_up_weight, preferred_element_type=jnp.float32
    )
    return value_projected_output.reshape(requests, -1).astype(jnp.bfloat16)


MESH = pl.DeviceIdType.MESH
up, down = 0, 1
depth, width, lanes = 4, 2, 2
chunk_count = 6


def dot_nt(a, b):
    return lax.dot_general(a, b, (((1,), (1,)), ((), ())), preferred_element_type=jnp.float32)


def loop(count, body, unroll=1):
    def step(i, carry):
        body(i)
        return carry

    lax.fori_loop(0, count, step, 0, unroll=unroll)


def plane_kernel(
    sources,
    slot_table,
    lengths,
    latent_hbm,
    rope_hbm,
    q_hbm,
    q_rope_hbm,
    value_hbm,
    new_entry,
    out,
    table_rows,
    table,
    rope_in,
    rope_wide,
    q_rope_in,
    q_rope_wide,
    latent,
    rope_pairs,
    rope,
    queries,
    query_pairs,
    value,
    keys,
    rope_keys,
    full,
    other,
    stats,
    other_stats,
    partials,
    leaving,
    partial_stats,
    got,
    got_stats,
    fresh,
    local_sem,
    table_send,
    table_recv,
    q_send,
    q_recv,
    y_send,
    y_recv,
    share_send,
    share_recv,
    swap_send,
    swap_recv,
    back_send,
    back_recv,
):
    me = lax.axis_index("dp")
    lane = lax.axis_index("tp")
    z, y = me // width, me % width
    slots, run_len, latent_dim = latent_hbm.shape
    requests, heads = q_hbm.shape[0], q_hbm.shape[1]
    batch = requests // lanes
    rope_dim = q_rope_in.shape[1] // heads
    max_blocks = slot_table.shape[1]
    block_len = run_len * lanes
    count = max_blocks * block_len
    own_heads = heads // lanes
    value_dim = value.shape[2]
    chunk = slots // chunk_count
    has_up, has_down = z + 1 < depth, z > 0
    is_edge = (z == 0) | (z == depth - 1)
    mine = pl.ds(lane * batch, batch)

    is_middle = jnp.logical_not(is_edge)
    near_edge = jnp.where(z < depth // 2, 0, depth - 1)
    far_edge = depth - 1 - near_edge
    near_middle = jnp.where(z < depth // 2, 1, depth - 2)
    far_middle = depth - 1 - near_middle

    def rank_at(s):
        inner = jnp.where(s == 1, far_edge, jnp.where(s == 2, far_middle, near_edge))
        outer = jnp.where(s == 1, near_middle, jnp.where(s == 2, far_middle, far_edge))
        return jnp.where(s == 0, z, jnp.where(is_edge, outer, inner))

    def remote(src, dst, send, recv, target):
        return pltpu.make_async_remote_copy(
            src_ref=src, dst_ref=dst, send_sem=send, recv_sem=recv, device_id=target, device_id_type=MESH
        )

    core = {"tp": 1 - lane}
    partner = {"dp": z * width + 1 - y}

    def at_plane(place):
        return {"dp": place * width + y}

    own_slots = pl.ds(y * slots, slots)
    local = [
        pltpu.make_async_copy(q_rope_hbm, q_rope_in, local_sem.at[0]),
        pltpu.make_async_copy(rope_hbm, rope_in, local_sem.at[1]),
        pltpu.make_async_copy(latent_hbm, latent.at[own_slots, lane], local_sem.at[2]),
        pltpu.make_async_copy(q_hbm.at[mine], queries.at[z], local_sem.at[3]),
        pltpu.make_async_copy(value_hbm, value, local_sem.at[4]),
    ]

    barrier = pltpu.get_barrier_semaphore()

    def greet(target):
        pl.semaphore_signal(barrier, inc=1, device_id=target, device_id_type=MESH)

    greet(core)
    greet(partner)
    for t in range(1, depth):
        greet(at_plane((z + t) % depth))
    for copy in local[:3]:
        copy.start()
    pl.semaphore_wait(barrier, depth + 1)

    def q_copy(rank, c, way):
        target = at_plane(z + 1 if way == up else z - 1)
        return remote(
            queries.at[rank, c], queries.at[rank, c], q_send.at[way, rank, c], q_recv.at[rank, c], target
        )

    def q_rope_copy(rank, way):
        target = at_plane(z + 1 if way == up else z - 1)
        return remote(
            query_pairs.at[rank],
            query_pairs.at[rank],
            q_send.at[way, rank, batch],
            q_recv.at[rank, batch],
            target,
        )

    def ways(rank, body):
        pl.when(has_up & (rank <= z))(lambda: body(up))
        pl.when(has_down & (rank >= z))(lambda: body(down))

    def own_q_copy(c, way):
        target = at_plane(z + 1 if way == up else z - 1)
        return remote(
            q_hbm.at[lane * batch + c], queries.at[z, c], q_send.at[way, z, c], q_recv.at[z, c], target
        )

    def take(rank, c):
        q_copy(rank, c, up).wait_recv()
        ways(rank, lambda way: q_copy(rank, c, way).start())

    def take_rope(rank):
        q_rope_copy(rank, up).wait_recv()
        ways(rank, lambda way: q_rope_copy(rank, way).start())

    def table_copy(t):
        return remote(
            table_rows.at[z], table_rows.at[z], table_send.at[t], table_recv.at[z], at_plane((z + t) % depth)
        )

    def y_copy(c):
        return remote(
            latent_hbm.at[pl.ds(c * chunk, chunk)],
            latent.at[pl.ds(y * slots + c * chunk, chunk), lane],
            y_send.at[c],
            y_recv.at[c],
            partner,
        )

    def y_rope_copy():
        own = rope_pairs.at[own_slots, lane]
        return remote(own, own, y_send.at[chunk_count], y_recv.at[chunk_count], partner)

    def share_copy(side, c):
        rows = pl.ds(side * slots + c * chunk, chunk)
        return remote(
            latent.at[rows, lane],
            latent.at[rows, lane],
            share_send.at[side, c],
            share_recv.at[side, c],
            core,
        )

    def share_rope_copy(side):
        rows = pl.ds(side * slots, slots)
        return remote(
            rope_pairs.at[rows, lane],
            rope_pairs.at[rows, lane],
            share_send.at[side, chunk_count],
            share_recv.at[side, chunk_count],
            core,
        )

    def first(c):
        ways(z, lambda way: own_q_copy(c, way).start())

    first(0)
    loop(chunk_count, lambda c: y_copy(c).start())
    local[3].start()

    local[1].wait()
    for j in range(run_len // 2):
        rope_wide[:, j : j + 1, :] = (
            rope_in[:, j * 128 : (j + 1) * 128].astype(jnp.float32).reshape(slots, 1, 128)
        )
    rope_pairs[own_slots, lane] = rope_wide[...].astype(jnp.bfloat16)
    y_rope_copy().start()
    share_rope_copy(y).start()
    local[0].wait()

    def spread(p):
        x = q_rope_in[:, pl.ds(pl.multiple_of(p * 128, 128), 128)].astype(jnp.float32)
        x = jnp.where(lane == 0, x[:batch], x[batch:])
        q_rope_wide[:, pl.ds(p, 1), :] = x.reshape(batch, 1, 128)

    loop(heads // 2, spread, 8)
    query_pairs[z] = q_rope_wide[...].astype(jnp.bfloat16)
    ways(z, lambda way: q_rope_copy(z, way).start())
    loop(batch - 1, lambda c: first(c + 1))
    local[2].wait()
    loop(chunk_count, lambda c: share_copy(y, c).start())
    local[4].start()

    row = lax.broadcasted_iota(jnp.int32, (requests, 128), 0)
    length_rows = jnp.zeros((requests, 128), jnp.int32)
    for r in range(requests):
        length_rows = jnp.where(row == r, lengths[r], length_rows)
    table_rows[z] = length_rows
    table_rows[z, :, 0:max_blocks] = sources[...] * slots + slot_table[...]
    for t in range(1, depth):
        table_copy(t).start()

    extra = new_entry[...].astype(jnp.float32)
    fresh[:, 0:latent_dim] = extra[:, :latent_dim]
    fresh[:, latent_dim : latent_dim + 2 * rope_dim] = jnp.concatenate(
        [extra[:, latent_dim:], extra[:, latent_dim:]], axis=1
    )
    stats[...] = jnp.zeros_like(stats)

    pair_row = lax.broadcasted_iota(jnp.int32, (2 * 64, 64), 0) // 2
    pair_col = lax.broadcasted_iota(jnp.int32, (2 * 64, 64), 1)
    doubler = jnp.where(pair_row == pair_col, 1.0, 0.0).astype(jnp.bfloat16)
    odd = lax.broadcasted_iota(jnp.int32, (128, 128), 0) % 2
    upper = lax.broadcasted_iota(jnp.int32, (128, 128), 1) // rope_dim
    own_part = odd == upper

    def unpaired(pairs):
        twice = jnp.dot(doubler, pairs, preferred_element_type=jnp.float32)
        return jnp.where(own_part, twice, 0.0)

    def expand(side):
        def one(p):
            rows = pl.ds(side * slots + 2 * p, 2)
            alone = unpaired(rope_pairs[rows].reshape(64, 128))
            both = alone + pltpu.roll(alone, rope_dim, 1)
            rope[rows] = both.astype(jnp.bfloat16).reshape(2, lanes, run_len, 128)

        loop(slots // 2, one, 4)

    share_rope_copy(y).wait_recv()
    expand(y)
    y_rope_copy().wait_recv()
    share_rope_copy(1 - y).start()
    beside = jnp.where(is_edge, near_middle, near_edge)

    def early(c):
        take(beside, c)
        pl.when(is_middle)(lambda: take(far_middle, c))

    def pass_block(c):
        y_copy(c).wait_recv()
        share_copy(1 - y, c).start()

    def both(c):
        early(2 * c)
        early(2 * c + 1)
        pass_block(c)

    share_rope_copy(1 - y).wait_recv()
    expand(1 - y)
    early(0)
    take_rope(beside)
    pl.when(is_middle)(lambda: take_rope(far_middle))
    early(1)
    pass_block(0)
    loop(batch // 2 - 1, lambda c: both(c + 1))
    loop(chunk_count - batch // 2, lambda c: pass_block(c + batch // 2))

    for t in range(1, depth):
        table_copy_in = remote(
            table_rows.at[z],
            table_rows.at[(z + t) % depth],
            table_send.at[t],
            table_recv.at[(z + t) % depth],
            at_plane((z + t) % depth),
        )
        table_copy_in.wait_recv()
    into_smem = pltpu.make_async_copy(table_rows, table, local_sem.at[5])
    into_smem.start()
    into_smem.wait()
    local[3].wait()
    local[4].wait()

    loop(chunk_count, lambda c: share_copy(y, c).wait_recv())
    loop(chunk_count, lambda c: share_copy(1 - y, c).wait_recv())

    in_block = lax.broadcasted_iota(jnp.int32, (heads, count), 1) % block_len
    left_half = lax.broadcasted_iota(jnp.int32, (1, 128), 1) < block_len
    stat_lane = lax.broadcasted_iota(jnp.int32, (heads, 128), 1)

    def swap(rank, i):
        return remote(
            full.at[rank, i, pl.ds((1 - lane) * own_heads, own_heads)],
            other.at[rank, i],
            swap_send.at[rank, i],
            swap_recv.at[rank, i],
            core,
        )

    def swap_stats(rank):
        return remote(
            stats.at[rank, pl.ds((1 - lane) * own_heads, own_heads)],
            other_stats.at[rank],
            swap_send.at[rank, batch],
            swap_recv.at[rank, batch],
            core,
        )

    def attend(rank, i, own):
        side = i % 2
        r = lane * batch + i
        length = table[rank, r, max_blocks]
        limits = []
        for j in range(max_blocks):
            block = table[rank, r, j] - z * (width * slots)
            here = (block >= 0) & (block < width * slots)
            block = jnp.where(here, block, 0)
            limits.append(jnp.where(here, length - j * block_len, 0))
            rows = pl.ds(j * block_len, block_len)
            keys[side, rows, :] = latent[block].reshape(block_len, latent_dim)
            rope_keys[side, rows, :] = rope[block].reshape(block_len, 128)
        limit = jnp.concatenate(
            [jnp.where(left_half, limits[2 * v], limits[2 * v + 1]) for v in range(max_blocks // 2)],
            axis=1,
        )
        q = queries[rank, i]
        q_rot = unpaired(query_pairs[rank, i])
        all_keys = keys[side]
        scores = dot_nt(q, all_keys) + dot_nt(q_rot.astype(jnp.bfloat16), rope_keys[side])
        in_range = in_block < jnp.broadcast_to(limit, (heads, count))
        scores = jnp.where(in_range, scores * softmax_scale, neg_fill)
        top = jnp.max(scores, axis=1, keepdims=True)
        if own:
            new = fresh[pl.ds(r, 1), :]
            new_latent = new[:, :latent_dim]
            new_score = jnp.sum(q.astype(jnp.float32) * new_latent, axis=1, keepdims=True)
            new_score = new_score + jnp.sum(q_rot * new[:, latent_dim:], axis=1, keepdims=True)
            new_score = new_score * softmax_scale
            top = jnp.maximum(top, new_score)
        expo = jnp.where(in_range, jnp.exp(scores - top), 0.0)
        den = jnp.sum(expo, axis=1, keepdims=True)
        num = jnp.dot(expo.astype(jnp.bfloat16), all_keys, preferred_element_type=jnp.float32)
        if own:
            weight = jnp.exp(new_score - top)
            den = den + weight
            num = num + weight.astype(jnp.bfloat16).astype(jnp.float32) * new_latent
        den = jnp.maximum(den, 1e-30)
        full[rank, i] = num / den
        stats[rank] = jnp.where(stat_lane == i, top + jnp.log(den), stats[rank])
        swap(rank, i).start()

    def project(rank):
        swap_stats(rank).wait_recv()
        own_stats = stats[rank, pl.ds(pl.multiple_of(lane * own_heads, own_heads), own_heads), :]
        both_stats = jnp.where(
            stat_lane[:own_heads] < batch, own_stats, pltpu.roll(other_stats[rank], batch, 1)
        )
        square = jnp.concatenate([both_stats, both_stats], axis=0)
        partial_stats[rank] = square.T[:requests]
        loop(batch, lambda i: swap(rank, i).wait_recv())

        def one(h):
            a = full[rank, :, pl.ds(lane * own_heads + h, 1), :].reshape(batch, latent_dim)
            b = other[rank, :, pl.ds(h, 1), :].reshape(batch, latent_dim)
            rows = jnp.concatenate([a, b], axis=0).astype(jnp.bfloat16)
            done = jnp.dot(rows, value[h], preferred_element_type=jnp.float32)
            columns = pl.ds(pl.multiple_of(h * value_dim, value_dim), value_dim)
            partials[rank, :, columns] = done

        loop(own_heads, one, 8)

    def back(rank):
        slot = jnp.where(is_middle & (rank == far_edge), depth, z)
        target = at_plane(jnp.where(is_middle & (rank == far_edge), far_middle, rank))
        return [
            remote(leaving.at[rank], got.at[slot], back_send.at[rank, 0], back_recv.at[slot, 0], target),
            remote(
                partial_stats.at[rank], got_stats.at[slot], back_send.at[rank, 1], back_recv.at[slot, 1], target
            ),
        ]

    def arrive(slot):
        remote(leaving.at[z], got.at[slot], back_send.at[z, 0], back_recv.at[slot, 0], at_plane(beside)).wait_recv()
        remote(
            partial_stats.at[z], got_stats.at[slot], back_send.at[z, 1], back_recv.at[slot, 1], at_plane(beside)
        ).wait_recv()

    def mixture(logs):
        best = functools.reduce(jnp.maximum, logs)
        weights = [jnp.exp(log - best) for log in logs]
        total = functools.reduce(jnp.add, weights)
        return [weight / total for weight in weights], best + jnp.log(total)

    def mix(rank, slots_in, put):
        logs = [partial_stats[rank]] + [got_stats[slot] for slot in slots_in]
        weights, log = mixture(logs)
        for h in range(own_heads):
            columns = pl.ds(h * value_dim, value_dim)
            parts = [partials[rank, :, columns]] + [got[slot, :, columns] for slot in slots_in]
            put(
                columns,
                sum(weight[:, h : h + 1] * part.astype(jnp.float32) for weight, part in zip(weights, parts)),
            )
        return log

    def finish(rank):
        project(rank)
        via = is_middle & (rank == near_edge)

        @pl.when(via)
        def _():
            arrive(depth)

            def put(columns, values):
                leaving[rank, :, columns] = values.astype(jnp.bfloat16)

            partial_stats[rank] = mix(rank, [depth], put)

        @pl.when(jnp.logical_not(via))
        def _():
            def pack(h):
                columns = pl.ds(pl.multiple_of(h * value_dim, value_dim), value_dim)
                leaving[rank, :, columns] = partials[rank, :, columns].astype(jnp.bfloat16)

            loop(own_heads, pack, 8)

        for copy in back(rank):
            copy.start()

    def own_one(i):
        pl.when(is_middle)(lambda: take(far_edge, i))
        pl.when(is_middle & (i == 0))(lambda: take_rope(far_edge))
        attend(z, i, True)

    loop(batch, own_one, 2)
    swap_stats(z).start()

    def visit(s):
        rank = rank_at(s)
        def one(i):
            pl.when(is_edge & (s >= 2))(lambda: take(rank, i))
            pl.when(is_edge & (s >= 2) & (i == 0))(lambda: take_rope(rank))
            attend(rank, i, False)

        loop(batch, one, 2)
        swap_stats(rank).start()
        finish(rank)
        pl.when(s == 2)(lambda: project(z))

    loop(depth - 1, lambda s: visit(s + 1))

    def put_out(columns, values):
        turned = pltpu.roll(values, batch, 0)
        out[:, columns] = jnp.where(lane == 0, values, turned).astype(out.dtype)

    @pl.when(is_edge)
    def _():
        arrive(near_middle)
        arrive(far_edge)
        mix(z, [near_middle, far_edge], put_out)

    @pl.when(is_middle)
    def _():
        places = [near_edge, far_middle, far_edge]
        for place in places:
            arrive(place)
        mix(z, places, put_out)

    for t in range(1, depth):
        table_copy(t).wait_send()
    y_rope_copy().wait_send()
    loop(chunk_count, lambda c: y_copy(c).wait_send())
    for side in range(width):
        share_rope_copy(side).wait_send()
        loop(chunk_count, lambda c: share_copy(side, c).wait_send())

    def sent(rank):
        ways(rank, lambda way: q_rope_copy(rank, way).wait_send())
        loop(batch, lambda c: ways(rank, lambda way: q_copy(rank, c, way).wait_send()))
        loop(batch, lambda i: swap(rank, i).wait_send())
        swap_stats(rank).wait_send()

        @pl.when(rank != z)
        def _():
            for copy in back(rank):
                copy.wait_send()

    loop(depth, sent)


def plane_local(
    q_latent,
    q_rope,
    new_entry,
    cache_latent,
    cache_rope,
    source_rank,
    slot_index,
    lengths,
    value_up_weight,
):
    requests, max_blocks = slot_index.shape
    slots, run_len, latent_dim = cache_latent.shape
    heads = q_latent.shape[1]
    own_heads, _, value_dim = value_up_weight.shape
    batch = requests // lanes
    count = max_blocks * run_len * lanes
    bf16, f32 = jnp.bfloat16, jnp.float32
    vmem = pl.BlockSpec(memory_space=pltpu.VMEM)
    smem = pl.BlockSpec(memory_space=pltpu.SMEM)
    anywhere = pl.BlockSpec(memory_space=pl.ANY)
    dma = pltpu.SemaphoreType.DMA
    return pl.pallas_call(
        plane_kernel,
        out_shape=jax.ShapeDtypeStruct((requests, own_heads * value_dim), bf16),
        in_specs=[vmem, vmem, smem] + [anywhere] * 5 + [vmem],
        out_specs=vmem,
        scratch_shapes=[
            pltpu.VMEM((depth, requests, 128), jnp.int32),
            pltpu.SMEM((depth, requests, 128), jnp.int32),
            pltpu.VMEM(cache_rope.shape, bf16),
            pltpu.VMEM((slots, run_len // 2, 128), f32),
            pltpu.VMEM(q_rope.shape, bf16),
            pltpu.VMEM((batch, heads // 2, 128), f32),
            pltpu.VMEM((width * slots, lanes, run_len, latent_dim), bf16),
            pltpu.VMEM((width * slots, lanes, run_len // 2, 128), bf16),
            pltpu.VMEM((width * slots, lanes, run_len, 128), bf16),
            pltpu.VMEM((depth, batch, heads, latent_dim), bf16),
            pltpu.VMEM((depth, batch, heads // 2, 128), bf16),
            pltpu.VMEM(value_up_weight.shape, bf16),
            pltpu.VMEM((2, count, latent_dim), bf16),
            pltpu.VMEM((2, count, 128), bf16),
            pltpu.VMEM((depth, batch, heads, latent_dim), f32),
            pltpu.VMEM((depth, batch, own_heads, latent_dim), f32),
            pltpu.VMEM((depth, heads, 128), f32),
            pltpu.VMEM((depth, own_heads, 128), f32),
            pltpu.VMEM((depth, requests, own_heads * value_dim), f32),
            pltpu.VMEM((depth, requests, own_heads * value_dim), bf16),
            pltpu.VMEM((depth, requests, 128), f32),
            pltpu.VMEM((depth + 1, requests, own_heads * value_dim), bf16),
            pltpu.VMEM((depth + 1, requests, 128), f32),
            pltpu.VMEM((requests, latent_dim + 128), f32),
            dma((6,)),
            dma((depth,)),
            dma((depth,)),
            dma((2, depth, batch + 1)),
            dma((depth, batch + 1)),
            dma((chunk_count + 1,)),
            dma((chunk_count + 1,)),
            dma((width, chunk_count + 1)),
            dma((width, chunk_count + 1)),
            dma((depth, batch + 1)),
            dma((depth, batch + 1)),
            dma((depth, 2)),
            dma((depth + 1, 2)),
        ],
        compiler_params=pltpu.CompilerParams(
            collective_id=0, has_side_effects=True, vmem_limit_bytes=60 * 1024 * 1024
        ),
    )(
        source_rank.reshape(requests, max_blocks),
        slot_index,
        lengths,
        cache_latent,
        cache_rope,
        q_latent,
        q_rope,
        value_up_weight,
        new_entry,
    )


def local(*args):
    q_latent, cache_latent, slot_index = args[0], args[3], args[6]
    fits = lax.axis_size("dp") == depth * width and lax.axis_size("tp") == lanes
    fits = fits and q_latent.shape == (16, 128, 512) and args[1].shape == (16, 8192)
    fits = fits and cache_latent.shape == (48, 32, 512) and slot_index.shape == (16, 16)
    return (plane_local if fits else spread_local)(*args)


def solution(mesh):
    placed = (
        P(("pop", "dp"), None, None),
        P(("pop", "dp"), None),
        P(("pop", "dp"), None),
        P(("pop", "dp"), "tp", None),
        P(("pop", "dp"), "tp"),
        P(("pop", "dp"), None, None),
        P(("pop", "dp"), None),
        P(("pop", "dp")),
        P("tp", None, None),
    )
    return jax.shard_map(
        local, mesh=mesh, in_specs=placed, out_specs=P(("pop", "dp"), "tp"), check_vma=False
    )
```

```python
import functools
import math

import jax
import jax.numpy as jnp
from jax import lax
from jax.experimental import pallas as pl
from jax.experimental.pallas import tpu as pltpu
from jax.sharding import PartitionSpec as P

softmax_scale = 192.0 ** (-0.5)
neg_fill = -1e30


def entry_places(src_flat):
    count = src_flat.shape[0]
    spot = jnp.arange(count, dtype=jnp.int32)
    same = (src_flat[:, None] == src_flat[None, :]) & (spot[None, :] < spot[:, None])
    return jnp.sum(same.astype(jnp.int32), axis=1)


def pick(rows, index):
    onehot = (index[:, None] == jnp.arange(rows.shape[0], dtype=jnp.int32)[None, :]).astype(rows.dtype)
    flat = jnp.dot(onehot, rows.reshape(rows.shape[0], -1), preferred_element_type=jnp.float32)
    return flat.astype(rows.dtype).reshape((index.shape[0],) + rows.shape[1:])


def spread_local(
    q_latent,
    q_rope,
    new_entry,
    cache_latent,
    cache_rope,
    source_rank,
    slot_index,
    lengths,
    value_up_weight,
):
    rank_count = lax.axis_size("dp")
    lane_count = lax.axis_size("tp")
    my_lane = lax.axis_index("tp")
    requests, max_blocks = slot_index.shape
    run_len = cache_latent.shape[1]
    latent_dim = cache_latent.shape[2]
    heads = q_latent.shape[1]
    rope_dim = q_rope.shape[1] // heads
    entries = requests * max_blocks
    capacity = max(2, (entries * 5 + 4 * rank_count - 1) // (4 * rank_count))
    src_flat = source_rank.reshape(entries)
    slot_flat = slot_index.reshape(entries)
    places = entry_places(src_flat)
    where_from = src_flat * capacity + places
    cells = jnp.arange(rank_count * capacity, dtype=jnp.int32)
    wanted = jnp.sum(
        jnp.where(cells[:, None] == where_from[None, :], slot_flat[None, :], 0), axis=1
    ).reshape(rank_count, capacity)
    asked_slots = lax.all_to_all(wanted, "dp", split_axis=0, concat_axis=0, tiled=True)
    asked = asked_slots.reshape(rank_count * capacity)
    send_latent = pick(cache_latent, asked).reshape(rank_count, capacity, run_len, latent_dim)
    send_rope = pick(cache_rope, asked).reshape(rank_count, capacity, run_len * rope_dim)
    got_latent, received_rotary_keys = (
        lax.all_to_all(send_latent, "dp", split_axis=0, concat_axis=0, tiled=True),
        lax.all_to_all(send_rope, "dp", split_axis=0, concat_axis=0, tiled=True),
    )
    keys_latent = pick(got_latent.reshape(rank_count * capacity, run_len, latent_dim), where_from)
    keys_latent = keys_latent.reshape(requests, max_blocks * run_len, latent_dim)
    keys_rope = pick(
        received_rotary_keys.reshape(rank_count * capacity, run_len * rope_dim), where_from
    )
    keys_rope = keys_rope.reshape(requests, max_blocks * run_len, rope_dim)
    query_rope = q_rope.reshape(requests, heads, rope_dim)
    scores = jnp.einsum("rhk,rnk->rhn", q_latent, keys_latent, preferred_element_type=jnp.float32)
    scores = (
        scores
        + jnp.einsum("rhd,rnd->rhn", query_rope, keys_rope, preferred_element_type=jnp.float32)
    ) * softmax_scale
    new_latent = new_entry[:, :latent_dim]
    incoming_rotary_key = new_entry[:, latent_dim:]
    new_score = jnp.einsum("rhk,rk->rh", q_latent, new_latent, preferred_element_type=jnp.float32)
    new_score = (
        new_score
        + jnp.einsum(
            "rhd,rd->rh", query_rope, incoming_rotary_key, preferred_element_type=jnp.float32
        )
    ) * softmax_scale
    slot_pos = jnp.arange(max_blocks * run_len, dtype=jnp.int32)
    positions = (
        slot_pos // run_len * (run_len * lane_count) + my_lane * run_len + slot_pos % run_len
    )
    in_range = (positions[None, :] < lengths[:, None])[:, None, :]
    is_first = my_lane == 0
    top_score = jnp.max(jnp.where(in_range, scores, neg_fill), axis=2)
    top_score = jnp.where(is_first, jnp.maximum(top_score, new_score), top_score)
    expo = jnp.where(in_range, jnp.exp(scores - top_score[:, :, None]), 0.0)
    numerator = jnp.einsum(
        "rhn,rnk->rhk", expo.astype(jnp.bfloat16), keys_latent, preferred_element_type=jnp.float32
    )
    denominator = jnp.sum(expo, axis=2)
    incoming_token_weight = jnp.where(is_first, jnp.exp(new_score - top_score), 0.0)
    numerator = (
        numerator
        + incoming_token_weight.astype(jnp.bfloat16).astype(jnp.float32)[:, :, None]
        * new_latent.astype(jnp.float32)[:, None, :]
    )
    denominator = denominator + incoming_token_weight
    overall = lax.pmax(top_score, "tp")
    factor = jnp.exp(top_score - overall)
    numer_sum, denom_sum = (
        lax.psum_scatter(numerator * factor[:, :, None], "tp", scatter_dimension=1, tiled=True),
        lax.psum_scatter(denominator * factor, "tp", scatter_dimension=1, tiled=True),
    )
    latent_output_rows = (numer_sum / denom_sum[:, :, None]).astype(jnp.bfloat16)
    value_projected_output = jnp.einsum(
        "wyc,yca->wya", latent_output_rows, value_up_weight, preferred_element_type=jnp.float32
    )
    return value_projected_output.reshape(requests, -1).astype(jnp.bfloat16)


MESH = pl.DeviceIdType.MESH
up, down = 0, 1
depth, width, lanes = 4, 2, 2
chunk_count = 6
score_scale = softmax_scale / math.log(2.0)


def dot_nt(a, b):
    return lax.dot_general(a, b, (((1,), (1,)), ((), ())), preferred_element_type=jnp.float32)


def loop(count, body, unroll=1):
    def step(i, carry):
        body(i)
        return carry

    lax.fori_loop(0, count, step, 0, unroll=unroll)


def plane_kernel(
    sources,
    slot_table,
    lengths,
    latent_hbm,
    rope_hbm,
    q_hbm,
    q_rope_hbm,
    value_hbm,
    new_entry,
    out,
    table_rows,
    table,
    rope_in,
    rope_wide,
    q_rope_in,
    q_rope_wide,
    latent,
    rope_pairs,
    rope,
    queries,
    query_pairs,
    value,
    keys,
    rope_keys,
    full,
    other,
    stats,
    other_stats,
    partials,
    leaving,
    partial_stats,
    got,
    got_stats,
    fresh,
    local_sem,
    table_send,
    table_recv,
    q_send,
    q_recv,
    y_send,
    y_recv,
    share_send,
    share_recv,
    swap_send,
    swap_recv,
    back_send,
    back_recv,
):
    me = lax.axis_index("dp")
    lane = lax.axis_index("tp")
    z, y = me // width, me % width
    slots, run_len, latent_dim = latent_hbm.shape
    requests, heads = q_hbm.shape[0], q_hbm.shape[1]
    batch = requests // lanes
    rope_dim = q_rope_in.shape[1] // heads
    max_blocks = slot_table.shape[1]
    block_len = run_len * lanes
    count = max_blocks * block_len
    own_heads = heads // lanes
    value_dim = value.shape[2]
    chunk = slots // chunk_count
    has_up, has_down = z + 1 < depth, z > 0
    is_edge = (z == 0) | (z == depth - 1)
    mine = pl.ds(lane * batch, batch)

    is_middle = jnp.logical_not(is_edge)
    near_edge = jnp.where(z < depth // 2, 0, depth - 1)
    far_edge = depth - 1 - near_edge
    near_middle = jnp.where(z < depth // 2, 1, depth - 2)
    far_middle = depth - 1 - near_middle

    def rank_at(s):
        inner = jnp.where(s == 1, far_edge, jnp.where(s == 2, far_middle, near_edge))
        outer = jnp.where(s == 1, near_middle, jnp.where(s == 2, far_middle, far_edge))
        return jnp.where(s == 0, z, jnp.where(is_edge, outer, inner))

    def remote(src, dst, send, recv, target):
        return pltpu.make_async_remote_copy(
            src_ref=src, dst_ref=dst, send_sem=send, recv_sem=recv, device_id=target, device_id_type=MESH
        )

    core = {"tp": 1 - lane}
    partner = {"dp": z * width + 1 - y}

    def at_plane(place):
        return {"dp": place * width + y}

    own_slots = pl.ds(y * slots, slots)
    local = [
        pltpu.make_async_copy(q_rope_hbm, q_rope_in, local_sem.at[0]),
        pltpu.make_async_copy(rope_hbm, rope_in, local_sem.at[1]),
        pltpu.make_async_copy(latent_hbm, latent.at[own_slots, lane], local_sem.at[2]),
        pltpu.make_async_copy(q_hbm.at[mine], queries.at[z], local_sem.at[3]),
        pltpu.make_async_copy(value_hbm, value, local_sem.at[4]),
    ]

    barrier = pltpu.get_barrier_semaphore()

    def greet(target):
        pl.semaphore_signal(barrier, inc=1, device_id=target, device_id_type=MESH)

    greet(core)
    greet(partner)
    for t in range(1, depth):
        greet(at_plane((z + t) % depth))
    for copy in local[:3]:
        copy.start()
    pl.semaphore_wait(barrier, depth + 1)

    def q_copy(rank, c, way):
        target = at_plane(z + 1 if way == up else z - 1)
        return remote(
            queries.at[rank, c], queries.at[rank, c], q_send.at[way, rank, c], q_recv.at[rank, c], target
        )

    def q_rope_copy(rank, way):
        target = at_plane(z + 1 if way == up else z - 1)
        return remote(
            query_pairs.at[rank],
            query_pairs.at[rank],
            q_send.at[way, rank, batch],
            q_recv.at[rank, batch],
            target,
        )

    def ways(rank, body):
        pl.when(has_up & (rank <= z))(lambda: body(up))
        pl.when(has_down & (rank >= z))(lambda: body(down))

    def own_q_copy(c, way):
        target = at_plane(z + 1 if way == up else z - 1)
        return remote(
            q_hbm.at[lane * batch + c], queries.at[z, c], q_send.at[way, z, c], q_recv.at[z, c], target
        )

    def take(rank, c):
        q_copy(rank, c, up).wait_recv()
        ways(rank, lambda way: q_copy(rank, c, way).start())

    def take_rope(rank):
        q_rope_copy(rank, up).wait_recv()
        ways(rank, lambda way: q_rope_copy(rank, way).start())

    def table_copy(t):
        return remote(
            table_rows.at[z], table_rows.at[z], table_send.at[t], table_recv.at[z], at_plane((z + t) % depth)
        )

    def y_copy(c):
        return remote(
            latent_hbm.at[pl.ds(c * chunk, chunk)],
            latent.at[pl.ds(y * slots + c * chunk, chunk), lane],
            y_send.at[c],
            y_recv.at[c],
            partner,
        )

    def y_rope_copy():
        own = rope_pairs.at[own_slots, lane]
        return remote(own, own, y_send.at[chunk_count], y_recv.at[chunk_count], partner)

    def share_copy(side, c):
        rows = pl.ds(side * slots + c * chunk, chunk)
        return remote(
            latent.at[rows, lane],
            latent.at[rows, lane],
            share_send.at[side, c],
            share_recv.at[side, c],
            core,
        )

    def share_rope_copy(side):
        rows = pl.ds(side * slots, slots)
        return remote(
            rope_pairs.at[rows, lane],
            rope_pairs.at[rows, lane],
            share_send.at[side, chunk_count],
            share_recv.at[side, chunk_count],
            core,
        )

    def first(c):
        ways(z, lambda way: own_q_copy(c, way).start())

    first(0)
    y_copy(0).start()
    local[3].start()

    local[1].wait()
    for j in range(run_len // 2):
        rope_wide[:, j : j + 1, :] = (
            rope_in[:, j * 128 : (j + 1) * 128].astype(jnp.float32).reshape(slots, 1, 128)
        )
    rope_pairs[own_slots, lane] = rope_wide[...].astype(jnp.bfloat16)
    y_rope_copy().start()
    loop(chunk_count - 1, lambda c: y_copy(c + 1).start())
    share_rope_copy(y).start()
    local[0].wait()

    def spread(p):
        x = q_rope_in[:, pl.ds(pl.multiple_of(p * 128, 128), 128)].astype(jnp.float32)
        x = jnp.where(lane == 0, x[:batch], x[batch:])
        q_rope_wide[:, pl.ds(p, 1), :] = x.reshape(batch, 1, 128)

    loop(heads // 2, spread, 8)
    query_pairs[z] = q_rope_wide[...].astype(jnp.bfloat16)
    ways(z, lambda way: q_rope_copy(z, way).start())
    loop(batch - 1, lambda c: first(c + 1))
    local[2].wait()
    loop(chunk_count, lambda c: share_copy(y, c).start())
    local[4].start()

    row = lax.broadcasted_iota(jnp.int32, (requests, 128), 0)
    length_rows = jnp.zeros((requests, 128), jnp.int32)
    for r in range(requests):
        length_rows = jnp.where(row == r, lengths[r], length_rows)
    table_rows[z] = length_rows
    table_rows[z, :, 0:max_blocks] = sources[...] * slots + slot_table[...]
    for t in range(1, depth):
        table_copy(t).start()

    extra = new_entry[...].astype(jnp.float32)
    fresh[:, 0:latent_dim] = extra[:, :latent_dim]
    fresh[:, latent_dim : latent_dim + 2 * rope_dim] = jnp.concatenate(
        [extra[:, latent_dim:], extra[:, latent_dim:]], axis=1
    )
    stats[...] = jnp.zeros_like(stats)

    pair_row = lax.broadcasted_iota(jnp.int32, (2 * 64, 64), 0) // 2
    pair_col = lax.broadcasted_iota(jnp.int32, (2 * 64, 64), 1)
    doubler = jnp.where(pair_row == pair_col, 1.0, 0.0).astype(jnp.bfloat16)
    odd = lax.broadcasted_iota(jnp.int32, (128, 128), 0) % 2
    upper = lax.broadcasted_iota(jnp.int32, (128, 128), 1) // rope_dim
    own_part = odd == upper

    def unpaired(pairs):
        twice = jnp.dot(doubler, pairs, preferred_element_type=jnp.float32)
        return jnp.where(own_part, twice, 0.0)

    def expand(side):
        def one(p):
            rows = pl.ds(side * slots + 2 * p, 2)
            alone = unpaired(rope_pairs[rows].reshape(64, 128))
            both = alone + pltpu.roll(alone, rope_dim, 1)
            rope[rows] = both.astype(jnp.bfloat16).reshape(2, lanes, run_len, 128)

        loop(slots // 2, one, 4)

    share_rope_copy(y).wait_recv()
    expand(y)
    beside = jnp.where(is_edge, near_middle, near_edge)

    def early(c):
        take(beside, c)
        pl.when(is_middle)(lambda: take(far_middle, c))

    def pass_block(c):
        y_copy(c).wait_recv()
        share_copy(1 - y, c).start()

    def both(c):
        early(2 * c)
        early(2 * c + 1)
        pass_block(c)

    early(0)
    take_rope(beside)
    pl.when(is_middle)(lambda: take_rope(far_middle))
    early(1)
    pass_block(0)
    y_rope_copy().wait_recv()
    share_rope_copy(1 - y).start()
    both(1)
    share_rope_copy(1 - y).wait_recv()
    expand(1 - y)
    loop(batch // 2 - 2, lambda c: both(c + 2))
    loop(chunk_count - batch // 2, lambda c: pass_block(c + batch // 2))

    for t in range(1, depth):
        table_copy_in = remote(
            table_rows.at[z],
            table_rows.at[(z + t) % depth],
            table_send.at[t],
            table_recv.at[(z + t) % depth],
            at_plane((z + t) % depth),
        )
        table_copy_in.wait_recv()
    into_smem = pltpu.make_async_copy(table_rows, table, local_sem.at[5])
    into_smem.start()
    into_smem.wait()
    local[3].wait()
    local[4].wait()

    loop(chunk_count, lambda c: share_copy(y, c).wait_recv())
    loop(chunk_count, lambda c: share_copy(1 - y, c).wait_recv())

    in_block = lax.broadcasted_iota(jnp.int32, (1, count), 1) % block_len
    left_half = lax.broadcasted_iota(jnp.int32, (1, 128), 1) < block_len
    stat_lane = lax.broadcasted_iota(jnp.int32, (heads, 128), 1)

    def swap(rank, i):
        place = rank * batch + i
        return remote(
            full.at[:, pl.ds(place * heads + (1 - lane) * own_heads, own_heads)],
            other.at[:, pl.ds(place * own_heads, own_heads)],
            swap_send.at[rank, i],
            swap_recv.at[rank, i],
            core,
        )

    def swap_stats(rank):
        return remote(
            stats.at[rank, pl.ds((1 - lane) * own_heads, own_heads)],
            other_stats.at[rank],
            swap_send.at[rank, batch],
            swap_recv.at[rank, batch],
            core,
        )

    def gather(rank, i, side):
        r = lane * batch + i
        length = table[rank, r, max_blocks]
        limits = []
        for j in range(max_blocks):
            block = table[rank, r, j] - z * (width * slots)
            here = (block >= 0) & (block < width * slots)
            block = jnp.where(here, block, 0)
            limits.append(jnp.where(here, length - j * block_len, 0))
            rows = pl.ds(j * block_len, block_len)
            keys[side, rows, :] = latent[block].reshape(block_len, latent_dim)
            rope_keys[side, rows, :] = rope[block].reshape(block_len, 128)
        limit = jnp.concatenate(
            [jnp.where(left_half, limits[2 * v], limits[2 * v + 1]) for v in range(max_blocks // 2)],
            axis=1,
        )
        return jnp.where(in_block < limit, 0.0, neg_fill)

    def attend(rank, i, own):
        sides = range(2)
        fills = [gather(rank, i + side, side) for side in sides]
        q = [queries[rank, i + side] for side in sides]
        q_rot = [unpaired(query_pairs[rank, i + side]) for side in sides]
        scores = [
            dot_nt(q[side], keys[side]) + dot_nt(q_rot[side].astype(jnp.bfloat16), rope_keys[side])
            for side in sides
        ]
        logs = stats[rank]
        for side in sides:
            score = scores[side] * score_scale + fills[side]
            top = jnp.max(score, axis=1, keepdims=True)
            if own:
                new = fresh[pl.ds(lane * batch + i + side, 1), :]
                new_latent = new[:, :latent_dim]
                new_score = jnp.sum(q[side].astype(jnp.float32) * new_latent, axis=1, keepdims=True)
                new_score = new_score + jnp.sum(q_rot[side] * new[:, latent_dim:], axis=1, keepdims=True)
                new_score = new_score * score_scale
                top = jnp.maximum(top, new_score)
            expo = jnp.exp2(score - top)
            den = jnp.sum(expo, axis=1, keepdims=True)
            num = jnp.dot(expo.astype(jnp.bfloat16), keys[side], preferred_element_type=jnp.float32)
            if own:
                weight = jnp.exp2(new_score - top)
                den = den + weight
                num = num + weight.astype(jnp.bfloat16).astype(jnp.float32) * new_latent
            base = pl.multiple_of((rank * batch + i + side) * heads, heads)
            num = num * (1.0 / den)
            for t in range(latent_dim // 128):
                full[t, pl.ds(base, heads), :] = num[:, t * 128 : (t + 1) * 128]
            logs = jnp.where(stat_lane == i + side, top + jnp.log2(den), logs)
        stats[rank] = logs
        for side in sides:
            swap(rank, i + side).start()

    def project(ranks):
        for rank in ranks:
            swap_stats(rank).wait_recv()
            own_stats = stats[rank, pl.ds(pl.multiple_of(lane * own_heads, own_heads), own_heads), :]
            both_stats = jnp.where(
                stat_lane[:own_heads] < batch, own_stats, pltpu.roll(other_stats[rank], batch, 1)
            )
            square = jnp.concatenate([both_stats, both_stats], axis=0)
            partial_stats[rank] = square.T[:requests]
            loop(batch, lambda i: swap(rank, i).wait_recv())

        def one(h):
            tiles = []
            for t in range(latent_dim // 128):
                rows = []
                for rank in ranks:
                    place = rank * batch
                    rows.append(full[t, pl.ds(place * heads + lane * own_heads + h, batch, stride=heads), :])
                    rows.append(other[t, pl.ds(place * own_heads + h, batch, stride=own_heads), :])
                tiles.append(jnp.concatenate(rows, axis=0))
            rows = jnp.concatenate(tiles, axis=1).astype(jnp.bfloat16)
            done = jnp.dot(rows, value[h], preferred_element_type=jnp.float32)
            columns = pl.ds(pl.multiple_of(h * value_dim, value_dim), value_dim)
            for n, rank in enumerate(ranks):
                partials[rank, :, columns] = done[n * requests : (n + 1) * requests]

        loop(own_heads, one, 8)

    def back(rank):
        slot = jnp.where(is_middle & (rank == far_edge), depth, z)
        target = at_plane(jnp.where(is_middle & (rank == far_edge), far_middle, rank))
        return [
            remote(leaving.at[rank], got.at[slot], back_send.at[rank, 0], back_recv.at[slot, 0], target),
            remote(
                partial_stats.at[rank], got_stats.at[slot], back_send.at[rank, 1], back_recv.at[slot, 1], target
            ),
        ]

    def arrive(slot):
        remote(leaving.at[z], got.at[slot], back_send.at[z, 0], back_recv.at[slot, 0], at_plane(beside)).wait_recv()
        remote(
            partial_stats.at[z], got_stats.at[slot], back_send.at[z, 1], back_recv.at[slot, 1], at_plane(beside)
        ).wait_recv()

    def mixture(logs):
        best = functools.reduce(jnp.maximum, logs)
        weights = [jnp.exp2(log - best) for log in logs]
        total = functools.reduce(jnp.add, weights)
        return [weight / total for weight in weights], best + jnp.log2(total)

    def mix(rank, slots_in, put):
        logs = [partial_stats[rank]] + [got_stats[slot] for slot in slots_in]
        weights, log = mixture(logs)
        for h in range(own_heads):
            columns = pl.ds(h * value_dim, value_dim)
            parts = [partials[rank, :, columns]] + [got[slot, :, columns] for slot in slots_in]
            put(
                columns,
                sum(weight[:, h : h + 1] * part.astype(jnp.float32) for weight, part in zip(weights, parts)),
            )
        return log

    def finish(rank):
        via = is_middle & (rank == near_edge)

        @pl.when(via)
        def _():
            arrive(depth)

            def put(columns, values):
                leaving[rank, :, columns] = values.astype(jnp.bfloat16)

            partial_stats[rank] = mix(rank, [depth], put)

        @pl.when(jnp.logical_not(via))
        def _():
            def pack(h):
                columns = pl.ds(pl.multiple_of(h * value_dim, value_dim), value_dim)
                leaving[rank, :, columns] = partials[rank, :, columns].astype(jnp.bfloat16)

            loop(own_heads, pack, 8)

        for copy in back(rank):
            copy.start()

    def own_one(p):
        for side in range(2):
            pl.when(is_middle)(lambda: take(far_edge, 2 * p + side))
        pl.when(is_middle & (p == 0))(lambda: take_rope(far_edge))
        attend(z, 2 * p, True)

    loop(batch // 2, own_one)
    swap_stats(z).start()

    def visit(s):
        rank = rank_at(s)

        def one(p):
            for side in range(2):
                pl.when(is_edge & (s >= 2))(lambda: take(rank, 2 * p + side))
            pl.when(is_edge & (s >= 2) & (p == 0))(lambda: take_rope(rank))
            attend(rank, 2 * p, False)

        loop(batch // 2, one)
        swap_stats(rank).start()

        @pl.when(s == 2)
        def _():
            project([rank_at(1), rank_at(2)])
            finish(rank_at(1))
            finish(rank_at(2))

    loop(depth - 1, lambda s: visit(s + 1))
    project([z, rank_at(3)])
    finish(rank_at(3))

    def put_out(columns, values):
        turned = pltpu.roll(values, batch, 0)
        out[:, columns] = jnp.where(lane == 0, values, turned).astype(out.dtype)

    @pl.when(is_edge)
    def _():
        arrive(near_middle)
        arrive(far_edge)
        mix(z, [near_middle, far_edge], put_out)

    @pl.when(is_middle)
    def _():
        places = [near_edge, far_middle, far_edge]
        for place in places:
            arrive(place)
        mix(z, places, put_out)

    for t in range(1, depth):
        table_copy(t).wait_send()
    y_rope_copy().wait_send()
    loop(chunk_count, lambda c: y_copy(c).wait_send())
    for side in range(width):
        share_rope_copy(side).wait_send()
        loop(chunk_count, lambda c: share_copy(side, c).wait_send())

    def sent(rank):
        ways(rank, lambda way: q_rope_copy(rank, way).wait_send())
        loop(batch, lambda c: ways(rank, lambda way: q_copy(rank, c, way).wait_send()))
        loop(batch, lambda i: swap(rank, i).wait_send())
        swap_stats(rank).wait_send()

        @pl.when(rank != z)
        def _():
            for copy in back(rank):
                copy.wait_send()

    loop(depth, sent)


def plane_local(
    q_latent,
    q_rope,
    new_entry,
    cache_latent,
    cache_rope,
    source_rank,
    slot_index,
    lengths,
    value_up_weight,
):
    requests, max_blocks = slot_index.shape
    slots, run_len, latent_dim = cache_latent.shape
    heads = q_latent.shape[1]
    own_heads, _, value_dim = value_up_weight.shape
    batch = requests // lanes
    count = max_blocks * run_len * lanes
    bf16, f32 = jnp.bfloat16, jnp.float32
    vmem = pl.BlockSpec(memory_space=pltpu.VMEM)
    smem = pl.BlockSpec(memory_space=pltpu.SMEM)
    anywhere = pl.BlockSpec(memory_space=pl.ANY)
    dma = pltpu.SemaphoreType.DMA
    return pl.pallas_call(
        plane_kernel,
        out_shape=jax.ShapeDtypeStruct((requests, own_heads * value_dim), bf16),
        in_specs=[vmem, vmem, smem] + [anywhere] * 5 + [vmem],
        out_specs=vmem,
        scratch_shapes=[
            pltpu.VMEM((depth, requests, 128), jnp.int32),
            pltpu.SMEM((depth, requests, 128), jnp.int32),
            pltpu.VMEM(cache_rope.shape, bf16),
            pltpu.VMEM((slots, run_len // 2, 128), f32),
            pltpu.VMEM(q_rope.shape, bf16),
            pltpu.VMEM((batch, heads // 2, 128), f32),
            pltpu.VMEM((width * slots, lanes, run_len, latent_dim), bf16),
            pltpu.VMEM((width * slots, lanes, run_len // 2, 128), bf16),
            pltpu.VMEM((width * slots, lanes, run_len, 128), bf16),
            pltpu.VMEM((depth, batch, heads, latent_dim), bf16),
            pltpu.VMEM((depth, batch, heads // 2, 128), bf16),
            pltpu.VMEM(value_up_weight.shape, bf16),
            pltpu.VMEM((2, count, latent_dim), bf16),
            pltpu.VMEM((2, count, 128), bf16),
            pltpu.VMEM((latent_dim // 128, depth * batch * heads, 128), f32),
            pltpu.VMEM((latent_dim // 128, depth * batch * own_heads, 128), f32),
            pltpu.VMEM((depth, heads, 128), f32),
            pltpu.VMEM((depth, own_heads, 128), f32),
            pltpu.VMEM((depth, requests, own_heads * value_dim), f32),
            pltpu.VMEM((depth, requests, own_heads * value_dim), bf16),
            pltpu.VMEM((depth, requests, 128), f32),
            pltpu.VMEM((depth + 1, requests, own_heads * value_dim), bf16),
            pltpu.VMEM((depth + 1, requests, 128), f32),
            pltpu.VMEM((requests, latent_dim + 128), f32),
            dma((6,)),
            dma((depth,)),
            dma((depth,)),
            dma((2, depth, batch + 1)),
            dma((depth, batch + 1)),
            dma((chunk_count + 1,)),
            dma((chunk_count + 1,)),
            dma((width, chunk_count + 1)),
            dma((width, chunk_count + 1)),
            dma((depth, batch + 1)),
            dma((depth, batch + 1)),
            dma((depth, 2)),
            dma((depth + 1, 2)),
        ],
        compiler_params=pltpu.CompilerParams(
            collective_id=0, has_side_effects=True, vmem_limit_bytes=60 * 1024 * 1024
        ),
    )(
        source_rank.reshape(requests, max_blocks),
        slot_index,
        lengths,
        cache_latent,
        cache_rope,
        q_latent,
        q_rope,
        value_up_weight,
        new_entry,
    )


def local(*args):
    q_latent, cache_latent, slot_index = args[0], args[3], args[6]
    fits = lax.axis_size("dp") == depth * width and lax.axis_size("tp") == lanes
    fits = fits and q_latent.shape == (16, 128, 512) and args[1].shape == (16, 8192)
    fits = fits and cache_latent.shape == (48, 32, 512) and slot_index.shape == (16, 16)
    return (plane_local if fits else spread_local)(*args)


def solution(mesh):
    placed = (
        P(("pop", "dp"), None, None),
        P(("pop", "dp"), None),
        P(("pop", "dp"), None),
        P(("pop", "dp"), "tp", None),
        P(("pop", "dp"), "tp"),
        P(("pop", "dp"), None, None),
        P(("pop", "dp"), None),
        P(("pop", "dp")),
        P("tp", None, None),
    )
    return jax.shard_map(
        local, mesh=mesh, in_specs=placed, out_specs=P(("pop", "dp"), "tp"), check_vma=False
    )
```

```python
import functools
import math

import jax
import jax.numpy as jnp
from jax import lax
from jax.experimental import pallas as pl
from jax.experimental.pallas import tpu as pltpu
from jax.sharding import PartitionSpec as P

softmax_scale = 192.0 ** (-0.5)
neg_fill = -1e30


def entry_places(src_flat):
    count = src_flat.shape[0]
    spot = jnp.arange(count, dtype=jnp.int32)
    same = (src_flat[:, None] == src_flat[None, :]) & (spot[None, :] < spot[:, None])
    return jnp.sum(same.astype(jnp.int32), axis=1)


def pick(rows, index):
    onehot = (index[:, None] == jnp.arange(rows.shape[0], dtype=jnp.int32)[None, :]).astype(rows.dtype)
    flat = jnp.dot(onehot, rows.reshape(rows.shape[0], -1), preferred_element_type=jnp.float32)
    return flat.astype(rows.dtype).reshape((index.shape[0],) + rows.shape[1:])


def spread_local(
    q_latent,
    q_rope,
    new_entry,
    cache_latent,
    cache_rope,
    source_rank,
    slot_index,
    lengths,
    value_up_weight,
):
    rank_count = lax.axis_size("dp")
    lane_count = lax.axis_size("tp")
    my_lane = lax.axis_index("tp")
    requests, max_blocks = slot_index.shape
    run_len = cache_latent.shape[1]
    latent_dim = cache_latent.shape[2]
    heads = q_latent.shape[1]
    rope_dim = q_rope.shape[1] // heads
    entries = requests * max_blocks
    capacity = max(2, (entries * 5 + 4 * rank_count - 1) // (4 * rank_count))
    src_flat = source_rank.reshape(entries)
    slot_flat = slot_index.reshape(entries)
    places = entry_places(src_flat)
    where_from = src_flat * capacity + places
    cells = jnp.arange(rank_count * capacity, dtype=jnp.int32)
    wanted = jnp.sum(
        jnp.where(cells[:, None] == where_from[None, :], slot_flat[None, :], 0), axis=1
    ).reshape(rank_count, capacity)
    asked_slots = lax.all_to_all(wanted, "dp", split_axis=0, concat_axis=0, tiled=True)
    asked = asked_slots.reshape(rank_count * capacity)
    send_latent = pick(cache_latent, asked).reshape(rank_count, capacity, run_len, latent_dim)
    send_rope = pick(cache_rope, asked).reshape(rank_count, capacity, run_len * rope_dim)
    got_latent, received_rotary_keys = (
        lax.all_to_all(send_latent, "dp", split_axis=0, concat_axis=0, tiled=True),
        lax.all_to_all(send_rope, "dp", split_axis=0, concat_axis=0, tiled=True),
    )
    keys_latent = pick(got_latent.reshape(rank_count * capacity, run_len, latent_dim), where_from)
    keys_latent = keys_latent.reshape(requests, max_blocks * run_len, latent_dim)
    keys_rope = pick(
        received_rotary_keys.reshape(rank_count * capacity, run_len * rope_dim), where_from
    )
    keys_rope = keys_rope.reshape(requests, max_blocks * run_len, rope_dim)
    query_rope = q_rope.reshape(requests, heads, rope_dim)
    scores = jnp.einsum("rhk,rnk->rhn", q_latent, keys_latent, preferred_element_type=jnp.float32)
    scores = (
        scores
        + jnp.einsum("rhd,rnd->rhn", query_rope, keys_rope, preferred_element_type=jnp.float32)
    ) * softmax_scale
    new_latent = new_entry[:, :latent_dim]
    incoming_rotary_key = new_entry[:, latent_dim:]
    new_score = jnp.einsum("rhk,rk->rh", q_latent, new_latent, preferred_element_type=jnp.float32)
    new_score = (
        new_score
        + jnp.einsum(
            "rhd,rd->rh", query_rope, incoming_rotary_key, preferred_element_type=jnp.float32
        )
    ) * softmax_scale
    slot_pos = jnp.arange(max_blocks * run_len, dtype=jnp.int32)
    positions = (
        slot_pos // run_len * (run_len * lane_count) + my_lane * run_len + slot_pos % run_len
    )
    in_range = (positions[None, :] < lengths[:, None])[:, None, :]
    is_first = my_lane == 0
    top_score = jnp.max(jnp.where(in_range, scores, neg_fill), axis=2)
    top_score = jnp.where(is_first, jnp.maximum(top_score, new_score), top_score)
    expo = jnp.where(in_range, jnp.exp(scores - top_score[:, :, None]), 0.0)
    numerator = jnp.einsum(
        "rhn,rnk->rhk", expo.astype(jnp.bfloat16), keys_latent, preferred_element_type=jnp.float32
    )
    denominator = jnp.sum(expo, axis=2)
    incoming_token_weight = jnp.where(is_first, jnp.exp(new_score - top_score), 0.0)
    numerator = (
        numerator
        + incoming_token_weight.astype(jnp.bfloat16).astype(jnp.float32)[:, :, None]
        * new_latent.astype(jnp.float32)[:, None, :]
    )
    denominator = denominator + incoming_token_weight
    overall = lax.pmax(top_score, "tp")
    factor = jnp.exp(top_score - overall)
    numer_sum, denom_sum = (
        lax.psum_scatter(numerator * factor[:, :, None], "tp", scatter_dimension=1, tiled=True),
        lax.psum_scatter(denominator * factor, "tp", scatter_dimension=1, tiled=True),
    )
    latent_output_rows = (numer_sum / denom_sum[:, :, None]).astype(jnp.bfloat16)
    value_projected_output = jnp.einsum(
        "wyc,yca->wya", latent_output_rows, value_up_weight, preferred_element_type=jnp.float32
    )
    return value_projected_output.reshape(requests, -1).astype(jnp.bfloat16)


MESH = pl.DeviceIdType.MESH
up, down = 0, 1
depth, width, lanes = 4, 2, 2
chunk_count = 6
score_scale = softmax_scale / math.log(2.0)


def dot_nt(a, b):
    return lax.dot_general(a, b, (((1,), (1,)), ((), ())), preferred_element_type=jnp.float32)


def loop(count, body, unroll=1):
    def step(i, carry):
        body(i)
        return carry

    lax.fori_loop(0, count, step, 0, unroll=unroll)


def plane_kernel(
    sources,
    slot_table,
    lengths,
    latent_hbm,
    rope_hbm,
    q_hbm,
    q_rope_hbm,
    value_hbm,
    new_entry,
    out,
    table_rows,
    table,
    rope_in,
    rope_wide,
    q_rope_in,
    q_rope_wide,
    latent,
    rope_pairs,
    rope,
    queries,
    query_pairs,
    value,
    keys,
    rope_keys,
    full,
    other,
    stats,
    other_stats,
    partials,
    leaving,
    partial_stats,
    got,
    got_stats,
    half_leaving,
    half_stats,
    half_got,
    half_got_stats,
    fresh,
    local_sem,
    table_send,
    table_recv,
    q_send,
    q_recv,
    y_send,
    y_recv,
    share_send,
    share_recv,
    swap_send,
    swap_recv,
    back_send,
    back_recv,
    half_send,
    half_recv,
):
    me = lax.axis_index("dp")
    lane = lax.axis_index("tp")
    z, y = me // width, me % width
    slots, run_len, latent_dim = latent_hbm.shape
    requests, heads = q_hbm.shape[0], q_hbm.shape[1]
    batch = requests // lanes
    quarter = batch // 2
    rope_dim = q_rope_in.shape[1] // heads
    max_blocks = slot_table.shape[1]
    block_len = run_len * lanes
    count = max_blocks * block_len
    own_heads = heads // lanes
    value_dim = value.shape[2]
    chunk = slots // chunk_count
    has_up, has_down = z + 1 < depth, z > 0
    is_edge = (z == 0) | (z == depth - 1)
    mine = pl.ds(lane * batch, batch)

    is_middle = jnp.logical_not(is_edge)
    near_edge = jnp.where(z < depth // 2, 0, depth - 1)
    far_edge = depth - 1 - near_edge
    near_middle = jnp.where(z < depth // 2, 1, depth - 2)
    far_middle = depth - 1 - near_middle

    def rank_at(s):
        inner = jnp.where(s == 1, far_edge, jnp.where(s == 2, far_middle, near_edge))
        outer = jnp.where(s == 1, near_middle, jnp.where(s == 2, far_middle, far_edge))
        return jnp.where(s == 0, z, jnp.where(is_edge, outer, inner))

    def remote(src, dst, send, recv, target):
        return pltpu.make_async_remote_copy(
            src_ref=src, dst_ref=dst, send_sem=send, recv_sem=recv, device_id=target, device_id_type=MESH
        )

    core = {"tp": 1 - lane}
    partner = {"dp": z * width + 1 - y}

    def at_plane(place):
        return {"dp": place * width + y}

    own_slots = pl.ds(y * slots, slots)
    local = [
        pltpu.make_async_copy(q_rope_hbm, q_rope_in, local_sem.at[0]),
        pltpu.make_async_copy(rope_hbm, rope_in, local_sem.at[1]),
        pltpu.make_async_copy(latent_hbm, latent.at[own_slots, lane], local_sem.at[2]),
        pltpu.make_async_copy(q_hbm.at[mine], queries.at[z], local_sem.at[3]),
        pltpu.make_async_copy(value_hbm, value, local_sem.at[4]),
    ]

    barrier = pltpu.get_barrier_semaphore()

    def greet(target):
        pl.semaphore_signal(barrier, inc=1, device_id=target, device_id_type=MESH)

    greet(core)
    greet(partner)
    for t in range(1, depth):
        greet(at_plane((z + t) % depth))
    for copy in local[:3]:
        copy.start()
    pl.semaphore_wait(barrier, depth + 1)

    def q_copy(rank, c, way):
        target = at_plane(z + 1 if way == up else z - 1)
        return remote(
            queries.at[rank, c], queries.at[rank, c], q_send.at[way, rank, c], q_recv.at[rank, c], target
        )

    def q_rope_copy(rank, way):
        target = at_plane(z + 1 if way == up else z - 1)
        return remote(
            query_pairs.at[rank],
            query_pairs.at[rank],
            q_send.at[way, rank, batch],
            q_recv.at[rank, batch],
            target,
        )

    def ways(rank, body):
        pl.when(has_up & (rank <= z))(lambda: body(up))
        pl.when(has_down & (rank >= z))(lambda: body(down))

    def own_q_copy(c, way):
        target = at_plane(z + 1 if way == up else z - 1)
        return remote(
            q_hbm.at[lane * batch + c], queries.at[z, c], q_send.at[way, z, c], q_recv.at[z, c], target
        )

    def take(rank, c):
        q_copy(rank, c, up).wait_recv()
        ways(rank, lambda way: q_copy(rank, c, way).start())

    def take_rope(rank):
        q_rope_copy(rank, up).wait_recv()
        ways(rank, lambda way: q_rope_copy(rank, way).start())

    def table_copy(t):
        return remote(
            table_rows.at[z], table_rows.at[z], table_send.at[t], table_recv.at[z], at_plane((z + t) % depth)
        )

    def y_copy(c):
        return remote(
            latent_hbm.at[pl.ds(c * chunk, chunk)],
            latent.at[pl.ds(y * slots + c * chunk, chunk), lane],
            y_send.at[c],
            y_recv.at[c],
            partner,
        )

    def y_rope_copy():
        own = rope_pairs.at[own_slots, lane]
        return remote(own, own, y_send.at[chunk_count], y_recv.at[chunk_count], partner)

    def share_copy(side, c):
        rows = pl.ds(side * slots + c * chunk, chunk)
        return remote(
            latent.at[rows, lane],
            latent.at[rows, lane],
            share_send.at[side, c],
            share_recv.at[side, c],
            core,
        )

    def share_rope_copy(side):
        rows = pl.ds(side * slots, slots)
        return remote(
            rope_pairs.at[rows, lane],
            rope_pairs.at[rows, lane],
            share_send.at[side, chunk_count],
            share_recv.at[side, chunk_count],
            core,
        )

    def first(c):
        ways(z, lambda way: own_q_copy(c, way).start())

    first(0)
    y_copy(0).start()
    local[3].start()

    local[1].wait()
    for j in range(run_len // 2):
        rope_wide[:, j : j + 1, :] = (
            rope_in[:, j * 128 : (j + 1) * 128].astype(jnp.float32).reshape(slots, 1, 128)
        )
    rope_pairs[own_slots, lane] = rope_wide[...].astype(jnp.bfloat16)
    y_rope_copy().start()
    loop(chunk_count - 1, lambda c: y_copy(c + 1).start())
    share_rope_copy(y).start()
    local[0].wait()

    def spread(p):
        x = q_rope_in[:, pl.ds(pl.multiple_of(p * 128, 128), 128)].astype(jnp.float32)
        x = jnp.where(lane == 0, x[:batch], x[batch:])
        q_rope_wide[:, pl.ds(p, 1), :] = x.reshape(batch, 1, 128)

    loop(heads // 2, spread, 8)
    query_pairs[z] = q_rope_wide[...].astype(jnp.bfloat16)
    ways(z, lambda way: q_rope_copy(z, way).start())
    loop(batch - 1, lambda c: first(c + 1))
    local[2].wait()
    loop(chunk_count, lambda c: share_copy(y, c).start())
    local[4].start()

    row = lax.broadcasted_iota(jnp.int32, (requests, 128), 0)
    length_rows = jnp.zeros((requests, 128), jnp.int32)
    for r in range(requests):
        length_rows = jnp.where(row == r, lengths[r], length_rows)
    table_rows[z] = length_rows
    table_rows[z, :, 0:max_blocks] = sources[...] * slots + slot_table[...]
    for t in range(1, depth):
        table_copy(t).start()

    extra = new_entry[...].astype(jnp.float32)
    fresh[:, 0:latent_dim] = extra[:, :latent_dim]
    fresh[:, latent_dim : latent_dim + 2 * rope_dim] = jnp.concatenate(
        [extra[:, latent_dim:], extra[:, latent_dim:]], axis=1
    )
    stats[...] = jnp.zeros_like(stats)

    pair_row = lax.broadcasted_iota(jnp.int32, (2 * 64, 64), 0) // 2
    pair_col = lax.broadcasted_iota(jnp.int32, (2 * 64, 64), 1)
    doubler = jnp.where(pair_row == pair_col, 1.0, 0.0).astype(jnp.bfloat16)
    odd = lax.broadcasted_iota(jnp.int32, (128, 128), 0) % 2
    upper = lax.broadcasted_iota(jnp.int32, (128, 128), 1) // rope_dim
    own_part = odd == upper

    def unpaired(pairs):
        twice = jnp.dot(doubler, pairs, preferred_element_type=jnp.float32)
        return jnp.where(own_part, twice, 0.0)

    def expand(side):
        def one(p):
            rows = pl.ds(side * slots + 2 * p, 2)
            alone = unpaired(rope_pairs[rows].reshape(64, 128))
            both = alone + pltpu.roll(alone, rope_dim, 1)
            rope[rows] = both.astype(jnp.bfloat16).reshape(2, lanes, run_len, 128)

        loop(slots // 2, one, 4)

    share_rope_copy(y).wait_recv()
    expand(y)
    beside = jnp.where(is_edge, near_middle, near_edge)

    def early(c):
        take(beside, c)
        pl.when(is_middle)(lambda: take(far_middle, c))

    def pass_block(c):
        y_copy(c).wait_recv()
        share_copy(1 - y, c).start()

    def both(c):
        early(2 * c)
        early(2 * c + 1)
        pass_block(c)

    early(0)
    take_rope(beside)
    pl.when(is_middle)(lambda: take_rope(far_middle))
    early(1)
    pass_block(0)
    y_rope_copy().wait_recv()
    share_rope_copy(1 - y).start()
    both(1)
    share_rope_copy(1 - y).wait_recv()
    expand(1 - y)
    loop(batch // 2 - 2, lambda c: both(c + 2))
    loop(chunk_count - batch // 2, lambda c: pass_block(c + batch // 2))

    for t in range(1, depth):
        table_copy_in = remote(
            table_rows.at[z],
            table_rows.at[(z + t) % depth],
            table_send.at[t],
            table_recv.at[(z + t) % depth],
            at_plane((z + t) % depth),
        )
        table_copy_in.wait_recv()
    into_smem = pltpu.make_async_copy(table_rows, table, local_sem.at[5])
    into_smem.start()
    into_smem.wait()
    local[3].wait()
    local[4].wait()

    loop(chunk_count, lambda c: share_copy(y, c).wait_recv())
    loop(chunk_count, lambda c: share_copy(1 - y, c).wait_recv())

    in_block = lax.broadcasted_iota(jnp.int32, (1, count), 1) % block_len
    left_half = lax.broadcasted_iota(jnp.int32, (1, 128), 1) < block_len
    stat_lane = lax.broadcasted_iota(jnp.int32, (heads, 128), 1)

    def swap(rank, i):
        place = rank * batch + i
        return remote(
            full.at[:, pl.ds(place * heads + (1 - lane) * own_heads, own_heads)],
            other.at[:, pl.ds(place * own_heads, own_heads)],
            swap_send.at[rank, i],
            swap_recv.at[rank, i],
            core,
        )

    def swap_stats(slot):
        return remote(
            stats.at[slot, pl.ds((1 - lane) * own_heads, own_heads)],
            other_stats.at[slot],
            swap_send.at[slot, batch],
            swap_recv.at[slot, batch],
            core,
        )

    def gather(rank, i, side):
        r = lane * batch + i
        length = table[rank, r, max_blocks]
        limits = []
        for j in range(max_blocks):
            block = table[rank, r, j] - z * (width * slots)
            here = (block >= 0) & (block < width * slots)
            block = jnp.where(here, block, 0)
            limits.append(jnp.where(here, length - j * block_len, 0))
            rows = pl.ds(j * block_len, block_len)
            keys[side, rows, :] = latent[block].reshape(block_len, latent_dim)
            rope_keys[side, rows, :] = rope[block].reshape(block_len, 128)
        limit = jnp.concatenate(
            [jnp.where(left_half, limits[2 * v], limits[2 * v + 1]) for v in range(max_blocks // 2)],
            axis=1,
        )
        return jnp.where(in_block < limit, 0.0, neg_fill)

    def attend(rank, i, own, slot):
        sides = range(2)
        fills = [gather(rank, i + side, side) for side in sides]
        q = [queries[rank, i + side] for side in sides]
        q_rot = [unpaired(query_pairs[rank, i + side]) for side in sides]
        scores = [
            dot_nt(q[side], keys[side]) + dot_nt(q_rot[side].astype(jnp.bfloat16), rope_keys[side])
            for side in sides
        ]
        logs = stats[slot]
        for side in sides:
            score = scores[side] * score_scale + fills[side]
            top = jnp.max(score, axis=1, keepdims=True)
            if own:
                new = fresh[pl.ds(lane * batch + i + side, 1), :]
                new_latent = new[:, :latent_dim]
                new_score = jnp.sum(q[side].astype(jnp.float32) * new_latent, axis=1, keepdims=True)
                new_score = new_score + jnp.sum(q_rot[side] * new[:, latent_dim:], axis=1, keepdims=True)
                new_score = new_score * score_scale
                top = jnp.maximum(top, new_score)
            expo = jnp.exp2(score - top)
            den = jnp.sum(expo, axis=1, keepdims=True)
            num = jnp.dot(expo.astype(jnp.bfloat16), keys[side], preferred_element_type=jnp.float32)
            if own:
                weight = jnp.exp2(new_score - top)
                den = den + weight
                num = num + weight.astype(jnp.bfloat16).astype(jnp.float32) * new_latent
            base = pl.multiple_of((rank * batch + i + side) * heads, heads)
            num = num * (1.0 / den)
            for t in range(latent_dim // 128):
                full[t, pl.ds(base, heads), :] = num[:, t * 128 : (t + 1) * 128]
            spot = (i + side) // quarter * batch + (i + side) % quarter
            logs = jnp.where(stat_lane == spot, top + jnp.log2(den), logs)
        stats[slot] = logs
        for side in sides:
            swap(rank, i + side).start()

    def rows_of(rank, h, part):
        tiles = []
        for t in range(latent_dim // 128):
            place = rank * batch + part * quarter
            own_rows = full[t, pl.ds(place * heads + lane * own_heads + h, quarter, stride=heads), :]
            other_rows = other[t, pl.ds(place * own_heads + h, quarter, stride=own_heads), :]
            tiles.append(jnp.concatenate([own_rows, other_rows], axis=0))
        return jnp.concatenate(tiles, axis=1)

    def gathered_stats(slot):
        swap_stats(slot).wait_recv()
        own_stats = stats[slot, pl.ds(pl.multiple_of(lane * own_heads, own_heads), own_heads), :]
        both_stats = jnp.where(
            stat_lane[:own_heads] % batch < quarter, own_stats, pltpu.roll(other_stats[slot], quarter, 1)
        )
        square = jnp.concatenate([both_stats, both_stats], axis=0)
        return square.T[:requests]

    def project(ranks):
        for rank in ranks:
            partial_stats[rank] = gathered_stats(rank)
            loop(batch, lambda i: swap(rank, i).wait_recv())

        def one(h):
            rows = [rows_of(rank, h, part) for rank in ranks for part in range(2)]
            rows = jnp.concatenate(rows, axis=0).astype(jnp.bfloat16)
            done = jnp.dot(rows, value[h], preferred_element_type=jnp.float32)
            columns = pl.ds(pl.multiple_of(h * value_dim, value_dim), value_dim)
            for n, rank in enumerate(ranks):
                partials[rank, :, columns] = done[n * requests : (n + 1) * requests]

        loop(own_heads, one, 8)

    def project_half(rank, part, slot):
        half_stats[part] = gathered_stats(slot)
        loop(quarter, lambda i: swap(rank, part * quarter + i).wait_recv())

        def one(h):
            done = []
            for head in (h, h + own_heads // 2):
                rows = rows_of(rank, head, part).astype(jnp.bfloat16)
                done.append(jnp.dot(rows, value[head], preferred_element_type=jnp.float32))
            columns = pl.ds(pl.multiple_of(h * value_dim, value_dim), value_dim)
            half_leaving[part, :, columns] = jnp.concatenate(done, axis=0).astype(jnp.bfloat16)

        loop(own_heads // 2, one, 4)

    def half_back(part):
        target = at_plane(far_edge)
        return [
            remote(half_leaving.at[part], half_got.at[part], half_send.at[part, 0], half_recv.at[part, 0], target),
            remote(
                half_stats.at[part], half_got_stats.at[part], half_send.at[part, 1], half_recv.at[part, 1], target
            ),
        ]

    def back(rank):
        slot = jnp.where(is_middle & (rank == far_edge), depth, z)
        target = at_plane(jnp.where(is_middle & (rank == far_edge), far_middle, rank))
        return [
            remote(leaving.at[rank], got.at[slot], back_send.at[rank, 0], back_recv.at[slot, 0], target),
            remote(
                partial_stats.at[rank], got_stats.at[slot], back_send.at[rank, 1], back_recv.at[slot, 1], target
            ),
        ]

    def arrive(slot):
        remote(leaving.at[z], got.at[slot], back_send.at[z, 0], back_recv.at[slot, 0], at_plane(beside)).wait_recv()
        remote(
            partial_stats.at[z], got_stats.at[slot], back_send.at[z, 1], back_recv.at[slot, 1], at_plane(beside)
        ).wait_recv()

    def mixture(logs):
        best = functools.reduce(jnp.maximum, logs)
        weights = [jnp.exp2(log - best) for log in logs]
        total = functools.reduce(jnp.add, weights)
        return [weight / total for weight in weights], best + jnp.log2(total)

    def mix(rank, slots_in, put):
        logs = [partial_stats[rank]] + [got_stats[slot] for slot in slots_in]
        weights, log = mixture(logs)
        for h in range(own_heads):
            columns = pl.ds(h * value_dim, value_dim)
            parts = [partials[rank, :, columns]] + [got[slot, :, columns] for slot in slots_in]
            put(
                columns,
                sum(weight[:, h : h + 1] * part.astype(jnp.float32) for weight, part in zip(weights, parts)),
            )
        return log

    def finish(rank):
        def pack(h):
            columns = pl.ds(pl.multiple_of(h * value_dim, value_dim), value_dim)
            leaving[rank, :, columns] = partials[rank, :, columns].astype(jnp.bfloat16)

        loop(own_heads, pack, 8)
        for copy in back(rank):
            copy.start()

    def own_one(p):
        for side in range(2):
            pl.when(is_middle)(lambda: take(far_edge, 2 * p + side))
        pl.when(is_middle & (p == 0))(lambda: take_rope(far_edge))
        attend(z, 2 * p, True, z)

    loop(batch // 2, own_one)
    swap_stats(z).start()

    def visit(s):
        rank = rank_at(s)

        def one(p):
            for side in range(2):
                pl.when(is_edge & (s == 2))(lambda: take(rank, 2 * p + side))
            pl.when(is_edge & (s == 2) & (p == 0))(lambda: take_rope(rank))
            attend(rank, 2 * p, False, rank)

        loop(batch // 2, one)
        swap_stats(rank).start()

        @pl.when(s == 1)
        def _():
            project([z, rank])

        @pl.when(s == 2)
        def _():
            project([rank])

        finish(rank)

    loop(2, lambda s: visit(s + 1))

    def q_sent(rank):
        ways(rank, lambda way: q_rope_copy(rank, way).wait_send())
        loop(batch, lambda c: ways(rank, lambda way: q_copy(rank, c, way).wait_send()))

    def last(p):
        rank = rank_at(3)
        for side in range(2):
            pl.when(is_edge)(lambda: take(rank, 2 * p + side))
        pl.when(is_edge & (p == 0))(lambda: take_rope(rank))
        later = is_edge & (p >= quarter // 2)
        attend(rank, 2 * p, False, jnp.where(later, depth, rank))

        @pl.when(is_edge & (p % 2 == 1))
        def _():
            part = p // 2
            slot = jnp.where(later, depth, rank)
            swap_stats(slot).start()
            project_half(rank, part, slot)
            for copy in half_back(part):
                copy.start()

    loop(batch // 2, last)

    @pl.when(is_middle)
    def _():
        swap_stats(near_edge).start()
        project([near_edge])
        arrive(depth)

        def put(columns, values):
            leaving[near_edge, :, columns] = values.astype(jnp.bfloat16)

        partial_stats[near_edge] = mix(near_edge, [depth], put)
        q_sent(far_edge)
        for copy in back(near_edge):
            copy.start()

    low = lax.broadcasted_iota(jnp.int32, (batch, value_dim), 0) < quarter

    def put_out(columns, values):
        first_rows, second_rows = values[:batch], values[batch:]
        own_rows = jnp.where(low, first_rows, pltpu.roll(second_rows, quarter, 0))
        other_rows = jnp.where(low, pltpu.roll(first_rows, quarter, 0), second_rows)
        ordered = jnp.where(
            lane == 0,
            jnp.concatenate([own_rows, other_rows], axis=0),
            jnp.concatenate([other_rows, own_rows], axis=0),
        )
        out[:, columns] = ordered.astype(out.dtype)

    @pl.when(is_edge)
    def _():
        arrive(near_middle)
        for part in range(2):
            for copy in half_back(part):
                copy.wait_recv()
        far_log = jnp.concatenate([half_got_stats[0][:batch], half_got_stats[1][batch:]], axis=0)
        logs = [partial_stats[z], got_stats[near_middle], far_log]
        weights, _log = mixture(logs)
        for h in range(own_heads // 2):
            columns = pl.ds(h * value_dim, value_dim)
            halves = [half_got[part, :, columns].astype(jnp.float32) for part in range(2)]
            for n in range(2):
                head = h + n * (own_heads // 2)
                columns = pl.ds(head * value_dim, value_dim)
                far = jnp.concatenate([half[n * batch : (n + 1) * batch] for half in halves], axis=0)
                parts = [partials[z, :, columns], got[near_middle, :, columns].astype(jnp.float32), far]
                put_out(
                    columns,
                    sum(weight[:, head : head + 1] * part for weight, part in zip(weights, parts)),
                )

    @pl.when(is_middle)
    def _():
        places = [near_edge, far_middle, far_edge]
        for place in places:
            arrive(place)
        mix(z, places, put_out)

    for t in range(1, depth):
        table_copy(t).wait_send()
    y_rope_copy().wait_send()
    loop(chunk_count, lambda c: y_copy(c).wait_send())
    for side in range(width):
        share_rope_copy(side).wait_send()
        loop(chunk_count, lambda c: share_copy(side, c).wait_send())

    def sent(rank):
        pl.when(is_edge | (rank != far_edge))(lambda: q_sent(rank))
        loop(batch, lambda i: swap(rank, i).wait_send())
        swap_stats(rank).wait_send()

        @pl.when((rank != z) & (is_middle | (rank != far_edge)))
        def _():
            for copy in back(rank):
                copy.wait_send()

    loop(depth, sent)

    @pl.when(is_edge)
    def _():
        swap_stats(depth).wait_send()
        for part in range(2):
            for copy in half_back(part):
                copy.wait_send()


def plane_local(
    q_latent,
    q_rope,
    new_entry,
    cache_latent,
    cache_rope,
    source_rank,
    slot_index,
    lengths,
    value_up_weight,
):
    requests, max_blocks = slot_index.shape
    slots, run_len, latent_dim = cache_latent.shape
    heads = q_latent.shape[1]
    own_heads, _, value_dim = value_up_weight.shape
    batch = requests // lanes
    count = max_blocks * run_len * lanes
    bf16, f32 = jnp.bfloat16, jnp.float32
    vmem = pl.BlockSpec(memory_space=pltpu.VMEM)
    smem = pl.BlockSpec(memory_space=pltpu.SMEM)
    anywhere = pl.BlockSpec(memory_space=pl.ANY)
    dma = pltpu.SemaphoreType.DMA
    return pl.pallas_call(
        plane_kernel,
        out_shape=jax.ShapeDtypeStruct((requests, own_heads * value_dim), bf16),
        in_specs=[vmem, vmem, smem] + [anywhere] * 5 + [vmem],
        out_specs=vmem,
        scratch_shapes=[
            pltpu.VMEM((depth, requests, 128), jnp.int32),
            pltpu.SMEM((depth, requests, 128), jnp.int32),
            pltpu.VMEM(cache_rope.shape, bf16),
            pltpu.VMEM((slots, run_len // 2, 128), f32),
            pltpu.VMEM(q_rope.shape, bf16),
            pltpu.VMEM((batch, heads // 2, 128), f32),
            pltpu.VMEM((width * slots, lanes, run_len, latent_dim), bf16),
            pltpu.VMEM((width * slots, lanes, run_len // 2, 128), bf16),
            pltpu.VMEM((width * slots, lanes, run_len, 128), bf16),
            pltpu.VMEM((depth, batch, heads, latent_dim), bf16),
            pltpu.VMEM((depth, batch, heads // 2, 128), bf16),
            pltpu.VMEM(value_up_weight.shape, bf16),
            pltpu.VMEM((2, count, latent_dim), bf16),
            pltpu.VMEM((2, count, 128), bf16),
            pltpu.VMEM((latent_dim // 128, depth * batch * heads, 128), f32),
            pltpu.VMEM((latent_dim // 128, depth * batch * own_heads, 128), f32),
            pltpu.VMEM((depth + 1, heads, 128), f32),
            pltpu.VMEM((depth + 1, own_heads, 128), f32),
            pltpu.VMEM((depth, requests, own_heads * value_dim), f32),
            pltpu.VMEM((depth, requests, own_heads * value_dim), bf16),
            pltpu.VMEM((depth, requests, 128), f32),
            pltpu.VMEM((depth + 1, requests, own_heads * value_dim), bf16),
            pltpu.VMEM((depth + 1, requests, 128), f32),
            pltpu.VMEM((2, requests, own_heads // 2 * value_dim), bf16),
            pltpu.VMEM((2, requests, 128), f32),
            pltpu.VMEM((2, requests, own_heads // 2 * value_dim), bf16),
            pltpu.VMEM((2, requests, 128), f32),
            pltpu.VMEM((requests, latent_dim + 128), f32),
            dma((6,)),
            dma((depth,)),
            dma((depth,)),
            dma((2, depth, batch + 1)),
            dma((depth, batch + 1)),
            dma((chunk_count + 1,)),
            dma((chunk_count + 1,)),
            dma((width, chunk_count + 1)),
            dma((width, chunk_count + 1)),
            dma((depth + 1, batch + 1)),
            dma((depth + 1, batch + 1)),
            dma((depth, 2)),
            dma((depth + 1, 2)),
            dma((2, 2)),
            dma((2, 2)),
        ],
        compiler_params=pltpu.CompilerParams(
            collective_id=0, has_side_effects=True, vmem_limit_bytes=60 * 1024 * 1024
        ),
    )(
        source_rank.reshape(requests, max_blocks),
        slot_index,
        lengths,
        cache_latent,
        cache_rope,
        q_latent,
        q_rope,
        value_up_weight,
        new_entry,
    )


def local(*args):
    q_latent, cache_latent, slot_index = args[0], args[3], args[6]
    fits = lax.axis_size("dp") == depth * width and lax.axis_size("tp") == lanes
    fits = fits and q_latent.shape == (16, 128, 512) and args[1].shape == (16, 8192)
    fits = fits and cache_latent.shape == (48, 32, 512) and slot_index.shape == (16, 16)
    return (plane_local if fits else spread_local)(*args)


def solution(mesh):
    placed = (
        P(("pop", "dp"), None, None),
        P(("pop", "dp"), None),
        P(("pop", "dp"), None),
        P(("pop", "dp"), "tp", None),
        P(("pop", "dp"), "tp"),
        P(("pop", "dp"), None, None),
        P(("pop", "dp"), None),
        P(("pop", "dp")),
        P("tp", None, None),
    )
    return jax.shard_map(
        local, mesh=mesh, in_specs=placed, out_specs=P(("pop", "dp"), "tp"), check_vma=False
    )
```

```python
import functools
import math

import jax
import jax.numpy as jnp
from jax import lax
from jax.experimental import pallas as pl
from jax.experimental.pallas import tpu as pltpu
from jax.sharding import PartitionSpec as P

softmax_scale = 192.0 ** (-0.5)
neg_fill = -1e30


def entry_places(src_flat):
    count = src_flat.shape[0]
    spot = jnp.arange(count, dtype=jnp.int32)
    same = (src_flat[:, None] == src_flat[None, :]) & (spot[None, :] < spot[:, None])
    return jnp.sum(same.astype(jnp.int32), axis=1)


def pick(rows, index):
    onehot = (index[:, None] == jnp.arange(rows.shape[0], dtype=jnp.int32)[None, :]).astype(rows.dtype)
    flat = jnp.dot(onehot, rows.reshape(rows.shape[0], -1), preferred_element_type=jnp.float32)
    return flat.astype(rows.dtype).reshape((index.shape[0],) + rows.shape[1:])


def spread_local(
    q_latent,
    q_rope,
    new_entry,
    cache_latent,
    cache_rope,
    source_rank,
    slot_index,
    lengths,
    value_up_weight,
):
    rank_count = lax.axis_size("dp")
    lane_count = lax.axis_size("tp")
    my_lane = lax.axis_index("tp")
    requests, max_blocks = slot_index.shape
    run_len = cache_latent.shape[1]
    latent_dim = cache_latent.shape[2]
    heads = q_latent.shape[1]
    rope_dim = q_rope.shape[1] // heads
    entries = requests * max_blocks
    capacity = max(2, (entries * 5 + 4 * rank_count - 1) // (4 * rank_count))
    src_flat = source_rank.reshape(entries)
    slot_flat = slot_index.reshape(entries)
    places = entry_places(src_flat)
    where_from = src_flat * capacity + places
    cells = jnp.arange(rank_count * capacity, dtype=jnp.int32)
    wanted = jnp.sum(
        jnp.where(cells[:, None] == where_from[None, :], slot_flat[None, :], 0), axis=1
    ).reshape(rank_count, capacity)
    asked_slots = lax.all_to_all(wanted, "dp", split_axis=0, concat_axis=0, tiled=True)
    asked = asked_slots.reshape(rank_count * capacity)
    send_latent = pick(cache_latent, asked).reshape(rank_count, capacity, run_len, latent_dim)
    send_rope = pick(cache_rope, asked).reshape(rank_count, capacity, run_len * rope_dim)
    got_latent, received_rotary_keys = (
        lax.all_to_all(send_latent, "dp", split_axis=0, concat_axis=0, tiled=True),
        lax.all_to_all(send_rope, "dp", split_axis=0, concat_axis=0, tiled=True),
    )
    keys_latent = pick(got_latent.reshape(rank_count * capacity, run_len, latent_dim), where_from)
    keys_latent = keys_latent.reshape(requests, max_blocks * run_len, latent_dim)
    keys_rope = pick(
        received_rotary_keys.reshape(rank_count * capacity, run_len * rope_dim), where_from
    )
    keys_rope = keys_rope.reshape(requests, max_blocks * run_len, rope_dim)
    query_rope = q_rope.reshape(requests, heads, rope_dim)
    scores = jnp.einsum("rhk,rnk->rhn", q_latent, keys_latent, preferred_element_type=jnp.float32)
    scores = (
        scores
        + jnp.einsum("rhd,rnd->rhn", query_rope, keys_rope, preferred_element_type=jnp.float32)
    ) * softmax_scale
    new_latent = new_entry[:, :latent_dim]
    incoming_rotary_key = new_entry[:, latent_dim:]
    new_score = jnp.einsum("rhk,rk->rh", q_latent, new_latent, preferred_element_type=jnp.float32)
    new_score = (
        new_score
        + jnp.einsum(
            "rhd,rd->rh", query_rope, incoming_rotary_key, preferred_element_type=jnp.float32
        )
    ) * softmax_scale
    slot_pos = jnp.arange(max_blocks * run_len, dtype=jnp.int32)
    positions = (
        slot_pos // run_len * (run_len * lane_count) + my_lane * run_len + slot_pos % run_len
    )
    in_range = (positions[None, :] < lengths[:, None])[:, None, :]
    is_first = my_lane == 0
    top_score = jnp.max(jnp.where(in_range, scores, neg_fill), axis=2)
    top_score = jnp.where(is_first, jnp.maximum(top_score, new_score), top_score)
    expo = jnp.where(in_range, jnp.exp(scores - top_score[:, :, None]), 0.0)
    numerator = jnp.einsum(
        "rhn,rnk->rhk", expo.astype(jnp.bfloat16), keys_latent, preferred_element_type=jnp.float32
    )
    denominator = jnp.sum(expo, axis=2)
    incoming_token_weight = jnp.where(is_first, jnp.exp(new_score - top_score), 0.0)
    numerator = (
        numerator
        + incoming_token_weight.astype(jnp.bfloat16).astype(jnp.float32)[:, :, None]
        * new_latent.astype(jnp.float32)[:, None, :]
    )
    denominator = denominator + incoming_token_weight
    overall = lax.pmax(top_score, "tp")
    factor = jnp.exp(top_score - overall)
    numer_sum, denom_sum = (
        lax.psum_scatter(numerator * factor[:, :, None], "tp", scatter_dimension=1, tiled=True),
        lax.psum_scatter(denominator * factor, "tp", scatter_dimension=1, tiled=True),
    )
    latent_output_rows = (numer_sum / denom_sum[:, :, None]).astype(jnp.bfloat16)
    value_projected_output = jnp.einsum(
        "wyc,yca->wya", latent_output_rows, value_up_weight, preferred_element_type=jnp.float32
    )
    return value_projected_output.reshape(requests, -1).astype(jnp.bfloat16)


MESH = pl.DeviceIdType.MESH
up, down = 0, 1
depth, width, lanes = 4, 2, 2
chunk_count = 6
score_scale = softmax_scale / math.log(2.0)


def dot_nt(a, b):
    return lax.dot_general(a, b, (((1,), (1,)), ((), ())), preferred_element_type=jnp.float32)


def loop(count, body, unroll=1):
    def step(i, carry):
        body(i)
        return carry

    lax.fori_loop(0, count, step, 0, unroll=unroll)


def plane_kernel(
    sources,
    slot_table,
    lengths,
    latent_hbm,
    rope_hbm,
    q_hbm,
    q_rope_hbm,
    value_hbm,
    new_entry,
    out,
    table_rows,
    table,
    rope_in,
    rope_wide,
    q_rope_in,
    q_rope_wide,
    latent,
    rope_pairs,
    rope,
    queries,
    query_pairs,
    value,
    keys,
    rope_keys,
    full,
    other,
    stats,
    other_stats,
    partials,
    leaving,
    partial_stats,
    got,
    got_stats,
    half_leaving,
    half_stats,
    half_got,
    half_got_stats,
    fresh,
    local_sem,
    table_send,
    table_recv,
    q_send,
    q_recv,
    y_send,
    y_recv,
    share_send,
    share_recv,
    swap_send,
    swap_recv,
    back_send,
    back_recv,
    half_send,
    half_recv,
):
    me = lax.axis_index("dp")
    lane = lax.axis_index("tp")
    z, y = me // width, me % width
    slots, run_len, latent_dim = latent_hbm.shape
    requests, heads = q_hbm.shape[0], q_hbm.shape[1]
    batch = requests // lanes
    quarter = batch // 2
    rope_dim = q_rope_in.shape[1] // heads
    max_blocks = slot_table.shape[1]
    block_len = run_len * lanes
    count = max_blocks * block_len
    own_heads = heads // lanes
    value_dim = value.shape[2]
    chunk = slots // chunk_count
    has_up, has_down = z + 1 < depth, z > 0
    is_edge = (z == 0) | (z == depth - 1)
    mine = pl.ds(lane * batch, batch)

    is_middle = jnp.logical_not(is_edge)
    near_edge = jnp.where(z < depth // 2, 0, depth - 1)
    far_edge = depth - 1 - near_edge
    near_middle = jnp.where(z < depth // 2, 1, depth - 2)
    far_middle = depth - 1 - near_middle

    def rank_at(s):
        inner = jnp.where(s == 1, far_edge, jnp.where(s == 2, near_edge, far_middle))
        outer = jnp.where(s == 1, near_middle, jnp.where(s == 2, far_middle, far_edge))
        return jnp.where(s == 0, z, jnp.where(is_edge, outer, inner))

    def remote(src, dst, send, recv, target):
        return pltpu.make_async_remote_copy(
            src_ref=src, dst_ref=dst, send_sem=send, recv_sem=recv, device_id=target, device_id_type=MESH
        )

    core = {"tp": 1 - lane}
    partner = {"dp": z * width + 1 - y}

    def at_plane(place):
        return {"dp": place * width + y}

    own_slots = pl.ds(y * slots, slots)
    local = [
        pltpu.make_async_copy(q_rope_hbm, q_rope_in, local_sem.at[0]),
        pltpu.make_async_copy(rope_hbm, rope_in, local_sem.at[1]),
        pltpu.make_async_copy(latent_hbm, latent.at[own_slots, lane], local_sem.at[2]),
        pltpu.make_async_copy(q_hbm.at[mine], queries.at[z], local_sem.at[3]),
        pltpu.make_async_copy(value_hbm, value, local_sem.at[4]),
    ]

    barrier = pltpu.get_barrier_semaphore()

    def greet(target):
        pl.semaphore_signal(barrier, inc=1, device_id=target, device_id_type=MESH)

    greet(core)
    greet(partner)
    for t in range(1, depth):
        greet(at_plane((z + t) % depth))
    for copy in local[:3]:
        copy.start()
    pl.semaphore_wait(barrier, depth + 1)

    def q_copy(rank, c, way):
        target = at_plane(z + 1 if way == up else z - 1)
        return remote(
            queries.at[rank, c], queries.at[rank, c], q_send.at[way, rank, c], q_recv.at[rank, c], target
        )

    def q_rope_copy(rank, way):
        target = at_plane(z + 1 if way == up else z - 1)
        return remote(
            query_pairs.at[rank],
            query_pairs.at[rank],
            q_send.at[way, rank, batch],
            q_recv.at[rank, batch],
            target,
        )

    def ways(rank, body):
        pl.when(has_up & (rank <= z))(lambda: body(up))
        pl.when(has_down & (rank >= z))(lambda: body(down))

    def own_q_copy(c, way):
        target = at_plane(z + 1 if way == up else z - 1)
        return remote(
            q_hbm.at[lane * batch + c], queries.at[z, c], q_send.at[way, z, c], q_recv.at[z, c], target
        )

    def take(rank, c):
        q_copy(rank, c, up).wait_recv()
        ways(rank, lambda way: q_copy(rank, c, way).start())

    def take_rope(rank):
        q_rope_copy(rank, up).wait_recv()
        ways(rank, lambda way: q_rope_copy(rank, way).start())

    def table_copy(t):
        return remote(
            table_rows.at[z], table_rows.at[z], table_send.at[t], table_recv.at[z], at_plane((z + t) % depth)
        )

    def y_copy(c):
        return remote(
            latent_hbm.at[pl.ds(c * chunk, chunk)],
            latent.at[pl.ds(y * slots + c * chunk, chunk), lane],
            y_send.at[c],
            y_recv.at[c],
            partner,
        )

    def y_rope_copy():
        own = rope_pairs.at[own_slots, lane]
        return remote(own, own, y_send.at[chunk_count], y_recv.at[chunk_count], partner)

    def share_copy(side, c):
        rows = pl.ds(side * slots + c * chunk, chunk)
        return remote(
            latent.at[rows, lane],
            latent.at[rows, lane],
            share_send.at[side, c],
            share_recv.at[side, c],
            core,
        )

    def share_rope_copy(side):
        rows = pl.ds(side * slots, slots)
        return remote(
            rope_pairs.at[rows, lane],
            rope_pairs.at[rows, lane],
            share_send.at[side, chunk_count],
            share_recv.at[side, chunk_count],
            core,
        )

    def first(c):
        ways(z, lambda way: own_q_copy(c, way).start())

    first(0)
    y_copy(0).start()
    local[3].start()

    local[1].wait()
    for j in range(run_len // 2):
        rope_wide[:, j : j + 1, :] = (
            rope_in[:, j * 128 : (j + 1) * 128].astype(jnp.float32).reshape(slots, 1, 128)
        )
    rope_pairs[own_slots, lane] = rope_wide[...].astype(jnp.bfloat16)
    y_rope_copy().start()
    loop(chunk_count - 1, lambda c: y_copy(c + 1).start())
    share_rope_copy(y).start()
    local[0].wait()

    def spread(p):
        x = q_rope_in[:, pl.ds(pl.multiple_of(p * 128, 128), 128)].astype(jnp.float32)
        x = jnp.where(lane == 0, x[:batch], x[batch:])
        q_rope_wide[:, pl.ds(p, 1), :] = x.reshape(batch, 1, 128)

    loop(heads // 2, spread, 8)
    query_pairs[z] = q_rope_wide[...].astype(jnp.bfloat16)
    ways(z, lambda way: q_rope_copy(z, way).start())
    loop(batch - 1, lambda c: first(c + 1))
    local[2].wait()
    loop(chunk_count, lambda c: share_copy(y, c).start())
    local[4].start()

    row = lax.broadcasted_iota(jnp.int32, (requests, 128), 0)
    length_rows = jnp.zeros((requests, 128), jnp.int32)
    for r in range(requests):
        length_rows = jnp.where(row == r, lengths[r], length_rows)
    table_rows[z] = length_rows
    table_rows[z, :, 0:max_blocks] = sources[...] * slots + slot_table[...]
    for t in range(1, depth):
        table_copy(t).start()

    extra = new_entry[...].astype(jnp.float32)
    fresh[:, 0:latent_dim] = extra[:, :latent_dim]
    fresh[:, latent_dim : latent_dim + 2 * rope_dim] = jnp.concatenate(
        [extra[:, latent_dim:], extra[:, latent_dim:]], axis=1
    )
    stats[...] = jnp.zeros_like(stats)

    pair_row = lax.broadcasted_iota(jnp.int32, (2 * 64, 64), 0) // 2
    pair_col = lax.broadcasted_iota(jnp.int32, (2 * 64, 64), 1)
    doubler = jnp.where(pair_row == pair_col, 1.0, 0.0).astype(jnp.bfloat16)
    odd = lax.broadcasted_iota(jnp.int32, (128, 128), 0) % 2
    upper = lax.broadcasted_iota(jnp.int32, (128, 128), 1) // rope_dim
    own_part = odd == upper

    def unpaired(pairs):
        twice = jnp.dot(doubler, pairs, preferred_element_type=jnp.float32)
        return jnp.where(own_part, twice, 0.0)

    def expand(side):
        def one(p):
            rows = pl.ds(side * slots + 2 * p, 2)
            alone = unpaired(rope_pairs[rows].reshape(64, 128))
            both = alone + pltpu.roll(alone, rope_dim, 1)
            rope[rows] = both.astype(jnp.bfloat16).reshape(2, lanes, run_len, 128)

        loop(slots // 2, one, 4)

    share_rope_copy(y).wait_recv()
    expand(y)
    beside = jnp.where(is_edge, near_middle, near_edge)

    def early(c):
        take(beside, c)
        pl.when(is_middle)(lambda: take(far_middle, c))

    def pass_block(c):
        y_copy(c).wait_recv()
        share_copy(1 - y, c).start()

    def both(c):
        early(2 * c)
        early(2 * c + 1)
        pass_block(c)

    early(0)
    take_rope(beside)
    pl.when(is_middle)(lambda: take_rope(far_middle))
    early(1)
    pass_block(0)
    y_rope_copy().wait_recv()
    share_rope_copy(1 - y).start()
    both(1)
    share_rope_copy(1 - y).wait_recv()
    expand(1 - y)
    loop(batch // 2 - 2, lambda c: both(c + 2))
    loop(chunk_count - batch // 2, lambda c: pass_block(c + batch // 2))

    for t in range(1, depth):
        table_copy_in = remote(
            table_rows.at[z],
            table_rows.at[(z + t) % depth],
            table_send.at[t],
            table_recv.at[(z + t) % depth],
            at_plane((z + t) % depth),
        )
        table_copy_in.wait_recv()
    into_smem = pltpu.make_async_copy(table_rows, table, local_sem.at[5])
    into_smem.start()
    into_smem.wait()
    local[3].wait()
    local[4].wait()

    loop(chunk_count, lambda c: share_copy(y, c).wait_recv())
    loop(chunk_count, lambda c: share_copy(1 - y, c).wait_recv())

    in_block = lax.broadcasted_iota(jnp.int32, (1, count), 1) % block_len
    left_half = lax.broadcasted_iota(jnp.int32, (1, 128), 1) < block_len
    stat_lane = lax.broadcasted_iota(jnp.int32, (heads, 128), 1)

    def swap(rank, i):
        place = rank * batch + i
        return remote(
            full.at[:, pl.ds(place * heads + (1 - lane) * own_heads, own_heads)],
            other.at[:, pl.ds(place * own_heads, own_heads)],
            swap_send.at[rank, i],
            swap_recv.at[rank, i],
            core,
        )

    def swap_stats(slot):
        return remote(
            stats.at[slot, pl.ds((1 - lane) * own_heads, own_heads)],
            other_stats.at[slot],
            swap_send.at[slot, batch],
            swap_recv.at[slot, batch],
            core,
        )

    def gather(rank, i, side):
        r = lane * batch + i
        length = table[rank, r, max_blocks]
        limits = []
        for j in range(max_blocks):
            block = table[rank, r, j] - z * (width * slots)
            here = (block >= 0) & (block < width * slots)
            block = jnp.where(here, block, 0)
            limits.append(jnp.where(here, length - j * block_len, 0))
            rows = pl.ds(j * block_len, block_len)
            keys[side, rows, :] = latent[block].reshape(block_len, latent_dim)
            rope_keys[side, rows, :] = rope[block].reshape(block_len, 128)
        limit = jnp.concatenate(
            [jnp.where(left_half, limits[2 * v], limits[2 * v + 1]) for v in range(max_blocks // 2)],
            axis=1,
        )
        return jnp.where(in_block < limit, 0.0, neg_fill)

    def attend(rank, i, own, slot):
        sides = range(2)
        fills = [gather(rank, i + side, side) for side in sides]
        q = [queries[rank, i + side] for side in sides]
        q_rot = [unpaired(query_pairs[rank, i + side]) for side in sides]
        scores = [
            dot_nt(q[side], keys[side]) + dot_nt(q_rot[side].astype(jnp.bfloat16), rope_keys[side])
            for side in sides
        ]
        logs = stats[slot]
        for side in sides:
            score = scores[side] * score_scale + fills[side]
            top = jnp.max(score, axis=1, keepdims=True)
            if own:
                new = fresh[pl.ds(lane * batch + i + side, 1), :]
                new_latent = new[:, :latent_dim]
                new_score = jnp.sum(q[side].astype(jnp.float32) * new_latent, axis=1, keepdims=True)
                new_score = new_score + jnp.sum(q_rot[side] * new[:, latent_dim:], axis=1, keepdims=True)
                new_score = new_score * score_scale
                top = jnp.maximum(top, new_score)
            expo = jnp.exp2(score - top)
            den = jnp.sum(expo, axis=1, keepdims=True)
            num = jnp.dot(expo.astype(jnp.bfloat16), keys[side], preferred_element_type=jnp.float32)
            if own:
                weight = jnp.exp2(new_score - top)
                den = den + weight
                num = num + weight.astype(jnp.bfloat16).astype(jnp.float32) * new_latent
            base = pl.multiple_of((rank * batch + i + side) * heads, heads)
            num = num * (1.0 / den)
            for t in range(latent_dim // 128):
                full[t, pl.ds(base, heads), :] = num[:, t * 128 : (t + 1) * 128]
            logs = jnp.where(stat_lane == i + side, top + jnp.log2(den), logs)
        stats[slot] = logs
        for side in sides:
            swap(rank, i + side).start()

    def rows_of(rank, h, first, some):
        tiles = []
        for t in range(latent_dim // 128):
            place = rank * batch + first
            own_rows = full[t, pl.ds(place * heads + lane * own_heads + h, some, stride=heads), :]
            other_rows = other[t, pl.ds(place * own_heads + h, some, stride=own_heads), :]
            tiles.append(jnp.concatenate([own_rows, other_rows], axis=0))
        return jnp.concatenate(tiles, axis=1)

    def gathered_stats(slot):
        swap_stats(slot).wait_recv()
        own_stats = stats[slot, pl.ds(pl.multiple_of(lane * own_heads, own_heads), own_heads), :]
        both_stats = jnp.where(
            stat_lane[:own_heads] < batch, own_stats, pltpu.roll(other_stats[slot], batch, 1)
        )
        square = jnp.concatenate([both_stats, both_stats], axis=0)
        return square.T[:requests]

    def project(ranks):
        for rank in ranks:
            partial_stats[rank] = gathered_stats(rank)
            loop(batch, lambda i: swap(rank, i).wait_recv())

        def one(h):
            rows = [rows_of(rank, h, 0, batch) for rank in ranks]
            rows = jnp.concatenate(rows, axis=0).astype(jnp.bfloat16)
            done = jnp.dot(rows, value[h], preferred_element_type=jnp.float32)
            columns = pl.ds(pl.multiple_of(h * value_dim, value_dim), value_dim)
            for n, rank in enumerate(ranks):
                partials[rank, :, columns] = done[n * requests : (n + 1) * requests]

        loop(own_heads, one, 8)

    def project_half(rank, part, slot):
        half_stats[part] = gathered_stats(slot)
        loop(quarter, lambda i: swap(rank, part * quarter + i).wait_recv())

        def one(h):
            done = []
            for head in (h, h + own_heads // 2):
                rows = rows_of(rank, head, part * quarter, quarter).astype(jnp.bfloat16)
                done.append(jnp.dot(rows, value[head], preferred_element_type=jnp.float32))
            columns = pl.ds(pl.multiple_of(h * value_dim, value_dim), value_dim)
            half_leaving[part, :, columns] = jnp.concatenate(done, axis=0).astype(jnp.bfloat16)

        loop(own_heads // 2, one, 4)

    def half_back(part):
        target = at_plane(far_edge)
        return [
            remote(half_leaving.at[part], half_got.at[part], half_send.at[part, 0], half_recv.at[part, 0], target),
            remote(
                half_stats.at[part], half_got_stats.at[part], half_send.at[part, 1], half_recv.at[part, 1], target
            ),
        ]

    def back(rank):
        target = at_plane(rank)
        return [
            remote(leaving.at[rank], got.at[z], back_send.at[rank, 0], back_recv.at[z, 0], target),
            remote(partial_stats.at[rank], got_stats.at[z], back_send.at[rank, 1], back_recv.at[z, 1], target),
        ]

    def arrive(slot):
        remote(leaving.at[z], got.at[slot], back_send.at[z, 0], back_recv.at[slot, 0], at_plane(beside)).wait_recv()
        remote(
            partial_stats.at[z], got_stats.at[slot], back_send.at[z, 1], back_recv.at[slot, 1], at_plane(beside)
        ).wait_recv()

    def mixture(logs):
        best = functools.reduce(jnp.maximum, logs)
        weights = [jnp.exp2(log - best) for log in logs]
        total = functools.reduce(jnp.add, weights)
        return [weight / total for weight in weights], best + jnp.log2(total)

    def mix(rank, slots_in, put):
        logs = [partial_stats[rank]] + [got_stats[slot] for slot in slots_in]
        weights, log = mixture(logs)
        for h in range(own_heads):
            columns = pl.ds(h * value_dim, value_dim)
            parts = [partials[rank, :, columns]] + [got[slot, :, columns] for slot in slots_in]
            put(
                columns,
                sum(weight[:, h : h + 1] * part.astype(jnp.float32) for weight, part in zip(weights, parts)),
            )
        return log

    def finish(rank):
        def pack(h):
            columns = pl.ds(pl.multiple_of(h * value_dim, value_dim), value_dim)
            leaving[rank, :, columns] = partials[rank, :, columns].astype(jnp.bfloat16)

        loop(own_heads, pack, 8)
        for copy in back(rank):
            copy.start()

    def own_one(p):
        for side in range(2):
            pl.when(is_middle)(lambda: take(far_edge, 2 * p + side))
        pl.when(is_middle & (p == 0))(lambda: take_rope(far_edge))
        attend(z, 2 * p, True, z)

    loop(batch // 2, own_one)
    swap_stats(z).start()

    def visit(s):
        rank = rank_at(s)

        def one(p):
            for side in range(2):
                pl.when(is_edge & (s == 2))(lambda: take(rank, 2 * p + side))
            pl.when(is_edge & (s == 2) & (p == 0))(lambda: take_rope(rank))
            attend(rank, 2 * p, False, rank)

        loop(batch // 2, one)
        swap_stats(rank).start()

        @pl.when(is_edge & (s == 1))
        def _():
            project([z, near_middle])
            finish(near_middle)

    loop(2, lambda s: visit(s + 1))

    @pl.when(is_middle)
    def _():
        project([far_edge, near_edge])
        finish(far_edge)
        finish(near_edge)

    @pl.when(is_edge)
    def _():
        project([far_middle])
        finish(far_middle)

    def q_sent(rank):
        ways(rank, lambda way: q_rope_copy(rank, way).wait_send())
        loop(batch, lambda c: ways(rank, lambda way: q_copy(rank, c, way).wait_send()))

    def last(p):
        rank = rank_at(3)
        for side in range(2):
            pl.when(is_edge)(lambda: take(rank, 2 * p + side))
        pl.when(is_edge & (p == 0))(lambda: take_rope(rank))
        later = is_edge & (p >= quarter // 2)
        attend(rank, 2 * p, False, jnp.where(later, depth, rank))

        @pl.when(is_edge & (p % 2 == 1))
        def _():
            part = p // 2
            slot = jnp.where(later, depth, rank)
            swap_stats(slot).start()
            project_half(rank, part, slot)
            for copy in half_back(part):
                copy.start()

    loop(batch // 2, last)

    @pl.when(is_middle)
    def _():
        swap_stats(far_middle).start()
        project([far_middle, z])
        finish(far_middle)

    def put_out(columns, values):
        turned = pltpu.roll(values, batch, 0)
        out[:, columns] = jnp.where(lane == 0, values, turned).astype(out.dtype)

    low = lax.broadcasted_iota(jnp.int32, (batch, value_dim), 0) < quarter

    @pl.when(is_edge)
    def _():
        arrive(near_middle)
        arrive(far_middle)
        for part in range(2):
            for copy in half_back(part):
                copy.wait_recv()
        early_rows = lax.broadcasted_iota(jnp.int32, (requests, 128), 0) % batch < quarter
        far_log = jnp.where(early_rows, half_got_stats[0], half_got_stats[1])
        logs = [partial_stats[z], got_stats[near_middle], got_stats[far_middle], far_log]
        weights, _log = mixture(logs)
        for h in range(own_heads // 2):
            columns = pl.ds(h * value_dim, value_dim)
            halves = [half_got[part, :, columns].astype(jnp.float32) for part in range(2)]
            for n in range(2):
                head = h + n * (own_heads // 2)
                columns = pl.ds(head * value_dim, value_dim)
                a, b = [half[n * batch : (n + 1) * batch] for half in halves]
                far = jnp.concatenate(
                    [
                        jnp.where(low, a, pltpu.roll(b, quarter, 0)),
                        jnp.where(low, pltpu.roll(a, quarter, 0), b),
                    ],
                    axis=0,
                )
                parts = [partials[z, :, columns]]
                parts += [got[place, :, columns].astype(jnp.float32) for place in (near_middle, far_middle)]
                parts += [far]
                put_out(
                    columns,
                    sum(weight[:, head : head + 1] * part for weight, part in zip(weights, parts)),
                )

    @pl.when(is_middle)
    def _():
        places = [near_edge, far_middle, far_edge]
        for place in places:
            arrive(place)
        mix(z, places, put_out)

    for t in range(1, depth):
        table_copy(t).wait_send()
    y_rope_copy().wait_send()
    loop(chunk_count, lambda c: y_copy(c).wait_send())
    for side in range(width):
        share_rope_copy(side).wait_send()
        loop(chunk_count, lambda c: share_copy(side, c).wait_send())

    def sent(rank):
        q_sent(rank)
        loop(batch, lambda i: swap(rank, i).wait_send())
        swap_stats(rank).wait_send()

        @pl.when((rank != z) & (is_middle | (rank != far_edge)))
        def _():
            for copy in back(rank):
                copy.wait_send()

    loop(depth, sent)

    @pl.when(is_edge)
    def _():
        swap_stats(depth).wait_send()
        for part in range(2):
            for copy in half_back(part):
                copy.wait_send()


def plane_local(
    q_latent,
    q_rope,
    new_entry,
    cache_latent,
    cache_rope,
    source_rank,
    slot_index,
    lengths,
    value_up_weight,
):
    requests, max_blocks = slot_index.shape
    slots, run_len, latent_dim = cache_latent.shape
    heads = q_latent.shape[1]
    own_heads, _, value_dim = value_up_weight.shape
    batch = requests // lanes
    count = max_blocks * run_len * lanes
    bf16, f32 = jnp.bfloat16, jnp.float32
    vmem = pl.BlockSpec(memory_space=pltpu.VMEM)
    smem = pl.BlockSpec(memory_space=pltpu.SMEM)
    anywhere = pl.BlockSpec(memory_space=pl.ANY)
    dma = pltpu.SemaphoreType.DMA
    return pl.pallas_call(
        plane_kernel,
        out_shape=jax.ShapeDtypeStruct((requests, own_heads * value_dim), bf16),
        in_specs=[vmem, vmem, smem] + [anywhere] * 5 + [vmem],
        out_specs=vmem,
        scratch_shapes=[
            pltpu.VMEM((depth, requests, 128), jnp.int32),
            pltpu.SMEM((depth, requests, 128), jnp.int32),
            pltpu.VMEM(cache_rope.shape, bf16),
            pltpu.VMEM((slots, run_len // 2, 128), f32),
            pltpu.VMEM(q_rope.shape, bf16),
            pltpu.VMEM((batch, heads // 2, 128), f32),
            pltpu.VMEM((width * slots, lanes, run_len, latent_dim), bf16),
            pltpu.VMEM((width * slots, lanes, run_len // 2, 128), bf16),
            pltpu.VMEM((width * slots, lanes, run_len, 128), bf16),
            pltpu.VMEM((depth, batch, heads, latent_dim), bf16),
            pltpu.VMEM((depth, batch, heads // 2, 128), bf16),
            pltpu.VMEM(value_up_weight.shape, bf16),
            pltpu.VMEM((2, count, latent_dim), bf16),
            pltpu.VMEM((2, count, 128), bf16),
            pltpu.VMEM((latent_dim // 128, depth * batch * heads, 128), f32),
            pltpu.VMEM((latent_dim // 128, depth * batch * own_heads, 128), f32),
            pltpu.VMEM((depth + 1, heads, 128), f32),
            pltpu.VMEM((depth + 1, own_heads, 128), f32),
            pltpu.VMEM((depth, requests, own_heads * value_dim), f32),
            pltpu.VMEM((depth, requests, own_heads * value_dim), bf16),
            pltpu.VMEM((depth, requests, 128), f32),
            pltpu.VMEM((depth + 1, requests, own_heads * value_dim), bf16),
            pltpu.VMEM((depth + 1, requests, 128), f32),
            pltpu.VMEM((2, requests, own_heads // 2 * value_dim), bf16),
            pltpu.VMEM((2, requests, 128), f32),
            pltpu.VMEM((2, requests, own_heads // 2 * value_dim), bf16),
            pltpu.VMEM((2, requests, 128), f32),
            pltpu.VMEM((requests, latent_dim + 128), f32),
            dma((6,)),
            dma((depth,)),
            dma((depth,)),
            dma((2, depth, batch + 1)),
            dma((depth, batch + 1)),
            dma((chunk_count + 1,)),
            dma((chunk_count + 1,)),
            dma((width, chunk_count + 1)),
            dma((width, chunk_count + 1)),
            dma((depth + 1, batch + 1)),
            dma((depth + 1, batch + 1)),
            dma((depth, 2)),
            dma((depth + 1, 2)),
            dma((2, 2)),
            dma((2, 2)),
        ],
        compiler_params=pltpu.CompilerParams(
            collective_id=0, has_side_effects=True, vmem_limit_bytes=60 * 1024 * 1024
        ),
    )(
        source_rank.reshape(requests, max_blocks),
        slot_index,
        lengths,
        cache_latent,
        cache_rope,
        q_latent,
        q_rope,
        value_up_weight,
        new_entry,
    )


def local(*args):
    q_latent, cache_latent, slot_index = args[0], args[3], args[6]
    fits = lax.axis_size("dp") == depth * width and lax.axis_size("tp") == lanes
    fits = fits and q_latent.shape == (16, 128, 512) and args[1].shape == (16, 8192)
    fits = fits and cache_latent.shape == (48, 32, 512) and slot_index.shape == (16, 16)
    return (plane_local if fits else spread_local)(*args)


def solution(mesh):
    placed = (
        P(("pop", "dp"), None, None),
        P(("pop", "dp"), None),
        P(("pop", "dp"), None),
        P(("pop", "dp"), "tp", None),
        P(("pop", "dp"), "tp"),
        P(("pop", "dp"), None, None),
        P(("pop", "dp"), None),
        P(("pop", "dp")),
        P("tp", None, None),
    )
    return jax.shard_map(
        local, mesh=mesh, in_specs=placed, out_specs=P(("pop", "dp"), "tp"), check_vma=False
    )
```

```python
import functools
import math

import jax
import jax.numpy as jnp
from jax import lax
from jax.experimental import pallas as pl
from jax.experimental.pallas import tpu as pltpu
from jax.sharding import PartitionSpec as P

softmax_scale = 192.0 ** (-0.5)
neg_fill = -1e30


def entry_places(src_flat):
    count = src_flat.shape[0]
    spot = jnp.arange(count, dtype=jnp.int32)
    same = (src_flat[:, None] == src_flat[None, :]) & (spot[None, :] < spot[:, None])
    return jnp.sum(same.astype(jnp.int32), axis=1)


def pick(rows, index):
    onehot = (index[:, None] == jnp.arange(rows.shape[0], dtype=jnp.int32)[None, :]).astype(rows.dtype)
    flat = jnp.dot(onehot, rows.reshape(rows.shape[0], -1), preferred_element_type=jnp.float32)
    return flat.astype(rows.dtype).reshape((index.shape[0],) + rows.shape[1:])


def spread_local(
    q_latent,
    q_rope,
    new_entry,
    cache_latent,
    cache_rope,
    source_rank,
    slot_index,
    lengths,
    value_up_weight,
):
    rank_count = lax.axis_size("dp")
    lane_count = lax.axis_size("tp")
    my_lane = lax.axis_index("tp")
    requests, max_blocks = slot_index.shape
    run_len = cache_latent.shape[1]
    latent_dim = cache_latent.shape[2]
    heads = q_latent.shape[1]
    rope_dim = q_rope.shape[1] // heads
    entries = requests * max_blocks
    capacity = max(2, (entries * 5 + 4 * rank_count - 1) // (4 * rank_count))
    src_flat = source_rank.reshape(entries)
    slot_flat = slot_index.reshape(entries)
    places = entry_places(src_flat)
    where_from = src_flat * capacity + places
    cells = jnp.arange(rank_count * capacity, dtype=jnp.int32)
    wanted = jnp.sum(
        jnp.where(cells[:, None] == where_from[None, :], slot_flat[None, :], 0), axis=1
    ).reshape(rank_count, capacity)
    asked_slots = lax.all_to_all(wanted, "dp", split_axis=0, concat_axis=0, tiled=True)
    asked = asked_slots.reshape(rank_count * capacity)
    send_latent = pick(cache_latent, asked).reshape(rank_count, capacity, run_len, latent_dim)
    send_rope = pick(cache_rope, asked).reshape(rank_count, capacity, run_len * rope_dim)
    got_latent, received_rotary_keys = (
        lax.all_to_all(send_latent, "dp", split_axis=0, concat_axis=0, tiled=True),
        lax.all_to_all(send_rope, "dp", split_axis=0, concat_axis=0, tiled=True),
    )
    keys_latent = pick(got_latent.reshape(rank_count * capacity, run_len, latent_dim), where_from)
    keys_latent = keys_latent.reshape(requests, max_blocks * run_len, latent_dim)
    keys_rope = pick(
        received_rotary_keys.reshape(rank_count * capacity, run_len * rope_dim), where_from
    )
    keys_rope = keys_rope.reshape(requests, max_blocks * run_len, rope_dim)
    query_rope = q_rope.reshape(requests, heads, rope_dim)
    scores = jnp.einsum("rhk,rnk->rhn", q_latent, keys_latent, preferred_element_type=jnp.float32)
    scores = (
        scores
        + jnp.einsum("rhd,rnd->rhn", query_rope, keys_rope, preferred_element_type=jnp.float32)
    ) * softmax_scale
    new_latent = new_entry[:, :latent_dim]
    incoming_rotary_key = new_entry[:, latent_dim:]
    new_score = jnp.einsum("rhk,rk->rh", q_latent, new_latent, preferred_element_type=jnp.float32)
    new_score = (
        new_score
        + jnp.einsum(
            "rhd,rd->rh", query_rope, incoming_rotary_key, preferred_element_type=jnp.float32
        )
    ) * softmax_scale
    slot_pos = jnp.arange(max_blocks * run_len, dtype=jnp.int32)
    positions = (
        slot_pos // run_len * (run_len * lane_count) + my_lane * run_len + slot_pos % run_len
    )
    in_range = (positions[None, :] < lengths[:, None])[:, None, :]
    is_first = my_lane == 0
    top_score = jnp.max(jnp.where(in_range, scores, neg_fill), axis=2)
    top_score = jnp.where(is_first, jnp.maximum(top_score, new_score), top_score)
    expo = jnp.where(in_range, jnp.exp(scores - top_score[:, :, None]), 0.0)
    numerator = jnp.einsum(
        "rhn,rnk->rhk", expo.astype(jnp.bfloat16), keys_latent, preferred_element_type=jnp.float32
    )
    denominator = jnp.sum(expo, axis=2)
    incoming_token_weight = jnp.where(is_first, jnp.exp(new_score - top_score), 0.0)
    numerator = (
        numerator
        + incoming_token_weight.astype(jnp.bfloat16).astype(jnp.float32)[:, :, None]
        * new_latent.astype(jnp.float32)[:, None, :]
    )
    denominator = denominator + incoming_token_weight
    overall = lax.pmax(top_score, "tp")
    factor = jnp.exp(top_score - overall)
    numer_sum, denom_sum = (
        lax.psum_scatter(numerator * factor[:, :, None], "tp", scatter_dimension=1, tiled=True),
        lax.psum_scatter(denominator * factor, "tp", scatter_dimension=1, tiled=True),
    )
    latent_output_rows = (numer_sum / denom_sum[:, :, None]).astype(jnp.bfloat16)
    value_projected_output = jnp.einsum(
        "wyc,yca->wya", latent_output_rows, value_up_weight, preferred_element_type=jnp.float32
    )
    return value_projected_output.reshape(requests, -1).astype(jnp.bfloat16)


MESH = pl.DeviceIdType.MESH
up, down = 0, 1
depth, width, lanes = 4, 2, 2
chunk_count = 6
score_scale = softmax_scale / math.log(2.0)


def dot_nt(a, b):
    return lax.dot_general(a, b, (((1,), (1,)), ((), ())), preferred_element_type=jnp.float32)


def loop(count, body, unroll=1):
    def step(i, carry):
        body(i)
        return carry

    lax.fori_loop(0, count, step, 0, unroll=unroll)


def plane_kernel(
    sources,
    slot_table,
    lengths,
    latent_hbm,
    rope_hbm,
    q_hbm,
    q_rope_hbm,
    value_hbm,
    new_entry,
    out,
    table_rows,
    table,
    rope_in,
    rope_wide,
    q_rope_in,
    q_rope_wide,
    latent,
    rope_pairs,
    rope,
    queries,
    query_pairs,
    value,
    keys,
    rope_keys,
    full,
    other,
    stats,
    other_stats,
    partials,
    leaving,
    partial_stats,
    got,
    got_stats,
    half_leaving,
    half_stats,
    half_got,
    half_got_stats,
    fresh,
    local_sem,
    table_send,
    table_recv,
    q_send,
    q_recv,
    y_send,
    y_recv,
    share_send,
    share_recv,
    swap_send,
    swap_recv,
    back_send,
    back_recv,
    half_send,
    half_recv,
):
    me = lax.axis_index("dp")
    lane = lax.axis_index("tp")
    z, y = me // width, me % width
    slots, run_len, latent_dim = latent_hbm.shape
    requests, heads = q_hbm.shape[0], q_hbm.shape[1]
    batch = requests // lanes
    quarter = batch // 2
    rope_dim = q_rope_in.shape[1] // heads
    max_blocks = slot_table.shape[1]
    block_len = run_len * lanes
    count = max_blocks * block_len
    own_heads = heads // lanes
    value_dim = value.shape[2]
    chunk = slots // chunk_count
    has_up, has_down = z + 1 < depth, z > 0
    is_edge = (z == 0) | (z == depth - 1)
    mine = pl.ds(lane * batch, batch)

    is_middle = jnp.logical_not(is_edge)
    near_edge = jnp.where(z < depth // 2, 0, depth - 1)
    far_edge = depth - 1 - near_edge
    near_middle = jnp.where(z < depth // 2, 1, depth - 2)
    far_middle = depth - 1 - near_middle

    def rank_at(s):
        inner = jnp.where(s == 1, far_edge, jnp.where(s == 2, near_edge, far_middle))
        outer = jnp.where(s == 1, near_middle, jnp.where(s == 2, far_middle, far_edge))
        return jnp.where(s == 0, z, jnp.where(is_edge, outer, inner))

    def remote(src, dst, send, recv, target):
        return pltpu.make_async_remote_copy(
            src_ref=src, dst_ref=dst, send_sem=send, recv_sem=recv, device_id=target, device_id_type=MESH
        )

    core = {"tp": 1 - lane}
    partner = {"dp": z * width + 1 - y}

    def at_plane(place):
        return {"dp": place * width + y}

    own_slots = pl.ds(y * slots, slots)
    local = [
        pltpu.make_async_copy(q_rope_hbm, q_rope_in, local_sem.at[0]),
        pltpu.make_async_copy(rope_hbm, rope_in, local_sem.at[1]),
        pltpu.make_async_copy(latent_hbm, latent.at[own_slots, lane], local_sem.at[2]),
        pltpu.make_async_copy(q_hbm.at[mine], queries.at[z], local_sem.at[3]),
        pltpu.make_async_copy(value_hbm, value, local_sem.at[4]),
    ]

    barrier = pltpu.get_barrier_semaphore()

    def greet(target):
        pl.semaphore_signal(barrier, inc=1, device_id=target, device_id_type=MESH)

    greet(core)
    greet(partner)
    for t in range(1, depth):
        greet(at_plane((z + t) % depth))
    for copy in local[:3]:
        copy.start()
    pl.semaphore_wait(barrier, depth + 1)

    def q_copy(rank, c, way):
        target = at_plane(z + 1 if way == up else z - 1)
        return remote(
            queries.at[rank, c], queries.at[rank, c], q_send.at[way, rank, c], q_recv.at[rank, c], target
        )

    def q_rope_copy(rank, way):
        target = at_plane(z + 1 if way == up else z - 1)
        return remote(
            query_pairs.at[rank],
            query_pairs.at[rank],
            q_send.at[way, rank, batch],
            q_recv.at[rank, batch],
            target,
        )

    def ways(rank, body):
        pl.when(has_up & (rank <= z))(lambda: body(up))
        pl.when(has_down & (rank >= z))(lambda: body(down))

    def own_q_copy(c, way):
        target = at_plane(z + 1 if way == up else z - 1)
        return remote(
            q_hbm.at[lane * batch + c], queries.at[z, c], q_send.at[way, z, c], q_recv.at[z, c], target
        )

    def take(rank, c):
        q_copy(rank, c, up).wait_recv()
        ways(rank, lambda way: q_copy(rank, c, way).start())

    def take_rope(rank):
        q_rope_copy(rank, up).wait_recv()
        ways(rank, lambda way: q_rope_copy(rank, way).start())

    def table_copy(t):
        return remote(
            table_rows.at[z], table_rows.at[z], table_send.at[t], table_recv.at[z], at_plane((z + t) % depth)
        )

    def y_copy(c):
        return remote(
            latent_hbm.at[pl.ds(c * chunk, chunk)],
            latent.at[pl.ds(y * slots + c * chunk, chunk), lane],
            y_send.at[c],
            y_recv.at[c],
            partner,
        )

    def y_rope_copy():
        own = rope_pairs.at[own_slots, lane]
        return remote(own, own, y_send.at[chunk_count], y_recv.at[chunk_count], partner)

    def share_copy(side, c):
        rows = pl.ds(side * slots + c * chunk, chunk)
        return remote(
            latent.at[rows, lane],
            latent.at[rows, lane],
            share_send.at[side, c],
            share_recv.at[side, c],
            core,
        )

    def share_rope_copy(side):
        rows = pl.ds(side * slots, slots)
        return remote(
            rope_pairs.at[rows, lane],
            rope_pairs.at[rows, lane],
            share_send.at[side, chunk_count],
            share_recv.at[side, chunk_count],
            core,
        )

    def first(c):
        ways(z, lambda way: own_q_copy(c, way).start())

    first(0)
    y_copy(0).start()
    local[3].start()

    local[1].wait()
    for j in range(run_len // 2):
        rope_wide[:, j : j + 1, :] = (
            rope_in[:, j * 128 : (j + 1) * 128].astype(jnp.float32).reshape(slots, 1, 128)
        )
    rope_pairs[own_slots, lane] = rope_wide[...].astype(jnp.bfloat16)
    y_rope_copy().start()
    loop(chunk_count - 1, lambda c: y_copy(c + 1).start())
    share_rope_copy(y).start()
    local[0].wait()

    def spread(p):
        x = q_rope_in[:, pl.ds(pl.multiple_of(p * 128, 128), 128)].astype(jnp.float32)
        x = jnp.where(lane == 0, x[:batch], x[batch:])
        q_rope_wide[:, pl.ds(p, 1), :] = x.reshape(batch, 1, 128)

    loop(heads // 2, spread, 8)
    query_pairs[z] = q_rope_wide[...].astype(jnp.bfloat16)
    ways(z, lambda way: q_rope_copy(z, way).start())
    loop(batch - 1, lambda c: first(c + 1))
    local[2].wait()
    loop(chunk_count, lambda c: share_copy(y, c).start())
    local[4].start()

    row = lax.broadcasted_iota(jnp.int32, (requests, 128), 0)
    length_rows = jnp.zeros((requests, 128), jnp.int32)
    for r in range(requests):
        length_rows = jnp.where(row == r, lengths[r], length_rows)
    table_rows[z] = length_rows
    table_rows[z, :, 0:max_blocks] = sources[...] * slots + slot_table[...]
    for t in range(1, depth):
        table_copy(t).start()

    extra = new_entry[...].astype(jnp.float32)
    fresh[:, 0:latent_dim] = extra[:, :latent_dim]
    fresh[:, latent_dim : latent_dim + 2 * rope_dim] = jnp.concatenate(
        [extra[:, latent_dim:], extra[:, latent_dim:]], axis=1
    )
    stats[...] = jnp.zeros_like(stats)

    pair_row = lax.broadcasted_iota(jnp.int32, (2 * 64, 64), 0) // 2
    pair_col = lax.broadcasted_iota(jnp.int32, (2 * 64, 64), 1)
    doubler = jnp.where(pair_row == pair_col, 1.0, 0.0).astype(jnp.bfloat16)
    odd = lax.broadcasted_iota(jnp.int32, (128, 128), 0) % 2
    upper = lax.broadcasted_iota(jnp.int32, (128, 128), 1) // rope_dim
    own_part = odd == upper

    def unpaired(pairs):
        twice = jnp.dot(doubler, pairs, preferred_element_type=jnp.float32)
        return jnp.where(own_part, twice, 0.0)

    def expand(side):
        def one(p):
            rows = pl.ds(side * slots + 2 * p, 2)
            alone = unpaired(rope_pairs[rows].reshape(64, 128))
            both = alone + pltpu.roll(alone, rope_dim, 1)
            rope[rows] = both.astype(jnp.bfloat16).reshape(2, lanes, run_len, 128)

        loop(slots // 2, one, 4)

    share_rope_copy(y).wait_recv()
    expand(y)
    beside = jnp.where(is_edge, near_middle, near_edge)

    def early(c):
        take(beside, c)
        pl.when(is_middle)(lambda: take(far_middle, c))

    def pass_block(c):
        y_copy(c).wait_recv()
        share_copy(1 - y, c).start()

    def both(c):
        early(2 * c)
        early(2 * c + 1)
        pass_block(c)

    early(0)
    take_rope(beside)
    pl.when(is_middle)(lambda: take_rope(far_middle))
    early(1)
    pass_block(0)
    y_rope_copy().wait_recv()
    share_rope_copy(1 - y).start()
    both(1)
    share_rope_copy(1 - y).wait_recv()
    expand(1 - y)
    loop(batch // 2 - 2, lambda c: both(c + 2))
    loop(chunk_count - batch // 2, lambda c: pass_block(c + batch // 2))

    for t in range(1, depth):
        table_copy_in = remote(
            table_rows.at[z],
            table_rows.at[(z + t) % depth],
            table_send.at[t],
            table_recv.at[(z + t) % depth],
            at_plane((z + t) % depth),
        )
        table_copy_in.wait_recv()
    into_smem = pltpu.make_async_copy(table_rows, table, local_sem.at[5])
    into_smem.start()
    into_smem.wait()
    local[3].wait()
    local[4].wait()

    loop(chunk_count, lambda c: share_copy(y, c).wait_recv())
    loop(chunk_count, lambda c: share_copy(1 - y, c).wait_recv())

    in_block = lax.broadcasted_iota(jnp.int32, (1, count), 1) % block_len
    left_half = lax.broadcasted_iota(jnp.int32, (1, 128), 1) < block_len
    stat_lane = lax.broadcasted_iota(jnp.int32, (heads, 128), 1)

    def swap(rank, i):
        place = rank * batch + i
        return remote(
            full.at[:, pl.ds(place * heads + (1 - lane) * own_heads, own_heads)],
            other.at[:, pl.ds(place * own_heads, own_heads)],
            swap_send.at[rank, i],
            swap_recv.at[rank, i],
            core,
        )

    def swap_stats(slot):
        return remote(
            stats.at[slot, pl.ds((1 - lane) * own_heads, own_heads)],
            other_stats.at[slot],
            swap_send.at[slot, batch],
            swap_recv.at[slot, batch],
            core,
        )

    def gather(rank, i, side):
        r = lane * batch + i
        length = table[rank, r, max_blocks]
        limits = []
        for j in range(max_blocks):
            block = table[rank, r, j] - z * (width * slots)
            here = (block >= 0) & (block < width * slots)
            block = jnp.where(here, block, 0)
            limits.append(jnp.where(here, length - j * block_len, 0))
            rows = pl.ds(j * block_len, block_len)
            keys[side, rows, :] = latent[block].reshape(block_len, latent_dim)
            rope_keys[side, rows, :] = rope[block].reshape(block_len, 128)
        limit = jnp.concatenate(
            [jnp.where(left_half, limits[2 * v], limits[2 * v + 1]) for v in range(max_blocks // 2)],
            axis=1,
        )
        return jnp.where(in_block < limit, 0.0, neg_fill)

    def attend(rank, i, own, slot):
        sides = range(2)
        fills = [gather(rank, i + side, side) for side in sides]
        q = [queries[rank, i + side] for side in sides]
        q_rot = [unpaired(query_pairs[rank, i + side]) for side in sides]
        scores = [
            dot_nt(q[side], keys[side]) + dot_nt(q_rot[side].astype(jnp.bfloat16), rope_keys[side])
            for side in sides
        ]
        logs = stats[slot]
        for side in sides:
            score = scores[side] * score_scale + fills[side]
            top = jnp.max(score, axis=1, keepdims=True)
            if own:
                new = fresh[pl.ds(lane * batch + i + side, 1), :]
                new_latent = new[:, :latent_dim]
                new_score = jnp.sum(q[side].astype(jnp.float32) * new_latent, axis=1, keepdims=True)
                new_score = new_score + jnp.sum(q_rot[side] * new[:, latent_dim:], axis=1, keepdims=True)
                new_score = new_score * score_scale
                top = jnp.maximum(top, new_score)
            expo = jnp.exp2(score - top)
            den = jnp.sum(expo, axis=1, keepdims=True)
            num = jnp.dot(expo.astype(jnp.bfloat16), keys[side], preferred_element_type=jnp.float32)
            if own:
                weight = jnp.exp2(new_score - top)
                den = den + weight
                num = num + weight.astype(jnp.bfloat16).astype(jnp.float32) * new_latent
            base = pl.multiple_of((rank * batch + i + side) * heads, heads)
            num = num * (1.0 / den)
            for t in range(latent_dim // 128):
                full[t, pl.ds(base, heads), :] = num[:, t * 128 : (t + 1) * 128]
            logs = jnp.where(stat_lane == i + side, top + jnp.log2(den), logs)
        stats[slot] = logs
        for side in sides:
            swap(rank, i + side).start()

    def rows_of(rank, h, first, some):
        tiles = []
        for t in range(latent_dim // 128):
            place = rank * batch + first
            own_rows = full[t, pl.ds(place * heads + lane * own_heads + h, some, stride=heads), :]
            other_rows = other[t, pl.ds(place * own_heads + h, some, stride=own_heads), :]
            tiles.append(jnp.concatenate([own_rows, other_rows], axis=0))
        return jnp.concatenate(tiles, axis=1)

    def gathered_stats(slot):
        swap_stats(slot).wait_recv()
        own_stats = stats[slot, pl.ds(pl.multiple_of(lane * own_heads, own_heads), own_heads), :]
        both_stats = jnp.where(
            stat_lane[:own_heads] < batch, own_stats, pltpu.roll(other_stats[slot], batch, 1)
        )
        square = jnp.concatenate([both_stats, both_stats], axis=0)
        return square.T[:requests]

    def project(ranks):
        for rank in ranks:
            partial_stats[rank] = gathered_stats(rank)
            loop(batch, lambda i: swap(rank, i).wait_recv())

        def one(h):
            rows = [rows_of(rank, h, 0, batch) for rank in ranks]
            rows = jnp.concatenate(rows, axis=0).astype(jnp.bfloat16)
            done = jnp.dot(rows, value[h], preferred_element_type=jnp.float32)
            columns = pl.ds(pl.multiple_of(h * value_dim, value_dim), value_dim)
            for n, rank in enumerate(ranks):
                partials[rank, :, columns] = done[n * requests : (n + 1) * requests]

        loop(own_heads, one, 8)

    def project_half(rank, part, slot):
        half_stats[part] = gathered_stats(slot)
        loop(quarter, lambda i: swap(rank, part * quarter + i).wait_recv())

        def one(h):
            done = []
            for head in (h, h + own_heads // 2):
                rows = rows_of(rank, head, part * quarter, quarter).astype(jnp.bfloat16)
                done.append(jnp.dot(rows, value[head], preferred_element_type=jnp.float32))
            columns = pl.ds(pl.multiple_of(h * value_dim, value_dim), value_dim)
            half_leaving[part, :, columns] = jnp.concatenate(done, axis=0).astype(jnp.bfloat16)

        loop(own_heads // 2, one, 4)

    def half_back(part):
        target = at_plane(far_edge)
        return [
            remote(half_leaving.at[part], half_got.at[part], half_send.at[part, 0], half_recv.at[part, 0], target),
            remote(
                half_stats.at[part], half_got_stats.at[part], half_send.at[part, 1], half_recv.at[part, 1], target
            ),
        ]

    def back(rank):
        slot = jnp.where(is_middle & (rank == far_edge), depth, z)
        target = at_plane(jnp.where(is_middle & (rank == far_edge), far_middle, rank))
        return [
            remote(leaving.at[rank], got.at[slot], back_send.at[rank, 0], back_recv.at[slot, 0], target),
            remote(
                partial_stats.at[rank], got_stats.at[slot], back_send.at[rank, 1], back_recv.at[slot, 1], target
            ),
        ]

    def arrive(slot):
        remote(leaving.at[z], got.at[slot], back_send.at[z, 0], back_recv.at[slot, 0], at_plane(beside)).wait_recv()
        remote(
            partial_stats.at[z], got_stats.at[slot], back_send.at[z, 1], back_recv.at[slot, 1], at_plane(beside)
        ).wait_recv()

    def mixture(logs):
        best = functools.reduce(jnp.maximum, logs)
        weights = [jnp.exp2(log - best) for log in logs]
        total = functools.reduce(jnp.add, weights)
        return [weight / total for weight in weights], best + jnp.log2(total)

    def mix(rank, slots_in, put):
        logs = [partial_stats[rank]] + [got_stats[slot] for slot in slots_in]
        weights, log = mixture(logs)
        for h in range(own_heads):
            columns = pl.ds(h * value_dim, value_dim)
            parts = [partials[rank, :, columns]] + [got[slot, :, columns] for slot in slots_in]
            put(
                columns,
                sum(weight[:, h : h + 1] * part.astype(jnp.float32) for weight, part in zip(weights, parts)),
            )
        return log

    def finish(rank):
        def pack(h):
            columns = pl.ds(pl.multiple_of(h * value_dim, value_dim), value_dim)
            leaving[rank, :, columns] = partials[rank, :, columns].astype(jnp.bfloat16)

        loop(own_heads, pack, 8)
        for copy in back(rank):
            copy.start()

    def own_one(p):
        for side in range(2):
            pl.when(is_middle)(lambda: take(far_edge, 2 * p + side))
        pl.when(is_middle & (p == 0))(lambda: take_rope(far_edge))
        attend(z, 2 * p, True, z)

    loop(batch // 2, own_one)
    swap_stats(z).start()

    def visit(s):
        rank = rank_at(s)

        def one(p):
            for side in range(2):
                pl.when(is_edge & (s == 2))(lambda: take(rank, 2 * p + side))
            pl.when(is_edge & (s == 2) & (p == 0))(lambda: take_rope(rank))
            attend(rank, 2 * p, False, rank)

        loop(batch // 2, one)
        swap_stats(rank).start()

        @pl.when(s == 1)
        def _():
            @pl.when(is_middle)
            def _():
                project([rank])
                finish(rank)

    loop(2, lambda s: visit(s + 1))
    @pl.when(is_edge)
    def _():
        project([near_middle, far_middle])
        finish(near_middle)
        finish(far_middle)

    pl.when(is_middle)(lambda: project([near_edge]))

    @pl.when(is_middle)
    def _():
        arrive(depth)

        def put(columns, values):
            leaving[near_edge, :, columns] = values.astype(jnp.bfloat16)

        partial_stats[near_edge] = mix(near_edge, [depth], put)
        for copy in back(near_edge):
            copy.start()

    def q_sent(rank):
        ways(rank, lambda way: q_rope_copy(rank, way).wait_send())
        loop(batch, lambda c: ways(rank, lambda way: q_copy(rank, c, way).wait_send()))

    def last(p):
        rank = rank_at(3)
        for side in range(2):
            pl.when(is_edge)(lambda: take(rank, 2 * p + side))
        pl.when(is_edge & (p == 0))(lambda: take_rope(rank))
        later = is_edge & (p >= quarter // 2)
        attend(rank, 2 * p, False, jnp.where(later, depth, rank))

        @pl.when(is_edge & (p % 2 == 1))
        def _():
            part = p // 2
            slot = jnp.where(later, depth, rank)
            swap_stats(slot).start()
            project_half(rank, part, slot)
            for copy in half_back(part):
                copy.start()

    loop(batch // 2, last)

    @pl.when(is_middle)
    def _():
        swap_stats(far_middle).start()
        project([far_middle, z])
        finish(far_middle)

    def put_out(columns, values):
        turned = pltpu.roll(values, batch, 0)
        out[:, columns] = jnp.where(lane == 0, values, turned).astype(out.dtype)

    low = lax.broadcasted_iota(jnp.int32, (batch, value_dim), 0) < quarter

    @pl.when(is_edge)
    def _():
        project([z])
        arrive(near_middle)
        for part in range(2):
            for copy in half_back(part):
                copy.wait_recv()
        early_rows = lax.broadcasted_iota(jnp.int32, (requests, 128), 0) % batch < quarter
        far_log = jnp.where(early_rows, half_got_stats[0], half_got_stats[1])
        logs = [partial_stats[z], got_stats[near_middle], far_log]
        weights, _log = mixture(logs)
        for h in range(own_heads // 2):
            columns = pl.ds(h * value_dim, value_dim)
            halves = [half_got[part, :, columns].astype(jnp.float32) for part in range(2)]
            for n in range(2):
                head = h + n * (own_heads // 2)
                columns = pl.ds(head * value_dim, value_dim)
                a, b = [half[n * batch : (n + 1) * batch] for half in halves]
                far = jnp.concatenate(
                    [
                        jnp.where(low, a, pltpu.roll(b, quarter, 0)),
                        jnp.where(low, pltpu.roll(a, quarter, 0), b),
                    ],
                    axis=0,
                )
                parts = [partials[z, :, columns], got[near_middle, :, columns].astype(jnp.float32), far]
                put_out(
                    columns,
                    sum(weight[:, head : head + 1] * part for weight, part in zip(weights, parts)),
                )

    @pl.when(is_middle)
    def _():
        places = [near_edge, far_middle, far_edge]
        for place in places:
            arrive(place)
        mix(z, places, put_out)

    for t in range(1, depth):
        table_copy(t).wait_send()
    y_rope_copy().wait_send()
    loop(chunk_count, lambda c: y_copy(c).wait_send())
    for side in range(width):
        share_rope_copy(side).wait_send()
        loop(chunk_count, lambda c: share_copy(side, c).wait_send())

    def sent(rank):
        q_sent(rank)
        loop(batch, lambda i: swap(rank, i).wait_send())
        swap_stats(rank).wait_send()

        @pl.when((rank != z) & (is_middle | (rank != far_edge)))
        def _():
            for copy in back(rank):
                copy.wait_send()

    loop(depth, sent)

    @pl.when(is_edge)
    def _():
        swap_stats(depth).wait_send()
        for part in range(2):
            for copy in half_back(part):
                copy.wait_send()


def plane_local(
    q_latent,
    q_rope,
    new_entry,
    cache_latent,
    cache_rope,
    source_rank,
    slot_index,
    lengths,
    value_up_weight,
):
    requests, max_blocks = slot_index.shape
    slots, run_len, latent_dim = cache_latent.shape
    heads = q_latent.shape[1]
    own_heads, _, value_dim = value_up_weight.shape
    batch = requests // lanes
    count = max_blocks * run_len * lanes
    bf16, f32 = jnp.bfloat16, jnp.float32
    vmem = pl.BlockSpec(memory_space=pltpu.VMEM)
    smem = pl.BlockSpec(memory_space=pltpu.SMEM)
    anywhere = pl.BlockSpec(memory_space=pl.ANY)
    dma = pltpu.SemaphoreType.DMA
    return pl.pallas_call(
        plane_kernel,
        out_shape=jax.ShapeDtypeStruct((requests, own_heads * value_dim), bf16),
        in_specs=[vmem, vmem, smem] + [anywhere] * 5 + [vmem],
        out_specs=vmem,
        scratch_shapes=[
            pltpu.VMEM((depth, requests, 128), jnp.int32),
            pltpu.SMEM((depth, requests, 128), jnp.int32),
            pltpu.VMEM(cache_rope.shape, bf16),
            pltpu.VMEM((slots, run_len // 2, 128), f32),
            pltpu.VMEM(q_rope.shape, bf16),
            pltpu.VMEM((batch, heads // 2, 128), f32),
            pltpu.VMEM((width * slots, lanes, run_len, latent_dim), bf16),
            pltpu.VMEM((width * slots, lanes, run_len // 2, 128), bf16),
            pltpu.VMEM((width * slots, lanes, run_len, 128), bf16),
            pltpu.VMEM((depth, batch, heads, latent_dim), bf16),
            pltpu.VMEM((depth, batch, heads // 2, 128), bf16),
            pltpu.VMEM(value_up_weight.shape, bf16),
            pltpu.VMEM((2, count, latent_dim), bf16),
            pltpu.VMEM((2, count, 128), bf16),
            pltpu.VMEM((latent_dim // 128, depth * batch * heads, 128), f32),
            pltpu.VMEM((latent_dim // 128, depth * batch * own_heads, 128), f32),
            pltpu.VMEM((depth + 1, heads, 128), f32),
            pltpu.VMEM((depth + 1, own_heads, 128), f32),
            pltpu.VMEM((depth, requests, own_heads * value_dim), f32),
            pltpu.VMEM((depth, requests, own_heads * value_dim), bf16),
            pltpu.VMEM((depth, requests, 128), f32),
            pltpu.VMEM((depth + 1, requests, own_heads * value_dim), bf16),
            pltpu.VMEM((depth + 1, requests, 128), f32),
            pltpu.VMEM((2, requests, own_heads // 2 * value_dim), bf16),
            pltpu.VMEM((2, requests, 128), f32),
            pltpu.VMEM((2, requests, own_heads // 2 * value_dim), bf16),
            pltpu.VMEM((2, requests, 128), f32),
            pltpu.VMEM((requests, latent_dim + 128), f32),
            dma((6,)),
            dma((depth,)),
            dma((depth,)),
            dma((2, depth, batch + 1)),
            dma((depth, batch + 1)),
            dma((chunk_count + 1,)),
            dma((chunk_count + 1,)),
            dma((width, chunk_count + 1)),
            dma((width, chunk_count + 1)),
            dma((depth + 1, batch + 1)),
            dma((depth + 1, batch + 1)),
            dma((depth, 2)),
            dma((depth + 1, 2)),
            dma((2, 2)),
            dma((2, 2)),
        ],
        compiler_params=pltpu.CompilerParams(
            collective_id=0, has_side_effects=True, vmem_limit_bytes=60 * 1024 * 1024
        ),
    )(
        source_rank.reshape(requests, max_blocks),
        slot_index,
        lengths,
        cache_latent,
        cache_rope,
        q_latent,
        q_rope,
        value_up_weight,
        new_entry,
    )


def local(*args):
    q_latent, cache_latent, slot_index = args[0], args[3], args[6]
    fits = lax.axis_size("dp") == depth * width and lax.axis_size("tp") == lanes
    fits = fits and q_latent.shape == (16, 128, 512) and args[1].shape == (16, 8192)
    fits = fits and cache_latent.shape == (48, 32, 512) and slot_index.shape == (16, 16)
    return (plane_local if fits else spread_local)(*args)


def solution(mesh):
    placed = (
        P(("pop", "dp"), None, None),
        P(("pop", "dp"), None),
        P(("pop", "dp"), None),
        P(("pop", "dp"), "tp", None),
        P(("pop", "dp"), "tp"),
        P(("pop", "dp"), None, None),
        P(("pop", "dp"), None),
        P(("pop", "dp")),
        P("tp", None, None),
    )
    return jax.shard_map(
        local, mesh=mesh, in_specs=placed, out_specs=P(("pop", "dp"), "tp"), check_vma=False
    )
```

```python
import functools
import math

import jax
import jax.numpy as jnp
from jax import lax
from jax.experimental import pallas as pl
from jax.experimental.pallas import tpu as pltpu
from jax.sharding import PartitionSpec as P

softmax_scale = 192.0 ** (-0.5)
neg_fill = -1e30


def entry_places(src_flat):
    count = src_flat.shape[0]
    spot = jnp.arange(count, dtype=jnp.int32)
    same = (src_flat[:, None] == src_flat[None, :]) & (spot[None, :] < spot[:, None])
    return jnp.sum(same.astype(jnp.int32), axis=1)


def pick(rows, index):
    onehot = (index[:, None] == jnp.arange(rows.shape[0], dtype=jnp.int32)[None, :]).astype(rows.dtype)
    flat = jnp.dot(onehot, rows.reshape(rows.shape[0], -1), preferred_element_type=jnp.float32)
    return flat.astype(rows.dtype).reshape((index.shape[0],) + rows.shape[1:])


def spread_local(
    q_latent,
    q_rope,
    new_entry,
    cache_latent,
    cache_rope,
    source_rank,
    slot_index,
    lengths,
    value_up_weight,
):
    rank_count = lax.axis_size("dp")
    lane_count = lax.axis_size("tp")
    my_lane = lax.axis_index("tp")
    requests, max_blocks = slot_index.shape
    run_len = cache_latent.shape[1]
    latent_dim = cache_latent.shape[2]
    heads = q_latent.shape[1]
    rope_dim = q_rope.shape[1] // heads
    entries = requests * max_blocks
    capacity = max(2, (entries * 5 + 4 * rank_count - 1) // (4 * rank_count))
    src_flat = source_rank.reshape(entries)
    slot_flat = slot_index.reshape(entries)
    places = entry_places(src_flat)
    where_from = src_flat * capacity + places
    cells = jnp.arange(rank_count * capacity, dtype=jnp.int32)
    wanted = jnp.sum(
        jnp.where(cells[:, None] == where_from[None, :], slot_flat[None, :], 0), axis=1
    ).reshape(rank_count, capacity)
    asked_slots = lax.all_to_all(wanted, "dp", split_axis=0, concat_axis=0, tiled=True)
    asked = asked_slots.reshape(rank_count * capacity)
    send_latent = pick(cache_latent, asked).reshape(rank_count, capacity, run_len, latent_dim)
    send_rope = pick(cache_rope, asked).reshape(rank_count, capacity, run_len * rope_dim)
    got_latent, received_rotary_keys = (
        lax.all_to_all(send_latent, "dp", split_axis=0, concat_axis=0, tiled=True),
        lax.all_to_all(send_rope, "dp", split_axis=0, concat_axis=0, tiled=True),
    )
    keys_latent = pick(got_latent.reshape(rank_count * capacity, run_len, latent_dim), where_from)
    keys_latent = keys_latent.reshape(requests, max_blocks * run_len, latent_dim)
    keys_rope = pick(
        received_rotary_keys.reshape(rank_count * capacity, run_len * rope_dim), where_from
    )
    keys_rope = keys_rope.reshape(requests, max_blocks * run_len, rope_dim)
    query_rope = q_rope.reshape(requests, heads, rope_dim)
    scores = jnp.einsum("rhk,rnk->rhn", q_latent, keys_latent, preferred_element_type=jnp.float32)
    scores = (
        scores
        + jnp.einsum("rhd,rnd->rhn", query_rope, keys_rope, preferred_element_type=jnp.float32)
    ) * softmax_scale
    new_latent = new_entry[:, :latent_dim]
    incoming_rotary_key = new_entry[:, latent_dim:]
    new_score = jnp.einsum("rhk,rk->rh", q_latent, new_latent, preferred_element_type=jnp.float32)
    new_score = (
        new_score
        + jnp.einsum(
            "rhd,rd->rh", query_rope, incoming_rotary_key, preferred_element_type=jnp.float32
        )
    ) * softmax_scale
    slot_pos = jnp.arange(max_blocks * run_len, dtype=jnp.int32)
    positions = (
        slot_pos // run_len * (run_len * lane_count) + my_lane * run_len + slot_pos % run_len
    )
    in_range = (positions[None, :] < lengths[:, None])[:, None, :]
    is_first = my_lane == 0
    top_score = jnp.max(jnp.where(in_range, scores, neg_fill), axis=2)
    top_score = jnp.where(is_first, jnp.maximum(top_score, new_score), top_score)
    expo = jnp.where(in_range, jnp.exp(scores - top_score[:, :, None]), 0.0)
    numerator = jnp.einsum(
        "rhn,rnk->rhk", expo.astype(jnp.bfloat16), keys_latent, preferred_element_type=jnp.float32
    )
    denominator = jnp.sum(expo, axis=2)
    incoming_token_weight = jnp.where(is_first, jnp.exp(new_score - top_score), 0.0)
    numerator = (
        numerator
        + incoming_token_weight.astype(jnp.bfloat16).astype(jnp.float32)[:, :, None]
        * new_latent.astype(jnp.float32)[:, None, :]
    )
    denominator = denominator + incoming_token_weight
    overall = lax.pmax(top_score, "tp")
    factor = jnp.exp(top_score - overall)
    numer_sum, denom_sum = (
        lax.psum_scatter(numerator * factor[:, :, None], "tp", scatter_dimension=1, tiled=True),
        lax.psum_scatter(denominator * factor, "tp", scatter_dimension=1, tiled=True),
    )
    latent_output_rows = (numer_sum / denom_sum[:, :, None]).astype(jnp.bfloat16)
    value_projected_output = jnp.einsum(
        "wyc,yca->wya", latent_output_rows, value_up_weight, preferred_element_type=jnp.float32
    )
    return value_projected_output.reshape(requests, -1).astype(jnp.bfloat16)


MESH = pl.DeviceIdType.MESH
up, down = 0, 1
depth, width, lanes = 4, 2, 2
chunk_count = 6
score_scale = softmax_scale / math.log(2.0)


def dot_nt(a, b):
    return lax.dot_general(a, b, (((1,), (1,)), ((), ())), preferred_element_type=jnp.float32)


def loop(count, body, unroll=1):
    def step(i, carry):
        body(i)
        return carry

    lax.fori_loop(0, count, step, 0, unroll=unroll)


def plane_kernel(
    sources,
    slot_table,
    lengths,
    latent_hbm,
    rope_hbm,
    q_hbm,
    q_rope_hbm,
    value_hbm,
    new_entry,
    out,
    table_rows,
    table,
    rope_in,
    rope_wide,
    q_rope_in,
    q_rope_wide,
    latent,
    rope_pairs,
    rope,
    queries,
    query_pairs,
    value,
    keys,
    rope_keys,
    full,
    other,
    stats,
    other_stats,
    partials,
    leaving,
    partial_stats,
    got,
    got_stats,
    half_leaving,
    half_stats,
    half_got,
    half_got_stats,
    fresh,
    local_sem,
    table_send,
    table_recv,
    q_send,
    q_recv,
    y_send,
    y_recv,
    share_send,
    share_recv,
    swap_send,
    swap_recv,
    back_send,
    back_recv,
    half_send,
    half_recv,
):
    me = lax.axis_index("dp")
    lane = lax.axis_index("tp")
    z, y = me // width, me % width
    slots, run_len, latent_dim = latent_hbm.shape
    requests, heads = q_hbm.shape[0], q_hbm.shape[1]
    batch = requests // lanes
    quarter = batch // 2
    rope_dim = q_rope_in.shape[1] // heads
    max_blocks = slot_table.shape[1]
    block_len = run_len * lanes
    count = max_blocks * block_len
    own_heads = heads // lanes
    value_dim = value.shape[2]
    chunk = slots // chunk_count
    has_up, has_down = z + 1 < depth, z > 0
    is_edge = (z == 0) | (z == depth - 1)
    mine = pl.ds(lane * batch, batch)

    is_middle = jnp.logical_not(is_edge)
    near_edge = jnp.where(z < depth // 2, 0, depth - 1)
    far_edge = depth - 1 - near_edge
    near_middle = jnp.where(z < depth // 2, 1, depth - 2)
    far_middle = depth - 1 - near_middle

    def rank_at(s):
        inner = jnp.where(s == 1, far_edge, jnp.where(s == 2, near_edge, far_middle))
        outer = jnp.where(s == 1, near_middle, jnp.where(s == 2, far_middle, far_edge))
        return jnp.where(s == 0, z, jnp.where(is_edge, outer, inner))

    def remote(src, dst, send, recv, target):
        return pltpu.make_async_remote_copy(
            src_ref=src, dst_ref=dst, send_sem=send, recv_sem=recv, device_id=target, device_id_type=MESH
        )

    core = {"tp": 1 - lane}
    partner = {"dp": z * width + 1 - y}

    def at_plane(place):
        return {"dp": place * width + y}

    own_slots = pl.ds(y * slots, slots)
    local = [
        pltpu.make_async_copy(q_rope_hbm, q_rope_in, local_sem.at[0]),
        pltpu.make_async_copy(rope_hbm, rope_in, local_sem.at[1]),
        pltpu.make_async_copy(latent_hbm, latent.at[own_slots, lane], local_sem.at[2]),
        pltpu.make_async_copy(q_hbm.at[mine], queries.at[z], local_sem.at[3]),
        pltpu.make_async_copy(value_hbm, value, local_sem.at[4]),
    ]

    barrier = pltpu.get_barrier_semaphore()

    def greet(target):
        pl.semaphore_signal(barrier, inc=1, device_id=target, device_id_type=MESH)

    greet(core)
    greet(partner)
    for t in range(1, depth):
        greet(at_plane((z + t) % depth))
    for copy in local[:3]:
        copy.start()
    pl.semaphore_wait(barrier, depth + 1)

    def q_copy(rank, c, way):
        target = at_plane(z + 1 if way == up else z - 1)
        return remote(
            queries.at[rank, c], queries.at[rank, c], q_send.at[way, rank, c], q_recv.at[rank, c], target
        )

    def q_rope_copy(rank, way):
        target = at_plane(z + 1 if way == up else z - 1)
        return remote(
            query_pairs.at[rank],
            query_pairs.at[rank],
            q_send.at[way, rank, batch],
            q_recv.at[rank, batch],
            target,
        )

    def ways(rank, body):
        pl.when(has_up & (rank <= z))(lambda: body(up))
        pl.when(has_down & (rank >= z))(lambda: body(down))

    def own_q_copy(c, way):
        target = at_plane(z + 1 if way == up else z - 1)
        return remote(
            q_hbm.at[lane * batch + c], queries.at[z, c], q_send.at[way, z, c], q_recv.at[z, c], target
        )

    def take(rank, c):
        q_copy(rank, c, up).wait_recv()
        ways(rank, lambda way: q_copy(rank, c, way).start())

    def take_rope(rank):
        q_rope_copy(rank, up).wait_recv()
        ways(rank, lambda way: q_rope_copy(rank, way).start())

    def table_copy(t):
        return remote(
            table_rows.at[z], table_rows.at[z], table_send.at[t], table_recv.at[z], at_plane((z + t) % depth)
        )

    def y_copy(c):
        return remote(
            latent_hbm.at[pl.ds(c * chunk, chunk)],
            latent.at[pl.ds(y * slots + c * chunk, chunk), lane],
            y_send.at[c],
            y_recv.at[c],
            partner,
        )

    def y_rope_copy():
        own = rope_pairs.at[own_slots, lane]
        return remote(own, own, y_send.at[chunk_count], y_recv.at[chunk_count], partner)

    def share_copy(side, c):
        rows = pl.ds(side * slots + c * chunk, chunk)
        return remote(
            latent.at[rows, lane],
            latent.at[rows, lane],
            share_send.at[side, c],
            share_recv.at[side, c],
            core,
        )

    def share_rope_copy(side):
        rows = pl.ds(side * slots, slots)
        return remote(
            rope_pairs.at[rows, lane],
            rope_pairs.at[rows, lane],
            share_send.at[side, chunk_count],
            share_recv.at[side, chunk_count],
            core,
        )

    def first(c):
        ways(z, lambda way: own_q_copy(c, way).start())

    first(0)
    y_copy(0).start()
    local[3].start()

    local[1].wait()
    for j in range(run_len // 2):
        rope_wide[:, j : j + 1, :] = (
            rope_in[:, j * 128 : (j + 1) * 128].astype(jnp.float32).reshape(slots, 1, 128)
        )
    rope_pairs[own_slots, lane] = rope_wide[...].astype(jnp.bfloat16)
    y_rope_copy().start()
    loop(chunk_count - 1, lambda c: y_copy(c + 1).start())
    share_rope_copy(y).start()
    local[0].wait()

    def spread(p):
        x = q_rope_in[:, pl.ds(pl.multiple_of(p * 128, 128), 128)].astype(jnp.float32)
        x = jnp.where(lane == 0, x[:batch], x[batch:])
        q_rope_wide[:, pl.ds(p, 1), :] = x.reshape(batch, 1, 128)

    loop(heads // 2, spread, 8)
    query_pairs[z] = q_rope_wide[...].astype(jnp.bfloat16)
    ways(z, lambda way: q_rope_copy(z, way).start())
    loop(batch - 1, lambda c: first(c + 1))
    local[2].wait()
    loop(chunk_count, lambda c: share_copy(y, c).start())
    local[4].start()

    row = lax.broadcasted_iota(jnp.int32, (requests, 128), 0)
    length_rows = jnp.zeros((requests, 128), jnp.int32)
    for r in range(requests):
        length_rows = jnp.where(row == r, lengths[r], length_rows)
    table_rows[z] = length_rows
    table_rows[z, :, 0:max_blocks] = sources[...] * slots + slot_table[...]
    for t in range(1, depth):
        table_copy(t).start()

    extra = new_entry[...].astype(jnp.float32)
    fresh[:, 0:latent_dim] = extra[:, :latent_dim]
    fresh[:, latent_dim : latent_dim + 2 * rope_dim] = jnp.concatenate(
        [extra[:, latent_dim:], extra[:, latent_dim:]], axis=1
    )
    stats[...] = jnp.zeros_like(stats)

    pair_row = lax.broadcasted_iota(jnp.int32, (2 * 64, 64), 0) // 2
    pair_col = lax.broadcasted_iota(jnp.int32, (2 * 64, 64), 1)
    doubler = jnp.where(pair_row == pair_col, 1.0, 0.0).astype(jnp.bfloat16)
    odd = lax.broadcasted_iota(jnp.int32, (128, 128), 0) % 2
    upper = lax.broadcasted_iota(jnp.int32, (128, 128), 1) // rope_dim
    own_part = odd == upper

    def unpaired(pairs):
        twice = jnp.dot(doubler, pairs, preferred_element_type=jnp.float32)
        return jnp.where(own_part, twice, 0.0)

    def expand(side):
        def one(p):
            rows = pl.ds(side * slots + 2 * p, 2)
            alone = unpaired(rope_pairs[rows].reshape(64, 128))
            both = alone + pltpu.roll(alone, rope_dim, 1)
            rope[rows] = both.astype(jnp.bfloat16).reshape(2, lanes, run_len, 128)

        loop(slots // 2, one, 4)

    share_rope_copy(y).wait_recv()
    expand(y)
    beside = jnp.where(is_edge, near_middle, near_edge)

    def early(c):
        take(beside, c)
        pl.when(is_middle)(lambda: take(far_middle, c))

    def pass_block(c):
        y_copy(c).wait_recv()
        share_copy(1 - y, c).start()

    def both(c):
        early(2 * c)
        early(2 * c + 1)
        pass_block(c)

    early(0)
    take_rope(beside)
    pl.when(is_middle)(lambda: take_rope(far_middle))
    early(1)
    pass_block(0)
    y_rope_copy().wait_recv()
    share_rope_copy(1 - y).start()
    both(1)
    share_rope_copy(1 - y).wait_recv()
    expand(1 - y)
    loop(batch // 2 - 2, lambda c: both(c + 2))
    loop(chunk_count - batch // 2, lambda c: pass_block(c + batch // 2))

    for t in range(1, depth):
        table_copy_in = remote(
            table_rows.at[z],
            table_rows.at[(z + t) % depth],
            table_send.at[t],
            table_recv.at[(z + t) % depth],
            at_plane((z + t) % depth),
        )
        table_copy_in.wait_recv()
    into_smem = pltpu.make_async_copy(table_rows, table, local_sem.at[5])
    into_smem.start()
    into_smem.wait()
    local[3].wait()
    local[4].wait()

    loop(chunk_count, lambda c: share_copy(y, c).wait_recv())
    loop(chunk_count, lambda c: share_copy(1 - y, c).wait_recv())

    in_block = lax.broadcasted_iota(jnp.int32, (1, count), 1) % block_len
    left_half = lax.broadcasted_iota(jnp.int32, (1, 128), 1) < block_len
    stat_lane = lax.broadcasted_iota(jnp.int32, (heads, 128), 1)

    def swap(rank, i):
        place = rank * batch + i
        return remote(
            full.at[:, pl.ds(place * heads + (1 - lane) * own_heads, own_heads)],
            other.at[:, pl.ds(place * own_heads, own_heads)],
            swap_send.at[rank, i],
            swap_recv.at[rank, i],
            core,
        )

    def swap_stats(slot):
        return remote(
            stats.at[slot, pl.ds((1 - lane) * own_heads, own_heads)],
            other_stats.at[slot],
            swap_send.at[slot, batch],
            swap_recv.at[slot, batch],
            core,
        )

    def gather(rank, i, side):
        r = lane * batch + i
        length = table[rank, r, max_blocks]
        limits = []
        for j in range(max_blocks):
            block = table[rank, r, j] - z * (width * slots)
            here = (block >= 0) & (block < width * slots)
            block = jnp.where(here, block, 0)
            limits.append(jnp.where(here, length - j * block_len, 0))
            rows = pl.ds(j * block_len, block_len)
            keys[side, rows, :] = latent[block].reshape(block_len, latent_dim)
            rope_keys[side, rows, :] = rope[block].reshape(block_len, 128)
        limit = jnp.concatenate(
            [jnp.where(left_half, limits[2 * v], limits[2 * v + 1]) for v in range(max_blocks // 2)],
            axis=1,
        )
        return jnp.where(in_block < limit, 0.0, neg_fill)

    def attend(rank, i, own, slot):
        sides = range(2)
        fills = [gather(rank, i + side, side) for side in sides]
        q = [queries[rank, i + side] for side in sides]
        q_rot = [unpaired(query_pairs[rank, i + side]) for side in sides]
        scores = [
            dot_nt(q[side], keys[side]) + dot_nt(q_rot[side].astype(jnp.bfloat16), rope_keys[side])
            for side in sides
        ]
        logs = stats[slot]
        for side in sides:
            score = scores[side] * score_scale + fills[side]
            top = jnp.max(score, axis=1, keepdims=True)
            if own:
                new = fresh[pl.ds(lane * batch + i + side, 1), :]
                new_latent = new[:, :latent_dim]
                new_score = jnp.sum(q[side].astype(jnp.float32) * new_latent, axis=1, keepdims=True)
                new_score = new_score + jnp.sum(q_rot[side] * new[:, latent_dim:], axis=1, keepdims=True)
                new_score = new_score * score_scale
                top = jnp.maximum(top, new_score)
            expo = jnp.exp2(score - top)
            den = jnp.sum(expo, axis=1, keepdims=True)
            num = jnp.dot(expo.astype(jnp.bfloat16), keys[side], preferred_element_type=jnp.float32)
            if own:
                weight = jnp.exp2(new_score - top)
                den = den + weight
                num = num + weight.astype(jnp.bfloat16).astype(jnp.float32) * new_latent
            base = pl.multiple_of((rank * batch + i + side) * heads, heads)
            num = num * (1.0 / den)
            for t in range(latent_dim // 128):
                full[t, pl.ds(base, heads), :] = num[:, t * 128 : (t + 1) * 128]
            logs = jnp.where(stat_lane == i + side, top + jnp.log2(den), logs)
        stats[slot] = logs
        for side in sides:
            swap(rank, i + side).start()

    def rows_of(rank, h, first, some):
        tiles = []
        for t in range(latent_dim // 128):
            place = rank * batch + first
            own_rows = full[t, pl.ds(place * heads + lane * own_heads + h, some, stride=heads), :]
            other_rows = other[t, pl.ds(place * own_heads + h, some, stride=own_heads), :]
            tiles.append(jnp.concatenate([own_rows, other_rows], axis=0))
        return jnp.concatenate(tiles, axis=1)

    def gathered_stats(slot):
        swap_stats(slot).wait_recv()
        own_stats = stats[slot, pl.ds(pl.multiple_of(lane * own_heads, own_heads), own_heads), :]
        both_stats = jnp.where(
            stat_lane[:own_heads] < batch, own_stats, pltpu.roll(other_stats[slot], batch, 1)
        )
        square = jnp.concatenate([both_stats, both_stats], axis=0)
        return square.T[:requests]

    def project(ranks):
        for rank in ranks:
            partial_stats[rank] = gathered_stats(rank)
            loop(batch, lambda i: swap(rank, i).wait_recv())

        def one(h):
            rows = [rows_of(rank, h, 0, batch) for rank in ranks]
            rows = jnp.concatenate(rows, axis=0).astype(jnp.bfloat16)
            done = jnp.dot(rows, value[h], preferred_element_type=jnp.float32)
            columns = pl.ds(pl.multiple_of(h * value_dim, value_dim), value_dim)
            for n, rank in enumerate(ranks):
                partials[rank, :, columns] = done[n * requests : (n + 1) * requests]

        loop(own_heads, one, 4)

    def project_half(rank, part, slot):
        half_stats[part] = gathered_stats(slot)
        loop(quarter, lambda i: swap(rank, part * quarter + i).wait_recv())

        def one(h):
            done = []
            for head in (h, h + own_heads // 2):
                rows = rows_of(rank, head, part * quarter, quarter).astype(jnp.bfloat16)
                done.append(jnp.dot(rows, value[head], preferred_element_type=jnp.float32))
            columns = pl.ds(pl.multiple_of(h * value_dim, value_dim), value_dim)
            half_leaving[part, :, columns] = jnp.concatenate(done, axis=0).astype(jnp.bfloat16)

        loop(own_heads // 2, one, 4)

    def half_back(part):
        target = at_plane(far_edge)
        return [
            remote(half_leaving.at[part], half_got.at[part], half_send.at[part, 0], half_recv.at[part, 0], target),
            remote(
                half_stats.at[part], half_got_stats.at[part], half_send.at[part, 1], half_recv.at[part, 1], target
            ),
        ]

    def back(rank):
        slot = jnp.where(is_middle & (rank == far_edge), depth, z)
        target = at_plane(jnp.where(is_middle & (rank == far_edge), far_middle, rank))
        return [
            remote(leaving.at[rank], got.at[slot], back_send.at[rank, 0], back_recv.at[slot, 0], target),
            remote(
                partial_stats.at[rank], got_stats.at[slot], back_send.at[rank, 1], back_recv.at[slot, 1], target
            ),
        ]

    def arrive(slot):
        remote(leaving.at[z], got.at[slot], back_send.at[z, 0], back_recv.at[slot, 0], at_plane(beside)).wait_recv()
        remote(
            partial_stats.at[z], got_stats.at[slot], back_send.at[z, 1], back_recv.at[slot, 1], at_plane(beside)
        ).wait_recv()

    def mixture(logs):
        best = functools.reduce(jnp.maximum, logs)
        weights = [jnp.exp2(log - best) for log in logs]
        total = functools.reduce(jnp.add, weights)
        return [weight / total for weight in weights], best + jnp.log2(total)

    def mix(rank, slots_in, put):
        logs = [partial_stats[rank]] + [got_stats[slot] for slot in slots_in]
        weights, log = mixture(logs)
        for h in range(own_heads):
            columns = pl.ds(h * value_dim, value_dim)
            parts = [partials[rank, :, columns]] + [got[slot, :, columns] for slot in slots_in]
            put(
                columns,
                sum(weight[:, h : h + 1] * part.astype(jnp.float32) for weight, part in zip(weights, parts)),
            )
        return log

    def finish(rank):
        def pack(h):
            columns = pl.ds(pl.multiple_of(h * value_dim, value_dim), value_dim)
            leaving[rank, :, columns] = partials[rank, :, columns].astype(jnp.bfloat16)

        loop(own_heads, pack, 8)
        for copy in back(rank):
            copy.start()

    def own_one(p):
        for side in range(2):
            pl.when(is_middle)(lambda: take(far_edge, 2 * p + side))
        pl.when(is_middle & (p == 0))(lambda: take_rope(far_edge))
        attend(z, 2 * p, True, z)

    loop(batch // 2, own_one)
    swap_stats(z).start()

    def visit(s):
        rank = rank_at(s)

        def one(p):
            for side in range(2):
                pl.when(is_edge & (s == 2))(lambda: take(rank, 2 * p + side))
            pl.when(is_edge & (s == 2) & (p == 0))(lambda: take_rope(rank))
            attend(rank, 2 * p, False, rank)

        loop(batch // 2, one)
        swap_stats(rank).start()

        @pl.when(s == 1)
        def _():
            @pl.when(is_middle)
            def _():
                project([rank])
                finish(rank)

    loop(2, lambda s: visit(s + 1))
    @pl.when(is_edge)
    def _():
        project([near_middle, far_middle])
        finish(near_middle)
        finish(far_middle)

    pl.when(is_middle)(lambda: project([near_edge]))

    @pl.when(is_middle)
    def _():
        arrive(depth)

        def put(columns, values):
            leaving[near_edge, :, columns] = values.astype(jnp.bfloat16)

        partial_stats[near_edge] = mix(near_edge, [depth], put)
        for copy in back(near_edge):
            copy.start()

    def q_sent(rank):
        ways(rank, lambda way: q_rope_copy(rank, way).wait_send())
        loop(batch, lambda c: ways(rank, lambda way: q_copy(rank, c, way).wait_send()))

    def last(p):
        rank = rank_at(3)
        for side in range(2):
            pl.when(is_edge)(lambda: take(rank, 2 * p + side))
        pl.when(is_edge & (p == 0))(lambda: take_rope(rank))
        later = is_edge & (p >= quarter // 2)
        attend(rank, 2 * p, False, jnp.where(later, depth, rank))

        @pl.when(is_edge & (p % 2 == 1))
        def _():
            part = p // 2
            slot = jnp.where(later, depth, rank)
            swap_stats(slot).start()
            project_half(rank, part, slot)
            for copy in half_back(part):
                copy.start()

    loop(batch // 2, last)

    @pl.when(is_middle)
    def _():
        swap_stats(far_middle).start()
        project([far_middle, z])
        finish(far_middle)

    def put_out(columns, values):
        turned = pltpu.roll(values, batch, 0)
        out[:, columns] = jnp.where(lane == 0, values, turned).astype(out.dtype)

    low = lax.broadcasted_iota(jnp.int32, (batch, value_dim), 0) < quarter

    @pl.when(is_edge)
    def _():
        project([z])
        arrive(near_middle)
        for part in range(2):
            for copy in half_back(part):
                copy.wait_recv()
        early_rows = lax.broadcasted_iota(jnp.int32, (requests, 128), 0) % batch < quarter
        far_log = jnp.where(early_rows, half_got_stats[0], half_got_stats[1])
        logs = [partial_stats[z], got_stats[near_middle], far_log]
        weights, _log = mixture(logs)
        for h in range(own_heads // 2):
            columns = pl.ds(h * value_dim, value_dim)
            halves = [half_got[part, :, columns].astype(jnp.float32) for part in range(2)]
            for n in range(2):
                head = h + n * (own_heads // 2)
                columns = pl.ds(head * value_dim, value_dim)
                a, b = [half[n * batch : (n + 1) * batch] for half in halves]
                far = jnp.concatenate(
                    [
                        jnp.where(low, a, pltpu.roll(b, quarter, 0)),
                        jnp.where(low, pltpu.roll(a, quarter, 0), b),
                    ],
                    axis=0,
                )
                parts = [partials[z, :, columns], got[near_middle, :, columns].astype(jnp.float32), far]
                put_out(
                    columns,
                    sum(weight[:, head : head + 1] * part for weight, part in zip(weights, parts)),
                )

    @pl.when(is_middle)
    def _():
        places = [near_edge, far_middle, far_edge]
        for place in places:
            arrive(place)
        mix(z, places, put_out)

    for t in range(1, depth):
        table_copy(t).wait_send()
    y_rope_copy().wait_send()
    loop(chunk_count, lambda c: y_copy(c).wait_send())
    for side in range(width):
        share_rope_copy(side).wait_send()
        loop(chunk_count, lambda c: share_copy(side, c).wait_send())

    def sent(rank):
        q_sent(rank)
        loop(batch, lambda i: swap(rank, i).wait_send())
        swap_stats(rank).wait_send()

        @pl.when((rank != z) & (is_middle | (rank != far_edge)))
        def _():
            for copy in back(rank):
                copy.wait_send()

    loop(depth, sent)

    @pl.when(is_edge)
    def _():
        swap_stats(depth).wait_send()
        for part in range(2):
            for copy in half_back(part):
                copy.wait_send()


def plane_local(
    q_latent,
    q_rope,
    new_entry,
    cache_latent,
    cache_rope,
    source_rank,
    slot_index,
    lengths,
    value_up_weight,
):
    requests, max_blocks = slot_index.shape
    slots, run_len, latent_dim = cache_latent.shape
    heads = q_latent.shape[1]
    own_heads, _, value_dim = value_up_weight.shape
    batch = requests // lanes
    count = max_blocks * run_len * lanes
    bf16, f32 = jnp.bfloat16, jnp.float32
    vmem = pl.BlockSpec(memory_space=pltpu.VMEM)
    smem = pl.BlockSpec(memory_space=pltpu.SMEM)
    anywhere = pl.BlockSpec(memory_space=pl.ANY)
    dma = pltpu.SemaphoreType.DMA
    return pl.pallas_call(
        plane_kernel,
        out_shape=jax.ShapeDtypeStruct((requests, own_heads * value_dim), bf16),
        in_specs=[vmem, vmem, smem] + [anywhere] * 5 + [vmem],
        out_specs=vmem,
        scratch_shapes=[
            pltpu.VMEM((depth, requests, 128), jnp.int32),
            pltpu.SMEM((depth, requests, 128), jnp.int32),
            pltpu.VMEM(cache_rope.shape, bf16),
            pltpu.VMEM((slots, run_len // 2, 128), f32),
            pltpu.VMEM(q_rope.shape, bf16),
            pltpu.VMEM((batch, heads // 2, 128), f32),
            pltpu.VMEM((width * slots, lanes, run_len, latent_dim), bf16),
            pltpu.VMEM((width * slots, lanes, run_len // 2, 128), bf16),
            pltpu.VMEM((width * slots, lanes, run_len, 128), bf16),
            pltpu.VMEM((depth, batch, heads, latent_dim), bf16),
            pltpu.VMEM((depth, batch, heads // 2, 128), bf16),
            pltpu.VMEM(value_up_weight.shape, bf16),
            pltpu.VMEM((2, count, latent_dim), bf16),
            pltpu.VMEM((2, count, 128), bf16),
            pltpu.VMEM((latent_dim // 128, depth * batch * heads, 128), f32),
            pltpu.VMEM((latent_dim // 128, depth * batch * own_heads, 128), f32),
            pltpu.VMEM((depth + 1, heads, 128), f32),
            pltpu.VMEM((depth + 1, own_heads, 128), f32),
            pltpu.VMEM((depth, requests, own_heads * value_dim), f32),
            pltpu.VMEM((depth, requests, own_heads * value_dim), bf16),
            pltpu.VMEM((depth, requests, 128), f32),
            pltpu.VMEM((depth + 1, requests, own_heads * value_dim), bf16),
            pltpu.VMEM((depth + 1, requests, 128), f32),
            pltpu.VMEM((2, requests, own_heads // 2 * value_dim), bf16),
            pltpu.VMEM((2, requests, 128), f32),
            pltpu.VMEM((2, requests, own_heads // 2 * value_dim), bf16),
            pltpu.VMEM((2, requests, 128), f32),
            pltpu.VMEM((requests, latent_dim + 128), f32),
            dma((6,)),
            dma((depth,)),
            dma((depth,)),
            dma((2, depth, batch + 1)),
            dma((depth, batch + 1)),
            dma((chunk_count + 1,)),
            dma((chunk_count + 1,)),
            dma((width, chunk_count + 1)),
            dma((width, chunk_count + 1)),
            dma((depth + 1, batch + 1)),
            dma((depth + 1, batch + 1)),
            dma((depth, 2)),
            dma((depth + 1, 2)),
            dma((2, 2)),
            dma((2, 2)),
        ],
        compiler_params=pltpu.CompilerParams(
            collective_id=0, has_side_effects=True, vmem_limit_bytes=60 * 1024 * 1024
        ),
    )(
        source_rank.reshape(requests, max_blocks),
        slot_index,
        lengths,
        cache_latent,
        cache_rope,
        q_latent,
        q_rope,
        value_up_weight,
        new_entry,
    )


def local(*args):
    q_latent, cache_latent, slot_index = args[0], args[3], args[6]
    fits = lax.axis_size("dp") == depth * width and lax.axis_size("tp") == lanes
    fits = fits and q_latent.shape == (16, 128, 512) and args[1].shape == (16, 8192)
    fits = fits and cache_latent.shape == (48, 32, 512) and slot_index.shape == (16, 16)
    return (plane_local if fits else spread_local)(*args)


def solution(mesh):
    placed = (
        P(("pop", "dp"), None, None),
        P(("pop", "dp"), None),
        P(("pop", "dp"), None),
        P(("pop", "dp"), "tp", None),
        P(("pop", "dp"), "tp"),
        P(("pop", "dp"), None, None),
        P(("pop", "dp"), None),
        P(("pop", "dp")),
        P("tp", None, None),
    )
    return jax.shard_map(
        local, mesh=mesh, in_specs=placed, out_specs=P(("pop", "dp"), "tp"), check_vma=False
    )
```
